32 devices in a mesh: parts: 2 (over x), grp: 2 (over core), row: 8 (over z, y).
Axes of the slice: x: 2, y: 2, z: 4, core: 2. Of those that a mesh axis runs over, the one named last changes fastest.
Arguments:
- design: bfloat16 [8192, 1024], P(('parts', 'grp', 'row')), parts along dimension 0, may hold values from -6 to 6
- target: float32 [8192], P(('parts', 'grp', 'row')), parts along dimension 0, may hold values from -6 to 6
- coeffs: bfloat16 [2048], P('parts'), parts along dimension 0, may hold values from -0.1875 to 0.1875
- tau_level: int32 [64], P(('parts', 'grp', 'row')), parts along dimension 0, may hold values from 0 to 3
- bucket: int32 [8192], P(('parts', 'grp', 'row')), parts along dimension 0, may hold values from 0 to 63
- sign_bit: int32 [8192], P(('parts', 'grp', 'row')), parts along dimension 0, may hold values from 0 to 1
- panel_order: int32 [16], P('parts'), parts along dimension 0, may hold values from 0 to 7, each once
Outputs:
- rotated: float32 [2048, 1024], P(('parts', 'grp'), 'row'), parts along dimension 0
The draws below stay inside these ranges and needn't reach their ends.
There are 2 independent parts, one for each index of `parts`. The reference program is written for one: setup_inputs(seed, part) draws one part's arguments, and reference() takes and returns one part's arrays. A program takes and returns all parts, laid end to end along the dimension named above; each array names one. Nothing has to cross between parts.
Inputs may be any that keep to these rules, and one draw needn't show every extreme that they name: `panel_order`: each of 0 to 7 once.
All inputs are finite; a program needn't handle non-finite values. Where the reference program divides by a largest or mean magnitude, that divisor is 1e-20 or more.
Results may differ from the reference program's by a relative error of at most 0.0044.
Values may be sent and summed in bfloat16 or wider, within the bound.
No kernel may reach another device: no remote copies, remote signals or barrier semaphores. Data moves between devices by JAX's collectives and lax.ppermute only.
A program may use at most 64 MiB of HBM per device.

```python
import jax
import jax.numpy as jnp
import numpy as np
from jax import lax

PANEL = 128
N = 1024
PANELS = 8
ROW_DEV = 256
KB = 64
M = 4096
K = 1024
BLOCK = 128
ROUNDS = 5
NS_ITERS = 4


def plant(drawn, rng, least, largest):
    extent = drawn.shape
    place = [jax.random.randint(jax.random.fold_in(rng, axis), (), 0, extent[axis]) for axis in range(len(extent))]
    drawn = drawn.at[tuple(place)].set(least)
    longest = extent.index(max(extent))
    place[longest] = (place[longest] + 1) % extent[longest]
    return drawn.at[tuple(place)].set(largest)


def steps_of(own_key, extent, cuts, low, largest):
    gain = 1.0
    for axis_at, shards_of in cuts:
        draws = jax.random.uniform(jax.random.fold_in(jax.random.fold_in(own_key, 6), axis_at), (shards_of,), jnp.float32, low / len(cuts), largest / len(cuts))
        gain = gain * jnp.repeat(jnp.exp(draws), extent[axis_at] // shards_of).reshape((-1,) + (1,) * (len(extent) - 1 - axis_at))
    return gain


def noise(own_key, dims, deviation, limit, shards=(), kind=jnp.bfloat16):
    array = deviation * jax.random.normal(own_key, dims, jnp.float32)
    if shards:
        array = array * steps_of(own_key, dims, shards, -0.22, 0.18)
    return jnp.clip(array, -limit, limit).astype(kind)


def setup_inputs(seed: int = 0, part: int = 0) -> dict:
    seeds = jax.random.split(jax.random.key(seed), 8)
    own_keys = jax.random.split(jax.random.fold_in(seeds[7], part), 8)
    return {
        "design": noise(own_keys[0], (M, N), 1.0, 6.0, ((0, 16),)),
        "target": noise(own_keys[1], (M,), 1.0, 6.0, ((0, 16),), jnp.float32),
        "coeffs": noise(own_keys[2], (N,), N ** -0.5, 0.1875),
        "tau_level": plant(jax.random.randint(own_keys[3], (M // BLOCK,), 0, 4), jax.random.fold_in(own_keys[3], 1), 0, 3).astype(jnp.int32),
        "bucket": plant(jax.random.randint(own_keys[4], (M,), 0, KB), jax.random.fold_in(own_keys[4], 1), 0, KB - 1).astype(jnp.int32),
        "sign_bit": plant(jax.random.randint(own_keys[5], (M,), 0, 2), jax.random.fold_in(own_keys[5], 1), 0, 1).astype(jnp.int32),
        "panel_order": jax.random.permutation(own_keys[6], PANELS).astype(jnp.int32),
    }


def sketch_block(design, target, coeffs, tau_level, bucket, sign_bit):
    rows = design.shape[0]
    fitted = jnp.dot(design, coeffs, preferred_element_type=jnp.float32)
    residual = target - fitted
    blocks = tau_level.shape[0]
    quantile = 0.1 + 0.25 * tau_level.astype(jnp.float32)
    quantile = jnp.broadcast_to(quantile[:, None], (blocks, rows // blocks)).reshape(rows)
    upper = jax.nn.sigmoid(residual / 0.2)
    weight = (quantile * upper + (1.0 - quantile) * (1.0 - upper)) / jnp.sqrt(residual * residual + 0.25)
    signed = ((2.0 * sign_bit.astype(jnp.float32) - 1.0) * jnp.sqrt(weight)).astype(jnp.bfloat16)
    slots = lax.broadcasted_iota(jnp.int32, (KB, rows), 0)
    embed = jnp.where(slots == bucket[None, :], signed[None, :], jnp.zeros((), jnp.bfloat16))
    return jnp.dot(embed, design, preferred_element_type=jnp.float32).astype(jnp.bfloat16)

def pair_transform(gram):
    squares = jnp.diagonal(gram)
    inv_root = lax.rsqrt(squares)
    normed = gram * inv_root[:, None] * inv_root[None, :]
    bound = jnp.max(lax.optimization_barrier(jnp.sum(jnp.abs(normed), axis=1)))
    identity = jnp.eye(gram.shape[0], dtype=jnp.float32)
    current = normed / bound
    inverse = identity
    for iteration in range(NS_ITERS):
        middle = 1.5 * identity - 0.5 * jnp.dot(inverse, current, precision=lax.Precision.HIGHEST)
        current_next = jnp.dot(current, middle, precision=lax.Precision.HIGHEST)
        inverse = jnp.dot(middle, inverse, precision=lax.Precision.HIGHEST)
        current = current_next
    return inv_root[:, None] * inverse * (jnp.sqrt(squares) / jnp.sqrt(bound))[None, :]

def reference(design, target, coeffs, tau_level, bucket, sign_bit, panel_order):
    groups = design.shape[0] // ROW_DEV

    def one_block(pieces):
        block_design, block_target, block_level, block_bucket, block_sign = pieces
        return sketch_block(block_design, block_target, coeffs, block_level, block_bucket, block_sign)
    sketch = lax.map(one_block, (design.reshape(groups, ROW_DEV, N), target.reshape(groups, ROW_DEV), tau_level.reshape(groups, ROW_DEV // BLOCK), bucket.reshape(groups, ROW_DEV), sign_bit.reshape(groups, ROW_DEV)))
    sketch = sketch.reshape(K, PANELS, PANEL)
    panels = jnp.take(sketch, panel_order, axis=1).astype(jnp.float32)
    depth = PANELS.bit_length() - 1
    positions = np.arange(PANELS)
    for turn in range(ROUNDS):
        bit = turn % depth
        lows = positions[positions >> bit & 1 == 0]
        highs = lows + (1 << bit)
        pairs = jnp.concatenate([panels[:, lows, :], panels[:, highs, :]], axis=2)
        gram = jnp.einsum('kpa,kpb->pab', pairs, pairs, precision=lax.Precision.HIGHEST)
        mixing = jax.vmap(pair_transform)(gram)
        updated = jnp.einsum('kpa,pab->kpb', pairs, mixing, precision=lax.Precision.HIGHEST)
        panels = panels.at[:, lows, :].set(updated[:, :, :PANEL])
        panels = panels.at[:, highs, :].set(updated[:, :, PANEL:])
    return panels.reshape(K, N)
```

```python
import functools

import jax
import jax.numpy as jnp
from jax import lax
from jax.experimental import pallas as pl
from jax.experimental.pallas import tpu as pltpu
from jax.sharding import PartitionSpec as P

PANEL = 128
KB = 64
ROUNDS = 5
NS_ITERS = 4
GATHER_BYTES = 12 << 20


def swapped(block, axis, bit):
    count = lax.axis_size(axis)
    route = []
    for low in range(count):
        high = low | 1 << bit
        if high != low and high < count:
            route += [(low, high), (high, low)]
    return lax.ppermute(block, axis, route)


def sketch_block(design, target, coeffs, tau_level, bucket, sign_bit):
    rows = design.shape[0]
    fitted = jnp.dot(design, coeffs, preferred_element_type=jnp.float32)
    residual = target - fitted
    blocks = tau_level.shape[0]
    quantile = 0.1 + 0.25 * tau_level.astype(jnp.float32)
    quantile = jnp.broadcast_to(quantile[:, None], (blocks, rows // blocks)).reshape(rows)
    upper = jax.nn.sigmoid(residual / 0.2)
    weight = (quantile * upper + (1.0 - quantile) * (1.0 - upper)) / jnp.sqrt(
        residual * residual + 0.25
    )
    signed = ((2.0 * sign_bit.astype(jnp.float32) - 1.0) * jnp.sqrt(weight)).astype(jnp.bfloat16)
    slots = lax.broadcasted_iota(jnp.int32, (KB, rows), 0)
    embed = jnp.where(slots == bucket[None, :], signed[None, :], jnp.zeros((), jnp.bfloat16))
    return jnp.dot(embed, design, preferred_element_type=jnp.float32).astype(jnp.bfloat16)


def mul(left, right):
    return jnp.dot(
        left.astype(jnp.bfloat16), right.astype(jnp.bfloat16), preferred_element_type=jnp.float32
    )


def diagonal_mask(width):
    rows = lax.broadcasted_iota(jnp.int32, (width, width), 0)
    columns = lax.broadcasted_iota(jnp.int32, (width, width), 1)
    return rows == columns


def root_factors(grams):
    eye = diagonal_mask(grams[0].shape[0])
    state = []
    for gram in grams:
        bound = jnp.max(jnp.sum(jnp.abs(gram), axis=0, keepdims=True), axis=1, keepdims=True)
        inverse = 1.0 / bound
        state.append((inverse, jnp.where(eye, 0.0, gram) * inverse, lax.rsqrt(bound)))
    w = [entry[0] for entry in state]
    v = [entry[1] for entry in state]
    scale = [entry[2] for entry in state]
    t = [[1.5 - 0.5 * value for value in w]]
    vs = [v]
    for step in range(NS_ITERS - 1):
        square = [mul(a, a) for a in v]
        right = []
        for i in range(len(v)):
            beta = 0.25 * w[i] - t[-1][i]
            right.append(beta * v[i] + 0.25 * square[i])
        product = [mul(a, b) for a, b in zip(v, right)]
        v = [(t[-1][i] - w[i]) * t[-1][i] * v[i] + product[i] for i in range(len(v))]
        w = [w[i] * t[-1][i] * t[-1][i] for i in range(len(v))]
        t.append([1.5 - 0.5 * value for value in w])
        vs.append(v)
    terms = [[(t[k][i], -0.5 * vs[k][i]) for k in range(NS_ITERS)] for i in range(len(v))]
    while len(terms[0]) > 1:
        merged = []
        for row in terms:
            line = []
            for k in range(0, len(row) - 1, 2):
                (a, left), (b, right) = row[k], row[k + 1]
                line.append((a * b, a * right + b * left + mul(left, right)))
            if len(row) % 2:
                line.append(row[-1])
            merged.append(line)
        terms = merged
    return [(row[0][0] * scale[i], row[0][1] * scale[i]) for i, row in enumerate(terms)]


def apply_right(block, factor):
    z, e = factor
    return z * block + mul(block, e)


def apply_left(factor, block):
    z, e = factor
    return z * block + mul(e, block)


def diagonal_of(block, axis):
    return jnp.sum(jnp.where(diagonal_mask(block.shape[0]), block, 0.0), axis=axis, keepdims=True)


def rounds_kernel(count, order_ref, source_ref, sketch_ref, out_ref, ordered_ref):
    width = PANEL
    depth = count.bit_length() - 1
    for j in range(count):
        column = pl.multiple_of(order_ref[j] * width, width)
        ordered_ref[:, j * width : (j + 1) * width] = sketch_ref[:, pl.ds(column, width)]

    live = [None] * (ROUNDS + 1)
    live[ROUNDS] = [0]
    for turn in reversed(range(ROUNDS)):
        bit = 1 << turn % depth
        live[turn] = sorted({a for p in live[turn + 1] for a in (p, p ^ bit)})

    grams = {}
    for a in range(0, count, 2):
        for b in range(a, count, 2):
            grams[a, b] = lax.dot_general(
                ordered_ref[:, a * width : (a + 2) * width],
                ordered_ref[:, b * width : (b + 2) * width],
                (((0,), (0,)), ((), ())),
                preferred_element_type=jnp.float32,
            )
    row_scale, column_scale, total = {}, {}, {}
    for a in range(0, count, 2):
        along = diagonal_of(grams[a, a], 0)
        down = diagonal_of(grams[a, a], 1)
        for half in range(2):
            cut = slice(half * width, (half + 1) * width)
            total[a + half] = along[:, cut]
            row_scale[a + half] = lax.rsqrt(along[:, cut])
            column_scale[a + half] = lax.rsqrt(down[cut])
    first_scale = dict(column_scale)
    blocks = {}
    for (a, b), gram in grams.items():
        for i in range(2):
            for j in range(2):
                if a + i <= b + j:
                    part = gram[i * width : (i + 1) * width, j * width : (j + 1) * width]
                    blocks[a + i, b + j] = column_scale[a + i] * part * row_scale[b + j]

    def block_of(a, b):
        return blocks[a, b] if (a, b) in blocks else blocks[b, a].T

    def joined(left, right):
        return jnp.concatenate(
            [
                jnp.concatenate([block_of(left[0], right[0]), block_of(left[0], right[1])], axis=1),
                jnp.concatenate([block_of(left[1], right[0]), block_of(left[1], right[1])], axis=1),
            ],
            axis=0,
        )

    history = []
    for turn in range(ROUNDS):
        bit = 1 << turn % depth
        pairs = [(p, p | bit) for p in live[turn] if not p & bit]
        whole = {pair: joined(pair, pair) for pair in pairs}
        factors = dict(zip(pairs, root_factors([whole[pair] for pair in pairs])))
        keep = live[turn + 1]
        scales = {}
        if turn + 1 < ROUNDS:
            fresh = {}
            for i, left in enumerate(pairs):
                for right in pairs[i:]:
                    source = whole[left] if left == right else joined(left, right)
                    fresh[left, right] = apply_left(
                        factors[left], apply_right(source, factors[right])
                    )
            row_scale, column_scale = {}, {}
            for pair in pairs:
                along = diagonal_of(fresh[pair, pair], 0)
                down = diagonal_of(fresh[pair, pair], 1)
                for half in range(2):
                    cut = slice(half * width, (half + 1) * width)
                    row_scale[pair[half]] = lax.rsqrt(along[:, cut])
                    column_scale[pair[half]] = lax.rsqrt(down[cut])
                    total[pair[half]] = total[pair[half]] * along[:, cut]
            blocks = {}
            for (left, right), value in fresh.items():
                for i in range(2):
                    for j in range(2):
                        a, b = left[i], right[j]
                        if a in keep and b in keep and (left != right or i <= j):
                            part = value[i * width : (i + 1) * width, j * width : (j + 1) * width]
                            blocks[a, b] = column_scale[a] * part * row_scale[b]
            scales = column_scale
        history.append((pairs, factors, scales))

    pairs, factors, _ = history[-1]
    z, e = factors[pairs[0]]
    corner = jnp.where(diagonal_mask(width), z, 0.0)
    combined = {
        pairs[0][0]: corner + e[:width, :width],
        pairs[0][1]: e[width:, :width],
    }
    for pairs, factors, scales in reversed(history[:-1]):
        following = {}
        for pair in pairs:
            z, e = factors[pair]
            parts = [half for half in range(2) if pair[half] in combined]
            tops = {half: scales[pair[half]] * combined[pair[half]] for half in parts}
            stacked = jnp.concatenate([tops[half] for half in parts], axis=0)
            columns = e if len(parts) == 2 else e[:, parts[0] * width : (parts[0] + 1) * width]
            moved = mul(columns, stacked)
            for half in range(2):
                rows = moved[half * width : (half + 1) * width]
                following[pair[half]] = z * tops[half] + rows if half in tops else rows
        combined = following
    weights = jnp.concatenate(
        [first_scale[p] * combined[p] for p in range(count)], axis=0
    ) * jnp.sqrt(total[0])
    high = weights.astype(jnp.bfloat16)
    low = (weights - high.astype(jnp.float32)).astype(jnp.bfloat16)
    own = out_ref.shape[0]
    result = jnp.dot(ordered_ref[:own], high, preferred_element_type=jnp.float32)
    result = result + jnp.dot(ordered_ref[:own], low, preferred_element_type=jnp.float32)
    chunk = own // count
    for j in range(count):
        start = pl.multiple_of(source_ref[j] * chunk, chunk)
        out_ref[pl.ds(start, chunk), :] = result[j * chunk : (j + 1) * chunk]


def all_rounds(sketch, order, source, own_rows):
    count = order.shape[0]
    return pl.pallas_call(
        functools.partial(rounds_kernel, count),
        out_shape=jax.ShapeDtypeStruct((own_rows, PANEL), jnp.float32),
        in_specs=[
            pl.BlockSpec(memory_space=pltpu.SMEM),
            pl.BlockSpec(memory_space=pltpu.SMEM),
            pl.BlockSpec(memory_space=pltpu.VMEM),
        ],
        out_specs=pl.BlockSpec(memory_space=pltpu.VMEM),
        scratch_shapes=[pltpu.VMEM(sketch.shape, jnp.bfloat16)],
        compiler_params=pltpu.CompilerParams(vmem_limit_bytes=56 << 20),
    )(order, source, sketch)


def ring_gather(block, axis):
    count = lax.axis_size(axis)
    ring = list(range(0, count, 2)) + list(range(1, count, 2))[::-1]
    onward = [(ring[i], ring[(i + 1) % count]) for i in range(count)]
    back = [(b, a) for a, b in onward]
    place = [ring.index(i) for i in range(count)]
    here = jnp.array(place, jnp.int32)[lax.axis_index(axis)]
    name = jnp.array(ring, jnp.int32)
    blocks, origin = [block], [lax.axis_index(axis)]
    ahead = behind = block
    for step in range(1, count // 2):
        ahead = lax.ppermute(ahead, axis, onward)
        behind = lax.ppermute(behind, axis, back)
        blocks += [ahead, behind]
        origin += [name[(here - step) % count], name[(here + step) % count]]
    half = block.shape[0] // 2
    last = [lax.ppermute(ahead[:half], axis, onward), lax.ppermute(behind[half:], axis, back)]
    blocks += last
    origin.append(name[(here + count // 2) % count])
    return jnp.concatenate(blocks, axis=0), jnp.stack(origin).astype(jnp.int32)


def gathered_rounds(sketch, panel_order):
    mine, source = ring_gather(sketch, "row")
    other = lax.ppermute(mine, "grp", [(0, 1), (1, 0)])
    whole = jnp.concatenate([mine, other], axis=0)
    count = panel_order.shape[0]
    order = panel_order[jnp.arange(count) ^ lax.axis_index("row")]
    return all_rounds(whole, order, source, mine.shape[0])


def pair_transform(gram):
    squares = jnp.sum(jnp.where(diagonal_mask(gram.shape[0]), gram, 0.0), axis=0)
    inv_root = lax.rsqrt(squares)
    normed = gram * inv_root[:, None] * inv_root[None, :]
    bound = jnp.max(jnp.sum(jnp.abs(normed), axis=1))
    identity = jnp.eye(gram.shape[0], dtype=jnp.float32)
    current = normed / bound
    inverse = identity
    for iteration in range(NS_ITERS):
        middle = 1.5 * identity - 0.5 * jnp.dot(inverse, current, precision=lax.Precision.HIGHEST)
        current_next = jnp.dot(current, middle, precision=lax.Precision.HIGHEST)
        inverse = jnp.dot(middle, inverse, precision=lax.Precision.HIGHEST)
        current = current_next
    return inv_root[:, None] * inverse * (jnp.sqrt(squares) / jnp.sqrt(bound))[None, :]


def cross_product(left, right):
    return lax.dot_general(
        left,
        right,
        (((0,), (0,)), ((), ())),
        precision=lax.Precision.HIGHEST,
        preferred_element_type=jnp.float32,
    )


def gram_blocks(own, partner):
    return (cross_product(own, own), cross_product(own, partner), cross_product(partner, partner))


def pair_update(own, partner, blocks, lower):
    self_gram, cross_gram, other_gram = blocks
    low_low = jnp.where(lower, self_gram, other_gram)
    high_high = jnp.where(lower, other_gram, self_gram)
    low_high = jnp.where(lower, cross_gram, cross_gram.T)
    gram = jnp.concatenate(
        [
            jnp.concatenate([low_low, low_high], axis=1),
            jnp.concatenate([low_high.T, high_high], axis=1),
        ],
        axis=0,
    )
    mixing = pair_transform(gram)
    width = own.shape[1]
    own_own = jnp.where(lower, mixing[:width, :width], mixing[width:, width:])
    other_own = jnp.where(lower, mixing[width:, :width], mixing[:width, width:])
    return jnp.dot(own, own_own, precision=lax.Precision.HIGHEST) + jnp.dot(
        partner, other_own, precision=lax.Precision.HIGHEST
    )


def exchanged_rounds(sketch, panel_order):
    panels = sketch.reshape(KB, -1, PANEL)
    ordered = jnp.take(panels, panel_order, axis=1).reshape(KB, -1)
    regrouped = lax.all_to_all(ordered, "row", split_axis=1, concat_axis=0, tiled=True)
    half_rows = regrouped.shape[0]
    depth = lax.axis_size("row").bit_length() - 1
    position = lax.axis_index("row")
    working = lax.all_gather(regrouped, "grp", axis=0, tiled=True).astype(jnp.float32)
    for turn in range(ROUNDS):
        bit = turn % depth
        partner = swapped(working.astype(jnp.bfloat16), "row", bit).astype(working.dtype)
        lower = position >> bit & 1 == 0
        working = pair_update(working, partner, gram_blocks(working, partner), lower)
    return lax.dynamic_slice_in_dim(working, lax.axis_index("grp") * half_rows, half_rows, 0)


def per_device(design, target, coeffs, tau_level, bucket, sign_bit, panel_order):
    sketch = sketch_block(design, target, coeffs, tau_level, bucket, sign_bit)
    rows = KB * lax.axis_size("row") * lax.axis_size("grp")
    columns = design.shape[1]
    if 2 * rows * columns + 4 * columns * columns <= GATHER_BYTES:
        return gathered_rounds(sketch, panel_order)
    return exchanged_rounds(sketch, panel_order)


def solution(mesh):
    placed = (
        P(("parts", "grp", "row"), None),
        P(("parts", "grp", "row")),
        P("parts"),
        P(("parts", "grp", "row")),
        P(("parts", "grp", "row")),
        P(("parts", "grp", "row")),
        P("parts"),
    )
    return jax.shard_map(
        per_device,
        mesh=mesh,
        in_specs=placed,
        out_specs=P(("parts", "grp"), "row"),
        check_vma=False,
    )
```

```python
import functools

import jax
import jax.numpy as jnp
from jax import lax
from jax.experimental import pallas as pl
from jax.experimental.pallas import tpu as pltpu
from jax.sharding import PartitionSpec as P

PANEL = 128
KB = 64
ROUNDS = 5
NS_ITERS = 4
GATHER_BYTES = 12 << 20


def swapped(block, axis, bit):
    count = lax.axis_size(axis)
    route = []
    for low in range(count):
        high = low | 1 << bit
        if high != low and high < count:
            route += [(low, high), (high, low)]
    return lax.ppermute(block, axis, route)


def sketch_kernel(design_hbm, target_hbm, coeffs_hbm, level_ref, bucket_hbm, sign_hbm, out_ref,
                  design_ref, target_ref, coeffs_ref, bucket_ref, sign_ref, arrived):
    copies = [
        pltpu.make_async_copy(source, here, arrived.at[i])
        for i, (source, here) in enumerate(
            [
                (coeffs_hbm, coeffs_ref),
                (design_hbm, design_ref),
                (target_hbm, target_ref),
                (bucket_hbm, bucket_ref),
                (sign_hbm, sign_ref),
            ]
        )
    ]
    for copy in copies:
        copy.start()
    for copy in copies:
        copy.wait()
    rows = design_ref.shape[0]
    design = design_ref[...]
    fitted = lax.dot_general(
        coeffs_ref[...].reshape(1, -1),
        design,
        (((1,), (1,)), ((), ())),
        preferred_element_type=jnp.float32,
    )
    residual = target_ref[...].reshape(1, rows) - fitted
    blocks = level_ref.shape[0]
    lane = lax.broadcasted_iota(jnp.int32, (1, rows), 1)
    level = jnp.full((1, rows), level_ref[0], jnp.int32)
    for block in range(1, blocks):
        level = jnp.where(lane >= block * (rows // blocks), level_ref[block], level)
    quantile = 0.1 + 0.25 * level.astype(jnp.float32)
    upper = jax.nn.sigmoid(residual / 0.2)
    weight = (quantile * upper + (1.0 - quantile) * (1.0 - upper)) / jnp.sqrt(
        residual * residual + 0.25
    )
    sign = 2.0 * sign_ref[...].reshape(1, rows).astype(jnp.float32) - 1.0
    signed = (sign * jnp.sqrt(weight)).astype(jnp.bfloat16).astype(jnp.float32)
    slots = lax.broadcasted_iota(jnp.int32, (KB, rows), 0)
    embed = jnp.where(slots == bucket_ref[...].reshape(1, rows), signed, 0.0).astype(jnp.bfloat16)
    out_ref[...] = jnp.dot(embed, design, preferred_element_type=jnp.float32).astype(jnp.bfloat16)


def sketch_local(design, target, coeffs, tau_level, bucket, sign_bit):
    rows, columns = design.shape
    anywhere = pl.BlockSpec(memory_space=pl.ANY)
    return pl.pallas_call(
        sketch_kernel,
        out_shape=jax.ShapeDtypeStruct((KB, columns), jnp.bfloat16),
        in_specs=[anywhere] * 3 + [pl.BlockSpec(memory_space=pltpu.SMEM)] + [anywhere] * 2,
        out_specs=pl.BlockSpec(memory_space=pltpu.VMEM),
        scratch_shapes=[
            pltpu.VMEM((rows, columns), jnp.bfloat16),
            pltpu.VMEM((rows,), jnp.float32),
            pltpu.VMEM((columns,), jnp.bfloat16),
            pltpu.VMEM((rows,), jnp.int32),
            pltpu.VMEM((rows,), jnp.int32),
            pltpu.SemaphoreType.DMA((5,)),
        ],
        compiler_params=pltpu.CompilerParams(vmem_limit_bytes=16 << 20),
    )(design, target, coeffs, tau_level, bucket, sign_bit)


def mul(left, right):
    return jnp.dot(
        left.astype(jnp.bfloat16), right.astype(jnp.bfloat16), preferred_element_type=jnp.float32
    )


def diagonal_mask(width):
    rows = lax.broadcasted_iota(jnp.int32, (width, width), 0)
    columns = lax.broadcasted_iota(jnp.int32, (width, width), 1)
    return rows == columns


def root_factors(grams):
    eye = diagonal_mask(grams[0].shape[0])
    state = []
    for gram in grams:
        bound = jnp.max(jnp.sum(jnp.abs(gram), axis=0, keepdims=True), axis=1, keepdims=True)
        inverse = 1.0 / bound
        state.append((inverse, jnp.where(eye, 0.0, gram) * inverse, lax.rsqrt(bound)))
    w = [entry[0] for entry in state]
    v = [entry[1] for entry in state]
    scale = [entry[2] for entry in state]
    t = [[1.5 - 0.5 * value for value in w]]
    vs = [v]
    for step in range(NS_ITERS - 1):
        square = [mul(a, a) for a in v]
        right = []
        for i in range(len(v)):
            beta = 0.25 * w[i] - t[-1][i]
            right.append(beta * v[i] + 0.25 * square[i])
        product = [mul(a, b) for a, b in zip(v, right)]
        v = [(t[-1][i] - w[i]) * t[-1][i] * v[i] + product[i] for i in range(len(v))]
        w = [w[i] * t[-1][i] * t[-1][i] for i in range(len(v))]
        t.append([1.5 - 0.5 * value for value in w])
        vs.append(v)
    terms = [[(t[k][i], -0.5 * vs[k][i]) for k in range(NS_ITERS)] for i in range(len(v))]
    while len(terms[0]) > 1:
        merged = []
        for row in terms:
            line = []
            for k in range(0, len(row) - 1, 2):
                (a, left), (b, right) = row[k], row[k + 1]
                line.append((a * b, a * right + b * left + mul(left, right)))
            if len(row) % 2:
                line.append(row[-1])
            merged.append(line)
        terms = merged
    return [(row[0][0] * scale[i], row[0][1] * scale[i]) for i, row in enumerate(terms)]


def apply_right(block, factor):
    z, e = factor
    return z * block + mul(block, e)


def apply_left(factor, block):
    z, e = factor
    return z * block + mul(e, block)


def diagonal_of(block, axis):
    return jnp.sum(jnp.where(diagonal_mask(block.shape[0]), block, 0.0), axis=axis, keepdims=True)


def ring_place(index, count):
    return jnp.where(index % 2 == 0, index // 2, count - 1 - index // 2)


def ring_index(place, count):
    return jnp.where(place < count // 2, 2 * place, 2 * (count - 1 - place) + 1)


def ring_origins(count):
    here = ring_place(lax.axis_index("row"), count)
    turns = [0] + [step for k in range(1, count // 2) for step in (-k, k)] + [count // 2]
    return [ring_index((here + turn + count) % count, count) for turn in turns]


def rounds_kernel(count, pieces, order_ref, *refs):
    chunks, out_ref, ordered_ref = refs[: 2 * pieces], refs[2 * pieces], refs[2 * pieces + 1]
    width = PANEL
    depth = count.bit_length() - 1
    position = lax.axis_index("row")
    columns = [
        pl.multiple_of(order_ref[jnp.bitwise_xor(position, j)] * width, width) for j in range(count)
    ]
    start = 0
    for chunk in chunks:
        rows = chunk.shape[0]
        for j in range(count):
            ordered_ref[start : start + rows, j * width : (j + 1) * width] = chunk[
                :, pl.ds(columns[j], width)
            ]
        start += rows

    live = [None] * (ROUNDS + 1)
    live[ROUNDS] = [0]
    for turn in reversed(range(ROUNDS)):
        bit = 1 << turn % depth
        live[turn] = sorted({a for p in live[turn + 1] for a in (p, p ^ bit)})

    grams = {}
    for a in range(0, count, 2):
        for b in range(a, count, 2):
            grams[a, b] = lax.dot_general(
                ordered_ref[:, a * width : (a + 2) * width],
                ordered_ref[:, b * width : (b + 2) * width],
                (((0,), (0,)), ((), ())),
                preferred_element_type=jnp.float32,
            )
    row_scale, column_scale, total = {}, {}, {}
    for a in range(0, count, 2):
        along = diagonal_of(grams[a, a], 0)
        down = diagonal_of(grams[a, a], 1)
        for half in range(2):
            cut = slice(half * width, (half + 1) * width)
            total[a + half] = along[:, cut]
            row_scale[a + half] = lax.rsqrt(along[:, cut])
            column_scale[a + half] = lax.rsqrt(down[cut])
    first_scale = dict(column_scale)
    blocks = {}
    for (a, b), gram in grams.items():
        for i in range(2):
            for j in range(2):
                if a + i <= b + j:
                    part = gram[i * width : (i + 1) * width, j * width : (j + 1) * width]
                    blocks[a + i, b + j] = column_scale[a + i] * part * row_scale[b + j]

    def block_of(a, b):
        return blocks[a, b] if (a, b) in blocks else blocks[b, a].T

    def joined(left, right):
        return jnp.concatenate(
            [
                jnp.concatenate([block_of(left[0], right[0]), block_of(left[0], right[1])], axis=1),
                jnp.concatenate([block_of(left[1], right[0]), block_of(left[1], right[1])], axis=1),
            ],
            axis=0,
        )

    history = []
    for turn in range(ROUNDS):
        bit = 1 << turn % depth
        pairs = [(p, p | bit) for p in live[turn] if not p & bit]
        whole = {pair: joined(pair, pair) for pair in pairs}
        factors = dict(zip(pairs, root_factors([whole[pair] for pair in pairs])))
        keep = live[turn + 1]
        scales = {}
        if turn + 1 < ROUNDS:
            fresh = {}
            for i, left in enumerate(pairs):
                for right in pairs[i:]:
                    source = whole[left] if left == right else joined(left, right)
                    fresh[left, right] = apply_left(
                        factors[left], apply_right(source, factors[right])
                    )
            row_scale, column_scale = {}, {}
            for pair in pairs:
                along = diagonal_of(fresh[pair, pair], 0)
                down = diagonal_of(fresh[pair, pair], 1)
                for half in range(2):
                    cut = slice(half * width, (half + 1) * width)
                    row_scale[pair[half]] = lax.rsqrt(along[:, cut])
                    column_scale[pair[half]] = lax.rsqrt(down[cut])
                    total[pair[half]] = total[pair[half]] * along[:, cut]
            blocks = {}
            for (left, right), value in fresh.items():
                for i in range(2):
                    for j in range(2):
                        a, b = left[i], right[j]
                        if a in keep and b in keep and (left != right or i <= j):
                            part = value[i * width : (i + 1) * width, j * width : (j + 1) * width]
                            blocks[a, b] = column_scale[a] * part * row_scale[b]
            scales = column_scale
        history.append((pairs, factors, scales))

    pairs, factors, _ = history[-1]
    z, e = factors[pairs[0]]
    corner = jnp.where(diagonal_mask(width), z, 0.0)
    combined = {
        pairs[0][0]: corner + e[:width, :width],
        pairs[0][1]: e[width:, :width],
    }
    for pairs, factors, scales in reversed(history[:-1]):
        following = {}
        for pair in pairs:
            z, e = factors[pair]
            parts = [half for half in range(2) if pair[half] in combined]
            tops = {half: scales[pair[half]] * combined[pair[half]] for half in parts}
            stacked = jnp.concatenate([tops[half] for half in parts], axis=0)
            columns = e if len(parts) == 2 else e[:, parts[0] * width : (parts[0] + 1) * width]
            moved = mul(columns, stacked)
            for half in range(2):
                rows = moved[half * width : (half + 1) * width]
                following[pair[half]] = z * tops[half] + rows if half in tops else rows
        combined = following
    weights = jnp.concatenate(
        [first_scale[p] * combined[p] for p in range(count)], axis=0
    ) * jnp.sqrt(total[0])
    high = weights.astype(jnp.bfloat16)
    low = (weights - high.astype(jnp.float32)).astype(jnp.bfloat16)
    own = out_ref.shape[0]
    result = jnp.dot(ordered_ref[:own], high, preferred_element_type=jnp.float32)
    result = result + jnp.dot(ordered_ref[:own], low, preferred_element_type=jnp.float32)
    chunk = own // count
    for j, origin in enumerate(ring_origins(count)):
        start = pl.multiple_of(origin * chunk, chunk)
        out_ref[pl.ds(start, chunk), :] = result[j * chunk : (j + 1) * chunk]


def all_rounds(mine, other, panel_order):
    count = panel_order.shape[0]
    own_rows = sum(block.shape[0] for block in mine)
    inside = pl.BlockSpec(memory_space=pltpu.VMEM)
    return pl.pallas_call(
        functools.partial(rounds_kernel, count, len(mine)),
        out_shape=jax.ShapeDtypeStruct((own_rows, PANEL), jnp.float32),
        in_specs=[pl.BlockSpec(memory_space=pltpu.SMEM)] + [inside] * (2 * len(mine)),
        out_specs=inside,
        scratch_shapes=[pltpu.VMEM((2 * own_rows, mine[0].shape[1]), jnp.bfloat16)],
        compiler_params=pltpu.CompilerParams(vmem_limit_bytes=32 << 20),
    )(panel_order, *mine, *other)


def ring_gather(block, axis):
    count = lax.axis_size(axis)
    ring = list(range(0, count, 2)) + list(range(1, count, 2))[::-1]
    onward = [(ring[i], ring[(i + 1) % count]) for i in range(count)]
    back = [(b, a) for a, b in onward]
    blocks = [block]
    ahead = behind = block
    for step in range(1, count // 2):
        ahead = lax.ppermute(ahead, axis, onward)
        behind = lax.ppermute(behind, axis, back)
        blocks += [ahead, behind]
    half = block.shape[0] // 2
    blocks.append(lax.ppermute(ahead[:half], axis, onward))
    blocks.append(lax.ppermute(behind[half:], axis, back))
    return blocks


def gathered_rounds(sketch, panel_order):
    mine = ring_gather(sketch, "row")
    other = [lax.ppermute(block, "grp", [(0, 1), (1, 0)]) for block in mine]
    return all_rounds(mine, other, panel_order)


def pair_transform(gram):
    squares = jnp.sum(jnp.where(diagonal_mask(gram.shape[0]), gram, 0.0), axis=0)
    inv_root = lax.rsqrt(squares)
    normed = gram * inv_root[:, None] * inv_root[None, :]
    bound = jnp.max(jnp.sum(jnp.abs(normed), axis=1))
    identity = jnp.eye(gram.shape[0], dtype=jnp.float32)
    current = normed / bound
    inverse = identity
    for iteration in range(NS_ITERS):
        middle = 1.5 * identity - 0.5 * jnp.dot(inverse, current, precision=lax.Precision.HIGHEST)
        current_next = jnp.dot(current, middle, precision=lax.Precision.HIGHEST)
        inverse = jnp.dot(middle, inverse, precision=lax.Precision.HIGHEST)
        current = current_next
    return inv_root[:, None] * inverse * (jnp.sqrt(squares) / jnp.sqrt(bound))[None, :]


def cross_product(left, right):
    return lax.dot_general(
        left,
        right,
        (((0,), (0,)), ((), ())),
        precision=lax.Precision.HIGHEST,
        preferred_element_type=jnp.float32,
    )


def gram_blocks(own, partner):
    return (cross_product(own, own), cross_product(own, partner), cross_product(partner, partner))


def pair_update(own, partner, blocks, lower):
    self_gram, cross_gram, other_gram = blocks
    low_low = jnp.where(lower, self_gram, other_gram)
    high_high = jnp.where(lower, other_gram, self_gram)
    low_high = jnp.where(lower, cross_gram, cross_gram.T)
    gram = jnp.concatenate(
        [
            jnp.concatenate([low_low, low_high], axis=1),
            jnp.concatenate([low_high.T, high_high], axis=1),
        ],
        axis=0,
    )
    mixing = pair_transform(gram)
    width = own.shape[1]
    own_own = jnp.where(lower, mixing[:width, :width], mixing[width:, width:])
    other_own = jnp.where(lower, mixing[width:, :width], mixing[:width, width:])
    return jnp.dot(own, own_own, precision=lax.Precision.HIGHEST) + jnp.dot(
        partner, other_own, precision=lax.Precision.HIGHEST
    )


def exchanged_rounds(sketch, panel_order):
    panels = sketch.reshape(KB, -1, PANEL)
    ordered = jnp.take(panels, panel_order, axis=1).reshape(KB, -1)
    regrouped = lax.all_to_all(ordered, "row", split_axis=1, concat_axis=0, tiled=True)
    half_rows = regrouped.shape[0]
    depth = lax.axis_size("row").bit_length() - 1
    position = lax.axis_index("row")
    working = lax.all_gather(regrouped, "grp", axis=0, tiled=True).astype(jnp.float32)
    for turn in range(ROUNDS):
        bit = turn % depth
        partner = swapped(working.astype(jnp.bfloat16), "row", bit).astype(working.dtype)
        lower = position >> bit & 1 == 0
        working = pair_update(working, partner, gram_blocks(working, partner), lower)
    return lax.dynamic_slice_in_dim(working, lax.axis_index("grp") * half_rows, half_rows, 0)


def per_device(design, target, coeffs, tau_level, bucket, sign_bit, panel_order):
    sketch = sketch_local(design, target, coeffs, tau_level, bucket, sign_bit)
    rows = KB * lax.axis_size("row") * lax.axis_size("grp")
    columns = design.shape[1]
    if 2 * rows * columns + 4 * columns * columns <= GATHER_BYTES:
        return gathered_rounds(sketch, panel_order)
    return exchanged_rounds(sketch, panel_order)


def solution(mesh):
    placed = (
        P(("parts", "grp", "row"), None),
        P(("parts", "grp", "row")),
        P("parts"),
        P(("parts", "grp", "row")),
        P(("parts", "grp", "row")),
        P(("parts", "grp", "row")),
        P("parts"),
    )
    return jax.shard_map(
        per_device,
        mesh=mesh,
        in_specs=placed,
        out_specs=P(("parts", "grp"), "row"),
        check_vma=False,
    )
```

```python
import functools

import jax
import jax.numpy as jnp
from jax import lax
from jax.experimental import pallas as pl
from jax.experimental.pallas import tpu as pltpu
from jax.sharding import PartitionSpec as P

PANEL = 128
KB = 64
ROUNDS = 5
NS_ITERS = 4
GATHER_BYTES = 12 << 20


def swapped(block, axis, bit):
    count = lax.axis_size(axis)
    route = []
    for low in range(count):
        high = low | 1 << bit
        if high != low and high < count:
            route += [(low, high), (high, low)]
    return lax.ppermute(block, axis, route)


def sketch_kernel(design_hbm, target_hbm, coeffs_hbm, level_ref, bucket_hbm, sign_hbm, out_ref,
                  design_ref, target_ref, coeffs_ref, bucket_ref, sign_ref, arrived):
    copies = [
        pltpu.make_async_copy(source, here, arrived.at[i])
        for i, (source, here) in enumerate(
            [
                (coeffs_hbm, coeffs_ref),
                (design_hbm, design_ref),
                (target_hbm, target_ref),
                (bucket_hbm, bucket_ref),
                (sign_hbm, sign_ref),
            ]
        )
    ]
    for copy in copies:
        copy.start()
    for copy in copies:
        copy.wait()
    rows = design_ref.shape[0]
    design = design_ref[...]
    fitted = lax.dot_general(
        coeffs_ref[...].reshape(1, -1),
        design,
        (((1,), (1,)), ((), ())),
        preferred_element_type=jnp.float32,
    )
    residual = target_ref[...].reshape(1, rows) - fitted
    blocks = level_ref.shape[0]
    lane = lax.broadcasted_iota(jnp.int32, (1, rows), 1)
    level = jnp.full((1, rows), level_ref[0], jnp.int32)
    for block in range(1, blocks):
        level = jnp.where(lane >= block * (rows // blocks), level_ref[block], level)
    quantile = 0.1 + 0.25 * level.astype(jnp.float32)
    upper = jax.nn.sigmoid(residual / 0.2)
    weight = (quantile * upper + (1.0 - quantile) * (1.0 - upper)) / jnp.sqrt(
        residual * residual + 0.25
    )
    sign = 2.0 * sign_ref[...].reshape(1, rows).astype(jnp.float32) - 1.0
    signed = (sign * jnp.sqrt(weight)).astype(jnp.bfloat16).astype(jnp.float32)
    slots = lax.broadcasted_iota(jnp.int32, (KB, rows), 0)
    embed = jnp.where(slots == bucket_ref[...].reshape(1, rows), signed, 0.0).astype(jnp.bfloat16)
    out_ref[...] = jnp.dot(embed, design, preferred_element_type=jnp.float32).astype(jnp.bfloat16)


def sketch_local(design, target, coeffs, tau_level, bucket, sign_bit):
    rows, columns = design.shape
    anywhere = pl.BlockSpec(memory_space=pltpu.HBM)
    return pl.pallas_call(
        sketch_kernel,
        out_shape=jax.ShapeDtypeStruct((KB, columns), jnp.bfloat16),
        in_specs=[anywhere] * 3 + [pl.BlockSpec(memory_space=pltpu.SMEM)] + [anywhere] * 2,
        out_specs=pl.BlockSpec(memory_space=pltpu.VMEM),
        scratch_shapes=[
            pltpu.VMEM((rows, columns), jnp.bfloat16),
            pltpu.VMEM((rows,), jnp.float32),
            pltpu.VMEM((columns,), jnp.bfloat16),
            pltpu.VMEM((rows,), jnp.int32),
            pltpu.VMEM((rows,), jnp.int32),
            pltpu.SemaphoreType.DMA((5,)),
        ],
        compiler_params=pltpu.CompilerParams(vmem_limit_bytes=16 << 20),
    )(design, target, coeffs, tau_level, bucket, sign_bit)


def half(block):
    return block.astype(jnp.bfloat16)


def mul(left, right):
    return jnp.dot(left, right, preferred_element_type=jnp.float32)


def diagonal_mask(width):
    rows = lax.broadcasted_iota(jnp.int32, (width, width), 0)
    columns = lax.broadcasted_iota(jnp.int32, (width, width), 1)
    return rows == columns


def root_factors(grams, offs):
    w, t, x, z = [], [], [], []
    for gram, off in zip(grams, offs):
        bound = jnp.max(jnp.sum(jnp.abs(gram), axis=0, keepdims=True), axis=1, keepdims=True)
        w.append(1.0 / bound)
        t.append(1.5 - 0.5 * w[-1])
        x.append((-0.5 * w[-1] / t[-1]) * off)
        z.append(t[-1] * lax.rsqrt(bound))
    xs, halves = [x], [[half(a) for a in x]]
    for step in range(NS_ITERS - 1):
        thin = halves[-1]
        after = [1.5 - 0.5 * a * a * b for a, b in zip(t, w)]
        gain = [a * a * a / b for a, b in zip(t, after)]
        linear = [g * (1.0 - b / a) for g, a, b in zip(gain, t, w)]
        square = [g * (2.0 - 0.5 * b / a) for g, a, b in zip(gain, t, w)]
        inner = [
            half(q * a + g * mul(b, b)) for q, g, a, b in zip(square, gain, x, thin)
        ]
        x = [p * a + mul(r, b) for p, a, b, r in zip(linear, x, thin, inner)]
        w = [a * a * b for a, b in zip(t, w)]
        t = after
        z = [a * b for a, b in zip(z, t)]
        xs.append(x)
        halves.append([half(a) for a in x])
    while len(xs) > 1:
        merged, thinner = [], []
        for k in range(0, len(xs) - 1, 2):
            merged.append(
                [
                    a + b + mul(d, c)
                    for a, b, c, d in zip(xs[k], xs[k + 1], halves[k], halves[k + 1])
                ]
            )
            thinner.append([half(a) for a in merged[-1]])
        if len(xs) % 2:
            merged.append(xs[-1])
            thinner.append(halves[-1])
        xs, halves = merged, thinner
    return list(zip(z, xs[0], halves[0]))


def diagonal_of(block, axis):
    return jnp.sum(jnp.where(diagonal_mask(block.shape[0]), block, 0.0), axis=axis, keepdims=True)


def ring_place(index, count):
    return jnp.where(index % 2 == 0, index // 2, count - 1 - index // 2)


def ring_index(place, count):
    return jnp.where(place < count // 2, 2 * place, 2 * (count - 1 - place) + 1)


def ring_origins(count):
    here = ring_place(lax.axis_index("row"), count)
    turns = [0] + [step for k in range(1, count // 2) for step in (-k, k)] + [count // 2]
    return [ring_index((here + turn + count) % count, count) for turn in turns]


def rounds_kernel(count, pieces, order_ref, *refs):
    chunks = refs[: 2 * pieces]
    out_ref, ordered_ref, turned_ref = refs[2 * pieces :]
    width = PANEL
    depth = count.bit_length() - 1
    position = lax.axis_index("row")
    columns = [
        pl.multiple_of(order_ref[jnp.bitwise_xor(position, j)] * width, width) for j in range(count)
    ]
    start = 0
    for chunk in chunks:
        rows = chunk.shape[0]
        for j in range(count):
            ordered_ref[start : start + rows, j * width : (j + 1) * width] = chunk[
                :, pl.ds(columns[j], width)
            ]
        start += rows

    live = [None] * (ROUNDS + 1)
    live[ROUNDS] = [0]
    for turn in reversed(range(ROUNDS)):
        bit = 1 << turn % depth
        live[turn] = sorted({a for p in live[turn + 1] for a in (p, p ^ bit)})

    for p in range(0, count, 2):
        turned_ref[p * width : (p + 2) * width] = ordered_ref[
            :, p * width : (p + 2) * width
        ].T

    row_scale, column_scale, total, grams = {}, {}, {}, {}
    for b in range(0, count, 2):
        tall = mul(turned_ref[: (b + 2) * width], ordered_ref[:, b * width : (b + 2) * width])
        for i in range(b + 2):
            for j in range(2):
                if i <= b + j:
                    grams[i, b + j] = tall[
                        i * width : (i + 1) * width, j * width : (j + 1) * width
                    ]
    for p in range(count):
        total[p] = diagonal_of(grams[p, p], 0)
        row_scale[p] = lax.rsqrt(total[p])
        column_scale[p] = lax.rsqrt(diagonal_of(grams[p, p], 1))
    first_scale = dict(column_scale)
    blocks = {
        (a, b): column_scale[a] * gram * row_scale[b] for (a, b), gram in grams.items()
    }
    eye = diagonal_mask(width)

    def joined_from(blocks):
        def joined(left, right, corner=lambda block: block):
            def block_of(a, b):
                if a == b:
                    return corner(blocks[a, a])
                return blocks[a, b] if (a, b) in blocks else blocks[b, a].T

            return jnp.concatenate(
                [jnp.concatenate([block_of(a, b) for b in right], axis=1) for a in left], axis=0
            )

        return joined

    history = []
    finish = None
    for turn in range(ROUNDS):
        bit = 1 << turn % depth
        pairs = [(p, p | bit) for p in live[turn] if not p & bit]
        joined = joined_from(blocks)
        whole = [joined(pair, pair) for pair in pairs]
        offs = [
            joined(pair, pair, lambda block: jnp.where(eye, 0.0, block)) for pair in pairs
        ]
        factors = root_factors(whole, offs)
        if finish is not None:
            finish()
        keep = live[turn + 1]
        scales = {}
        if turn + 1 < ROUNDS:
            kept = [[i for i in range(2) if pair[i] in keep] for pair in pairs]
            spans = [
                slice(k[0] * width, (k[-1] + 1) * width) for k in kept
            ]
            fresh, row_scale, column_scale = {}, {}, {}
            for i, pair in enumerate(pairs):
                z, e, thin = factors[i]
                span = spans[i]
                part = offs[i][span] + e[span] + mul(thin[span], half(offs[i]))
                value = part[:, span] + e[span, span] + mul(half(part), thin[:, span])
                for k, at in enumerate(kept[i]):
                    cut = slice(k * width, (k + 1) * width)
                    block = value[cut, cut] + jnp.where(eye, 1.0, 0.0)
                    along = diagonal_of(block, 0)
                    row_scale[pair[at]] = lax.rsqrt(along)
                    column_scale[pair[at]] = lax.rsqrt(diagonal_of(block, 1))
                    total[pair[at]] = total[pair[at]] * along * z * z
                    fresh[pair[at], pair[at]] = block
                    for j, to in list(enumerate(kept[i]))[k + 1 :]:
                        fresh[pair[at], pair[to]] = value[cut, j * width : (j + 1) * width]
            following = 1 << (turn + 1) % depth
            soon, later = [], []
            for j in range(1, len(pairs)):
                near = [
                    i
                    for i in range(j)
                    if any(a ^ following in pairs[j] for a in pairs[i])
                ]
                soon.append((j, near))
                later.append((j, [i for i in range(j) if i not in near]))

            def cross(work, joined, pairs, factors, kept, spans, fresh):
                for j, members in work:
                    if not members:
                        continue
                    tops = []
                    for i in members:
                        source = joined(pairs[i], pairs[j])
                        tops.append(
                            source[spans[i]] + mul(factors[i][2][spans[i]], half(source))
                        )
                    tall = jnp.concatenate(tops, axis=0)
                    tall = tall[:, spans[j]] + mul(half(tall), factors[j][2][:, spans[j]])
                    start = 0
                    for i in members:
                        for at in kept[i]:
                            for k, to in enumerate(kept[j]):
                                fresh[pairs[i][at], pairs[j][to]] = tall[
                                    start : start + width, k * width : (k + 1) * width
                                ]
                            start += width

            def scaled(fresh, column_scale, row_scale):
                return {
                    (a, b): column_scale[a] * value * row_scale[b]
                    for (a, b), value in fresh.items()
                }

            known = (joined_from(blocks), pairs, factors, kept, spans)
            cross(soon, *known, fresh)
            blocks = scaled(fresh, column_scale, row_scale)

            def finish(blocks=blocks, later=later, known=known, down=column_scale, along=row_scale):
                rest = {}
                cross(later, *known, rest)
                blocks.update(scaled(rest, down, along))

            scales = column_scale
        history.append((pairs, factors, scales))

    pairs, factors, _ = history[-1]
    z, e, _ = factors[0]
    combined = {
        pairs[0][0]: jnp.where(eye, 1.0, 0.0) + e[:width, :width],
        pairs[0][1]: e[width:, :width],
    }
    final = z * jnp.sqrt(total[0])
    for pairs, factors, scales in reversed(history[:-1]):
        following = {}
        for pair, (z, e, thin) in zip(pairs, factors):
            parts = [i for i in range(2) if pair[i] in combined]
            tops = {i: scales[pair[i]] * combined[pair[i]] for i in parts}
            stacked = half(jnp.concatenate([tops[i] for i in parts], axis=0))
            moved = mul(thin[:, parts[0] * width : (parts[-1] + 1) * width], stacked)
            for i in range(2):
                rows = moved[i * width : (i + 1) * width]
                following[pair[i]] = tops[i] + rows if i in tops else rows
        combined = following
    weights = jnp.concatenate(
        [first_scale[p] * combined[p] for p in range(count)], axis=0
    ) * final
    high = half(weights)
    low = half(weights - high.astype(jnp.float32))
    own = out_ref.shape[0]
    both = mul(ordered_ref[:own], jnp.concatenate([high, low], axis=1))
    result = both[:, :width] + both[:, width:]
    chunk = own // count
    for j, origin in enumerate(ring_origins(count)):
        start = pl.multiple_of(origin * chunk, chunk)
        out_ref[pl.ds(start, chunk), :] = result[j * chunk : (j + 1) * chunk]


def all_rounds(mine, other, panel_order):
    count = panel_order.shape[0]
    own_rows = sum(block.shape[0] for block in mine)
    inside = pl.BlockSpec(memory_space=pltpu.VMEM)
    return pl.pallas_call(
        functools.partial(rounds_kernel, count, len(mine)),
        out_shape=jax.ShapeDtypeStruct((own_rows, PANEL), jnp.float32),
        in_specs=[pl.BlockSpec(memory_space=pltpu.SMEM)] + [inside] * (2 * len(mine)),
        out_specs=inside,
        scratch_shapes=[
            pltpu.VMEM((2 * own_rows, mine[0].shape[1]), jnp.bfloat16),
            pltpu.VMEM((mine[0].shape[1], 2 * own_rows), jnp.bfloat16),
        ],
        compiler_params=pltpu.CompilerParams(vmem_limit_bytes=32 << 20),
    )(panel_order, *mine, *other)


def ring_gather(block, axis):
    count = lax.axis_size(axis)
    ring = list(range(0, count, 2)) + list(range(1, count, 2))[::-1]
    onward = [(ring[i], ring[(i + 1) % count]) for i in range(count)]
    back = [(b, a) for a, b in onward]
    blocks = [block]
    ahead = behind = block
    for step in range(1, count // 2):
        ahead = lax.ppermute(ahead, axis, onward)
        behind = lax.ppermute(behind, axis, back)
        blocks += [ahead, behind]
    middle = block.shape[0] // 2
    blocks.append(lax.ppermute(ahead[:middle], axis, onward))
    blocks.append(lax.ppermute(behind[middle:], axis, back))
    return blocks


def gathered_rounds(sketch, panel_order):
    mine = ring_gather(sketch, "row")
    other = [lax.ppermute(block, "grp", [(0, 1), (1, 0)]) for block in mine]
    return all_rounds(mine, other, panel_order)


def pair_transform(gram):
    squares = jnp.sum(jnp.where(diagonal_mask(gram.shape[0]), gram, 0.0), axis=0)
    inv_root = lax.rsqrt(squares)
    normed = gram * inv_root[:, None] * inv_root[None, :]
    bound = jnp.max(jnp.sum(jnp.abs(normed), axis=1))
    identity = jnp.eye(gram.shape[0], dtype=jnp.float32)
    current = normed / bound
    inverse = identity
    for iteration in range(NS_ITERS):
        middle = 1.5 * identity - 0.5 * jnp.dot(inverse, current, precision=lax.Precision.HIGHEST)
        current_next = jnp.dot(current, middle, precision=lax.Precision.HIGHEST)
        inverse = jnp.dot(middle, inverse, precision=lax.Precision.HIGHEST)
        current = current_next
    return inv_root[:, None] * inverse * (jnp.sqrt(squares) / jnp.sqrt(bound))[None, :]


def cross_product(left, right):
    return lax.dot_general(
        left,
        right,
        (((0,), (0,)), ((), ())),
        precision=lax.Precision.HIGHEST,
        preferred_element_type=jnp.float32,
    )


def gram_blocks(own, partner):
    return (cross_product(own, own), cross_product(own, partner), cross_product(partner, partner))


def pair_update(own, partner, blocks, lower):
    self_gram, cross_gram, other_gram = blocks
    low_low = jnp.where(lower, self_gram, other_gram)
    high_high = jnp.where(lower, other_gram, self_gram)
    low_high = jnp.where(lower, cross_gram, cross_gram.T)
    gram = jnp.concatenate(
        [
            jnp.concatenate([low_low, low_high], axis=1),
            jnp.concatenate([low_high.T, high_high], axis=1),
        ],
        axis=0,
    )
    mixing = pair_transform(gram)
    width = own.shape[1]
    own_own = jnp.where(lower, mixing[:width, :width], mixing[width:, width:])
    other_own = jnp.where(lower, mixing[width:, :width], mixing[:width, width:])
    return jnp.dot(own, own_own, precision=lax.Precision.HIGHEST) + jnp.dot(
        partner, other_own, precision=lax.Precision.HIGHEST
    )


def exchanged_rounds(sketch, panel_order):
    panels = sketch.reshape(KB, -1, PANEL)
    ordered = jnp.take(panels, panel_order, axis=1).reshape(KB, -1)
    regrouped = lax.all_to_all(ordered, "row", split_axis=1, concat_axis=0, tiled=True)
    half_rows = regrouped.shape[0]
    depth = lax.axis_size("row").bit_length() - 1
    position = lax.axis_index("row")
    working = lax.all_gather(regrouped, "grp", axis=0, tiled=True).astype(jnp.float32)
    for turn in range(ROUNDS):
        bit = turn % depth
        partner = swapped(working.astype(jnp.bfloat16), "row", bit).astype(working.dtype)
        lower = position >> bit & 1 == 0
        working = pair_update(working, partner, gram_blocks(working, partner), lower)
    return lax.dynamic_slice_in_dim(working, lax.axis_index("grp") * half_rows, half_rows, 0)


def per_device(design, target, coeffs, tau_level, bucket, sign_bit, panel_order):
    sketch = sketch_local(design, target, coeffs, tau_level, bucket, sign_bit)
    rows = KB * lax.axis_size("row") * lax.axis_size("grp")
    columns = design.shape[1]
    if 2 * rows * columns + 4 * columns * columns <= GATHER_BYTES:
        return gathered_rounds(sketch, panel_order)
    return exchanged_rounds(sketch, panel_order)


def solution(mesh):
    placed = (
        P(("parts", "grp", "row"), None),
        P(("parts", "grp", "row")),
        P("parts"),
        P(("parts", "grp", "row")),
        P(("parts", "grp", "row")),
        P(("parts", "grp", "row")),
        P("parts"),
    )
    return jax.shard_map(
        per_device,
        mesh=mesh,
        in_specs=placed,
        out_specs=P(("parts", "grp"), "row"),
        check_vma=False,
    )
```

```python
import functools

import jax
import jax.numpy as jnp
from jax import lax
from jax.experimental import pallas as pl
from jax.experimental.pallas import tpu as pltpu
from jax.sharding import PartitionSpec as P

PANEL = 128
KB = 64
ROUNDS = 5
NS_ITERS = 4
GATHER_BYTES = 12 << 20


def swapped(block, axis, bit):
    count = lax.axis_size(axis)
    route = []
    for low in range(count):
        high = low | 1 << bit
        if high != low and high < count:
            route += [(low, high), (high, low)]
    return lax.ppermute(block, axis, route)


def sketch_kernel(design_hbm, target_hbm, coeffs_hbm, level_ref, bucket_hbm, sign_hbm, out_ref,
                  design_ref, target_ref, coeffs_ref, bucket_ref, sign_ref, arrived):
    copies = [
        pltpu.make_async_copy(source, here, arrived.at[i])
        for i, (source, here) in enumerate(
            [
                (coeffs_hbm, coeffs_ref),
                (design_hbm, design_ref),
                (target_hbm, target_ref),
                (bucket_hbm, bucket_ref),
                (sign_hbm, sign_ref),
            ]
        )
    ]
    for copy in copies:
        copy.start()
    for copy in copies:
        copy.wait()
    rows = design_ref.shape[0]
    design = design_ref[...]
    fitted = lax.dot_general(
        coeffs_ref[...].reshape(1, -1),
        design,
        (((1,), (1,)), ((), ())),
        preferred_element_type=jnp.float32,
    )
    residual = target_ref[...].reshape(1, rows) - fitted
    blocks = level_ref.shape[0]
    lane = lax.broadcasted_iota(jnp.int32, (1, rows), 1)
    level = jnp.full((1, rows), level_ref[0], jnp.int32)
    for block in range(1, blocks):
        level = jnp.where(lane >= block * (rows // blocks), level_ref[block], level)
    quantile = 0.1 + 0.25 * level.astype(jnp.float32)
    upper = jax.nn.sigmoid(residual / 0.2)
    weight = (quantile * upper + (1.0 - quantile) * (1.0 - upper)) / jnp.sqrt(
        residual * residual + 0.25
    )
    sign = 2.0 * sign_ref[...].reshape(1, rows).astype(jnp.float32) - 1.0
    signed = (sign * jnp.sqrt(weight)).astype(jnp.bfloat16).astype(jnp.float32)
    slots = lax.broadcasted_iota(jnp.int32, (KB, rows), 0)
    embed = jnp.where(slots == bucket_ref[...].reshape(1, rows), signed, 0.0).astype(jnp.bfloat16)
    out_ref[...] = jnp.dot(embed, design, preferred_element_type=jnp.float32).astype(jnp.bfloat16)


def sketch_local(design, target, coeffs, tau_level, bucket, sign_bit):
    rows, columns = design.shape
    anywhere = pl.BlockSpec(memory_space=pltpu.HBM)
    return pl.pallas_call(
        sketch_kernel,
        out_shape=jax.ShapeDtypeStruct((KB, columns), jnp.bfloat16),
        in_specs=[anywhere] * 3 + [pl.BlockSpec(memory_space=pltpu.SMEM)] + [anywhere] * 2,
        out_specs=pl.BlockSpec(memory_space=pltpu.VMEM),
        scratch_shapes=[
            pltpu.VMEM((rows, columns), jnp.bfloat16),
            pltpu.VMEM((rows,), jnp.float32),
            pltpu.VMEM((columns,), jnp.bfloat16),
            pltpu.VMEM((rows,), jnp.int32),
            pltpu.VMEM((rows,), jnp.int32),
            pltpu.SemaphoreType.DMA((5,)),
        ],
        compiler_params=pltpu.CompilerParams(vmem_limit_bytes=67043328),
    )(design, target, coeffs, tau_level, bucket, sign_bit)


def half(block):
    return block.astype(jnp.bfloat16)


def mul(left, right):
    return jnp.dot(left, right, preferred_element_type=jnp.float32)


def diagonal_mask(width):
    rows = lax.broadcasted_iota(jnp.int32, (width, width), 0)
    columns = lax.broadcasted_iota(jnp.int32, (width, width), 1)
    return rows == columns


def root_factors(grams, offs):
    w, t, x, z = [], [], [], []
    for gram, off in zip(grams, offs):
        bound = jnp.max(jnp.sum(jnp.abs(gram), axis=0, keepdims=True), axis=1, keepdims=True)
        w.append(1.0 / bound)
        t.append(1.5 - 0.5 * w[-1])
        x.append((-0.5 * w[-1] / t[-1]) * off)
        z.append(t[-1] * lax.rsqrt(bound))
    xs, halves = [x], [[half(a) for a in x]]
    for _ in range(NS_ITERS - 1):
        thin = halves[-1]
        after = [1.5 - 0.5 * a * a * b for a, b in zip(t, w)]
        gain = [a * a * a / b for a, b in zip(t, after)]
        linear = [g * (1.0 - b / a) for g, a, b in zip(gain, t, w)]
        square = [g * (2.0 - 0.5 * b / a) for g, a, b in zip(gain, t, w)]
        inner = [
            half(q * a + g * mul(b, b)) for q, g, a, b in zip(square, gain, x, thin)
        ]
        x = [p * a + mul(r, b) for p, a, b, r in zip(linear, x, thin, inner)]
        w = [a * a * b for a, b in zip(t, w)]
        t = after
        z = [a * b for a, b in zip(z, t)]
        xs.append(x)
        halves.append([half(a) for a in x])
    while len(xs) > 1:
        merged, thinner = [], []
        for k in range(0, len(xs) - 1, 2):
            merged.append(
                [
                    a + b + mul(d, c)
                    for a, b, c, d in zip(xs[k], xs[k + 1], halves[k], halves[k + 1])
                ]
            )
            thinner.append([half(a) for a in merged[-1]])
        if len(xs) % 2:
            merged.append(xs[-1])
            thinner.append(halves[-1])
        xs, halves = merged, thinner
    return list(zip(z, xs[0], halves[0]))


def diagonal_of(block, axis):
    return jnp.sum(jnp.where(diagonal_mask(block.shape[0]), block, 0.0), axis=axis, keepdims=True)


def ring_place(index, count):
    return jnp.where(index % 2 == 0, index // 2, count - 1 - index // 2)


def ring_index(place, count):
    return jnp.where(place < count // 2, 2 * place, 2 * (count - 1 - place) + 1)


def ring_origins(count):
    here = ring_place(lax.axis_index("row"), count)
    turns = [0] + [step for k in range(1, count // 2) for step in (-k, k)] + [count // 2]
    return [ring_index((here + turn + count) % count, count) for turn in turns]


def panel_columns(order_ref, count):
    position = lax.axis_index("row")
    return [
        pl.multiple_of(order_ref[jnp.bitwise_xor(position, j)] * PANEL, PANEL)
        for j in range(count)
    ]


def gather_panels(columns, chunks, ordered_ref, turned_ref):
    start = 0
    for chunk in chunks:
        rows = chunk.shape[0]
        for j, column in enumerate(columns):
            ordered_ref[start : start + rows, j * PANEL : (j + 1) * PANEL] = chunk[
                :, pl.ds(column, PANEL)
            ]
        start += rows
    for p in range(0, len(columns), 2):
        span = slice(p * PANEL, (p + 2) * PANEL)
        turned_ref[span] = ordered_ref[:, span].T


def tall_gram(turned_ref, ordered_ref, b):
    return mul(turned_ref[: (b + 2) * PANEL], ordered_ref[:, b * PANEL : (b + 2) * PANEL])


def gram_kernel(count, pieces, order_ref, *refs):
    chunks, (ordered_ref, *tall_refs), turned_ref = refs[:pieces], refs[pieces:-1], refs[-1]
    gather_panels(panel_columns(order_ref, count), chunks, ordered_ref, turned_ref)
    for k, tall_ref in enumerate(tall_refs):
        tall_ref[...] = tall_gram(turned_ref, ordered_ref, 2 * k)


def rounds_kernel(count, pieces, order_ref, *refs):
    chunks, refs = refs[:pieces], refs[pieces:]
    early_ref, tall_refs = refs[0], refs[1 : 1 + count // 2]
    out_ref, ordered_ref, turned_ref = refs[1 + count // 2 :]
    width = PANEL
    depth = count.bit_length() - 1
    gather_panels(panel_columns(order_ref, count), chunks, ordered_ref, turned_ref)

    live = [None] * (ROUNDS + 1)
    live[ROUNDS] = [0]
    for turn in reversed(range(ROUNDS)):
        bit = 1 << turn % depth
        live[turn] = sorted({a for p in live[turn + 1] for a in (p, p ^ bit)})

    row_scale, column_scale, total, grams = {}, {}, {}, {}
    for b in range(0, count, 2):
        tall = tall_refs[b // 2][...] + tall_gram(turned_ref, ordered_ref, b)
        for i in range(b + 2):
            for j in range(2):
                if i <= b + j:
                    grams[i, b + j] = tall[
                        i * width : (i + 1) * width, j * width : (j + 1) * width
                    ]
    for p in range(count):
        total[p] = diagonal_of(grams[p, p], 0)
        row_scale[p] = lax.rsqrt(total[p])
        column_scale[p] = lax.rsqrt(diagonal_of(grams[p, p], 1))
    first_scale = dict(column_scale)
    blocks = {
        (a, b): column_scale[a] * gram * row_scale[b] for (a, b), gram in grams.items()
    }
    eye = diagonal_mask(width)

    def joined_from(blocks):
        def joined(left, right, corner=lambda block: block):
            def block_of(a, b):
                if a == b:
                    return corner(blocks[a, a])
                return blocks[a, b] if (a, b) in blocks else blocks[b, a].T

            return jnp.concatenate(
                [jnp.concatenate([block_of(a, b) for b in right], axis=1) for a in left], axis=0
            )

        return joined

    history = []
    finish = None
    for turn in range(ROUNDS):
        bit = 1 << turn % depth
        pairs = [(p, p | bit) for p in live[turn] if not p & bit]
        joined = joined_from(blocks)
        whole = [joined(pair, pair) for pair in pairs]
        offs = [
            joined(pair, pair, lambda block: jnp.where(eye, 0.0, block)) for pair in pairs
        ]
        factors = root_factors(whole, offs)
        if finish is not None:
            finish()
        keep = live[turn + 1]
        scales = {}
        if turn + 1 < ROUNDS:
            kept = [[i for i in range(2) if pair[i] in keep] for pair in pairs]
            spans = [
                slice(k[0] * width, (k[-1] + 1) * width) for k in kept
            ]
            fresh, row_scale, column_scale = {}, {}, {}
            for i, pair in enumerate(pairs):
                z, e, thin = factors[i]
                span = spans[i]
                part = offs[i][span] + e[span] + mul(thin[span], half(offs[i]))
                value = part[:, span] + e[span, span] + mul(half(part), thin[:, span])
                for k, at in enumerate(kept[i]):
                    cut = slice(k * width, (k + 1) * width)
                    block = value[cut, cut] + jnp.where(eye, 1.0, 0.0)
                    along = diagonal_of(block, 0)
                    row_scale[pair[at]] = lax.rsqrt(along)
                    column_scale[pair[at]] = lax.rsqrt(diagonal_of(block, 1))
                    total[pair[at]] = total[pair[at]] * along * z * z
                    fresh[pair[at], pair[at]] = block
                    for j, to in list(enumerate(kept[i]))[k + 1 :]:
                        fresh[pair[at], pair[to]] = value[cut, j * width : (j + 1) * width]
            following = 1 << (turn + 1) % depth
            soon, later = [], []
            for j in range(1, len(pairs)):
                near = [
                    i
                    for i in range(j)
                    if any(a ^ following in pairs[j] for a in pairs[i])
                ]
                soon.append((j, near))
                later.append((j, [i for i in range(j) if i not in near]))

            def cross(work, joined, pairs, factors, kept, spans, fresh):
                for j, members in work:
                    if not members:
                        continue
                    tops = []
                    for i in members:
                        source = joined(pairs[i], pairs[j])
                        tops.append(
                            source[spans[i]] + mul(factors[i][2][spans[i]], half(source))
                        )
                    tall = jnp.concatenate(tops, axis=0)
                    tall = tall[:, spans[j]] + mul(half(tall), factors[j][2][:, spans[j]])
                    start = 0
                    for i in members:
                        for at in kept[i]:
                            for k, to in enumerate(kept[j]):
                                fresh[pairs[i][at], pairs[j][to]] = tall[
                                    start : start + width, k * width : (k + 1) * width
                                ]
                            start += width

            def scaled(fresh, column_scale, row_scale):
                return {
                    (a, b): column_scale[a] * value * row_scale[b]
                    for (a, b), value in fresh.items()
                }

            known = (joined_from(blocks), pairs, factors, kept, spans)
            cross(soon, *known, fresh)
            blocks = scaled(fresh, column_scale, row_scale)

            def finish(blocks=blocks, later=later, known=known, down=column_scale, along=row_scale):
                rest = {}
                cross(later, *known, rest)
                blocks.update(scaled(rest, down, along))

            scales = column_scale
        history.append((pairs, factors, scales))

    pairs, factors, _ = history[-1]
    z, e, _ = factors[0]
    combined = {
        pairs[0][0]: jnp.where(eye, 1.0, 0.0) + e[:width, :width],
        pairs[0][1]: e[width:, :width],
    }
    final = z * jnp.sqrt(total[0])
    for pairs, factors, scales in reversed(history[:-1]):
        following = {}
        for pair, (z, e, thin) in zip(pairs, factors):
            parts = [i for i in range(2) if pair[i] in combined]
            tops = {i: scales[pair[i]] * combined[pair[i]] for i in parts}
            stacked = half(jnp.concatenate([tops[i] for i in parts], axis=0))
            moved = mul(thin[:, parts[0] * width : (parts[-1] + 1) * width], stacked)
            for i in range(2):
                rows = moved[i * width : (i + 1) * width]
                following[pair[i]] = tops[i] + rows if i in tops else rows
        combined = following
    weights = jnp.concatenate(
        [first_scale[p] * combined[p] for p in range(count)], axis=0
    ) * final
    high = half(weights)
    low = half(weights - high.astype(jnp.float32))
    own = out_ref.shape[0]
    chunk = own // count
    both = jnp.concatenate([high, low], axis=1)
    origins = ring_origins(count)
    for source_ref, first, rows in ((early_ref, 0, own - chunk), (ordered_ref, count - 1, chunk)):
        product = mul(source_ref[:rows], both)
        result = product[:, :width] + product[:, width:]
        for k in range(rows // chunk):
            start = pl.multiple_of(origins[first + k] * chunk, chunk)
            out_ref[pl.ds(start, chunk), :] = result[k * chunk : (k + 1) * chunk]


def all_rounds(mine, other, panel_order):
    count = panel_order.shape[0]
    total = mine[0].shape[1]
    inside = pl.BlockSpec(memory_space=pltpu.VMEM)
    numbers = pl.BlockSpec(memory_space=pltpu.SMEM)
    early = mine[:-2] + other[:-2]
    last = mine[-2:] + other[-2:]
    early_rows = sum(block.shape[0] for block in early)
    last_rows = sum(block.shape[0] for block in last)
    early_gram = pl.pallas_call(
        functools.partial(gram_kernel, count, len(early)),
        out_shape=[jax.ShapeDtypeStruct((early_rows, total), jnp.bfloat16)]
        + [
            jax.ShapeDtypeStruct(((b + 2) * PANEL, 2 * PANEL), jnp.float32)
            for b in range(0, count, 2)
        ],
        in_specs=[numbers] + [inside] * len(early),
        out_specs=[inside] * (1 + count // 2),
        scratch_shapes=[pltpu.VMEM((total, early_rows), jnp.bfloat16)],
        compiler_params=pltpu.CompilerParams(vmem_limit_bytes=16 << 20),
        cost_estimate=pl.CostEstimate(
            flops=2 * early_rows * total * total,
            bytes_accessed=4 * early_rows * total + 3 * total * total,
            transcendentals=0,
        ),
    )
    ordered, *talls = early_gram(panel_order, *early)
    return pl.pallas_call(
        functools.partial(rounds_kernel, count, len(last)),
        out_shape=jax.ShapeDtypeStruct(((early_rows + last_rows) // 2, PANEL), jnp.float32),
        in_specs=[numbers] + [inside] * (len(last) + 1 + len(talls)),
        out_specs=inside,
        scratch_shapes=[
            pltpu.VMEM((last_rows, total), jnp.bfloat16),
            pltpu.VMEM((total, last_rows), jnp.bfloat16),
        ],
        compiler_params=pltpu.CompilerParams(vmem_limit_bytes=32 << 20),
    )(panel_order, *last, ordered, *talls)


def ring_gather(block, axis):
    count = lax.axis_size(axis)
    ring = list(range(0, count, 2)) + list(range(1, count, 2))[::-1]
    onward = [(ring[i], ring[(i + 1) % count]) for i in range(count)]
    back = [(b, a) for a, b in onward]
    blocks = [block]
    ahead = behind = block
    for _ in range(1, count // 2):
        ahead = lax.ppermute(ahead, axis, onward)
        behind = lax.ppermute(behind, axis, back)
        blocks += [ahead, behind]
    middle = block.shape[0] // 2
    blocks.append(lax.ppermute(ahead[:middle], axis, onward))
    blocks.append(lax.ppermute(behind[middle:], axis, back))
    return blocks


def gathered_rounds(sketch, panel_order):
    mine = ring_gather(sketch, "row")
    other = [lax.ppermute(block, "grp", [(0, 1), (1, 0)]) for block in mine]
    return all_rounds(mine, other, panel_order)


def pair_transform(gram):
    squares = jnp.sum(jnp.where(diagonal_mask(gram.shape[0]), gram, 0.0), axis=0)
    inv_root = lax.rsqrt(squares)
    normed = gram * inv_root[:, None] * inv_root[None, :]
    bound = jnp.max(jnp.sum(jnp.abs(normed), axis=1))
    identity = jnp.eye(gram.shape[0], dtype=jnp.float32)
    current = normed / bound
    inverse = identity
    for _ in range(NS_ITERS):
        middle = 1.5 * identity - 0.5 * jnp.dot(inverse, current, precision=lax.Precision.HIGHEST)
        current_next = jnp.dot(current, middle, precision=lax.Precision.HIGHEST)
        inverse = jnp.dot(middle, inverse, precision=lax.Precision.HIGHEST)
        current = current_next
    return inv_root[:, None] * inverse * (jnp.sqrt(squares) / jnp.sqrt(bound))[None, :]


def cross_product(left, right):
    return lax.dot_general(
        left,
        right,
        (((0,), (0,)), ((), ())),
        precision=lax.Precision.HIGHEST,
        preferred_element_type=jnp.float32,
    )


def gram_blocks(own, partner):
    return (cross_product(own, own), cross_product(own, partner), cross_product(partner, partner))


def pair_update(own, partner, blocks, lower):
    self_gram, cross_gram, other_gram = blocks
    low_low = jnp.where(lower, self_gram, other_gram)
    high_high = jnp.where(lower, other_gram, self_gram)
    low_high = jnp.where(lower, cross_gram, cross_gram.T)
    gram = jnp.concatenate(
        [
            jnp.concatenate([low_low, low_high], axis=1),
            jnp.concatenate([low_high.T, high_high], axis=1),
        ],
        axis=0,
    )
    mixing = pair_transform(gram)
    width = own.shape[1]
    own_own = jnp.where(lower, mixing[:width, :width], mixing[width:, width:])
    other_own = jnp.where(lower, mixing[width:, :width], mixing[:width, width:])
    return jnp.dot(own, own_own, precision=lax.Precision.HIGHEST) + jnp.dot(
        partner, other_own, precision=lax.Precision.HIGHEST
    )


def exchanged_rounds(sketch, panel_order):
    panels = sketch.reshape(KB, -1, PANEL)
    ordered = jnp.take(panels, panel_order, axis=1).reshape(KB, -1)
    regrouped = lax.all_to_all(ordered, "row", split_axis=1, concat_axis=0, tiled=True)
    half_rows = regrouped.shape[0]
    depth = lax.axis_size("row").bit_length() - 1
    position = lax.axis_index("row")
    working = lax.all_gather(regrouped, "grp", axis=0, tiled=True).astype(jnp.float32)
    for turn in range(ROUNDS):
        bit = turn % depth
        partner = swapped(working.astype(jnp.bfloat16), "row", bit).astype(working.dtype)
        lower = position >> bit & 1 == 0
        working = pair_update(working, partner, gram_blocks(working, partner), lower)
    return lax.dynamic_slice_in_dim(working, lax.axis_index("grp") * half_rows, half_rows, 0)


def gathers(devices, columns):
    return 2 * KB * devices * columns + 4 * columns * columns <= GATHER_BYTES


def per_device(design, target, coeffs, tau_level, bucket, sign_bit, panel_order):
    sketch = sketch_local(design, target, coeffs, tau_level, bucket, sign_bit)
    columns = design.shape[1]
    if gathers(lax.axis_size("row") * lax.axis_size("grp"), columns):
        return gathered_rounds(sketch, panel_order)
    return exchanged_rounds(sketch, panel_order)


def solution(mesh):
    placed = (
        P(("parts", "grp", "row"), None),
        P(("parts", "grp", "row")),
        P("parts"),
        P(("parts", "grp", "row")),
        P(("parts", "grp", "row")),
        P(("parts", "grp", "row")),
        P("parts"),
    )
    return jax.shard_map(
        per_device,
        mesh=mesh,
        in_specs=placed,
        out_specs=P(("parts", "grp"), "row"),
        check_vma=False,
    )
```

```python
import functools

import jax
import jax.numpy as jnp
from jax import lax
from jax.experimental import pallas as pl
from jax.experimental.pallas import tpu as pltpu
from jax.sharding import PartitionSpec as P

PANEL = 128
KB = 64
ROUNDS = 5
NS_ITERS = 4
GATHER_BYTES = 12 << 20


def swapped(block, axis, bit):
    count = lax.axis_size(axis)
    route = []
    for low in range(count):
        high = low | 1 << bit
        if high != low and high < count:
            route += [(low, high), (high, low)]
    return lax.ppermute(block, axis, route)


def sketch_kernel(design_hbm, target_hbm, coeffs_hbm, level_ref, bucket_hbm, sign_hbm, order_ref,
                  out_ref, design_ref, target_ref, coeffs_ref, bucket_ref, sign_ref, arrived):
    copies = [
        pltpu.make_async_copy(source, here, arrived.at[i])
        for i, (source, here) in enumerate(
            [
                (coeffs_hbm, coeffs_ref),
                (design_hbm, design_ref),
                (target_hbm, target_ref),
                (bucket_hbm, bucket_ref),
                (sign_hbm, sign_ref),
            ]
        )
    ]
    for copy in copies:
        copy.start()
    for copy in copies:
        copy.wait()
    rows = design_ref.shape[0]
    design = design_ref[...]
    fitted = lax.dot_general(
        coeffs_ref[...].reshape(1, -1),
        design,
        (((1,), (1,)), ((), ())),
        preferred_element_type=jnp.float32,
    )
    residual = target_ref[...].reshape(1, rows) - fitted
    blocks = level_ref.shape[0]
    lane = lax.broadcasted_iota(jnp.int32, (1, rows), 1)
    level = jnp.full((1, rows), level_ref[0], jnp.int32)
    for block in range(1, blocks):
        level = jnp.where(lane >= block * (rows // blocks), level_ref[block], level)
    quantile = 0.1 + 0.25 * level.astype(jnp.float32)
    upper = jax.nn.sigmoid(residual / 0.2)
    weight = (quantile * upper + (1.0 - quantile) * (1.0 - upper)) / jnp.sqrt(
        residual * residual + 0.25
    )
    sign = 2.0 * sign_ref[...].reshape(1, rows).astype(jnp.float32) - 1.0
    signed = (sign * jnp.sqrt(weight)).astype(jnp.bfloat16).astype(jnp.float32)
    slots = lax.broadcasted_iota(jnp.int32, (KB, rows), 0)
    embed = jnp.where(slots == bucket_ref[...].reshape(1, rows), signed, 0.0).astype(jnp.bfloat16)
    for j in range(order_ref.shape[0]):
        column = pl.multiple_of(order_ref[j] * PANEL, PANEL)
        out_ref[:, j * PANEL : (j + 1) * PANEL] = jnp.dot(
            embed, design_ref[:, pl.ds(column, PANEL)], preferred_element_type=jnp.float32
        ).astype(jnp.bfloat16)


def sketch_local(design, target, coeffs, tau_level, bucket, sign_bit, panel_order):
    rows, columns = design.shape
    anywhere = pl.BlockSpec(memory_space=pltpu.HBM)
    numbers = pl.BlockSpec(memory_space=pltpu.SMEM)
    return pl.pallas_call(
        sketch_kernel,
        out_shape=jax.ShapeDtypeStruct((KB, columns), jnp.bfloat16),
        in_specs=[anywhere] * 3 + [numbers] + [anywhere] * 2 + [numbers],
        out_specs=pl.BlockSpec(memory_space=pltpu.VMEM),
        scratch_shapes=[
            pltpu.VMEM((rows, columns), jnp.bfloat16),
            pltpu.VMEM((rows,), jnp.float32),
            pltpu.VMEM((columns,), jnp.bfloat16),
            pltpu.VMEM((rows,), jnp.int32),
            pltpu.VMEM((rows,), jnp.int32),
            pltpu.SemaphoreType.DMA((5,)),
        ],
        compiler_params=pltpu.CompilerParams(vmem_limit_bytes=67043328),
    )(design, target, coeffs, tau_level, bucket, sign_bit, panel_order)


def half(block):
    return block.astype(jnp.bfloat16)


def mul(left, right):
    return jnp.dot(left, right, preferred_element_type=jnp.float32)


def diagonal_mask(width):
    rows = lax.broadcasted_iota(jnp.int32, (width, width), 0)
    columns = lax.broadcasted_iota(jnp.int32, (width, width), 1)
    return rows == columns


def root_factors(grams, offs):
    w, t, v, z = [], [], [], []
    for gram, off in zip(grams, offs):
        bound = jnp.max(jnp.sum(jnp.abs(gram), axis=0, keepdims=True), axis=1, keepdims=True)
        w.append(1.0 / bound)
        t.append(1.5 - 0.5 * w[-1])
        v.append((-0.5 * w[-1] / t[-1]) * off)
        z.append(lax.rsqrt(bound))
    s = [jnp.ones_like(a) for a in w]
    thin = [half(a) for a in v]
    doubles = []
    for step in range(NS_ITERS):
        z = [a * b for a, b in zip(z, t)]
        after = [1.5 - 0.5 * a * a * b for a, b in zip(t, w)]
        gain = [a * a * a / b for a, b in zip(t, after)]
        linear = [1.0 - b / a for a, b in zip(t, w)]
        square = [2.0 - 0.5 * b / a for a, b in zip(t, w)]
        if step % 2 == 0:
            squared = [mul(a, a) for a in thin]
        if step % 2 == 0 and step + 2 >= NS_ITERS and step + 1 < NS_ITERS:
            parts = []
            for g, a, b, c, x, q in zip(gain, linear, square, s, v, squared):
                outer = half(q)
                inner = half((g * (1.0 + b) * c * c * c) * x + (g * c * c * c * c) * q)
                parts.append(
                    ((1.0 + g * a) * c) * x + (g * (a + b) * c * c) * q + mul(inner, outer)
                )
            doubles.append(parts)
        elif step % 2 == 0 and step + 1 == NS_ITERS:
            doubles.append([c * x for c, x in zip(s, v)])
        if step + 2 < NS_ITERS or step % 2 == 1 and step + 1 < NS_ITERS:
            if step % 2 == 1:
                squared = [mul(a, a) for a in thin]
            inner = [half((b / c) * x + q) for b, c, x, q in zip(square, s, v, squared)]
            before, flat, size = v, thin, s
            v = [
                (a / (c * c)) * x + mul(r, y)
                for a, c, x, r, y in zip(linear, s, v, inner, thin)
            ]
            thin = [half(a) for a in v]
            s = [g * c * c * c for g, c in zip(gain, s)]
            if step % 2 == 0:
                doubles.append(
                    [
                        c * x + d * (y + c * mul(a, b))
                        for c, x, d, y, a, b in zip(size, before, s, v, thin, flat)
                    ]
                )
        w = [a * a * b for a, b in zip(t, w)]
        t = after
    e = doubles[0]
    thin = [half(a) for a in e]
    for parts in doubles[1:]:
        e = [a + b + mul(half(b), c) for a, b, c in zip(e, parts, thin)]
        thin = [half(a) for a in e]
    return list(zip(z, e, thin))


def diagonal_of(block, axis):
    return jnp.sum(jnp.where(diagonal_mask(block.shape[0]), block, 0.0), axis=axis, keepdims=True)


def ring_place(index, count):
    return jnp.where(index % 2 == 0, index // 2, count - 1 - index // 2)


def ring_index(place, count):
    return jnp.where(place < count // 2, 2 * place, 2 * (count - 1 - place) + 1)


def ring_origins(count):
    here = ring_place(lax.axis_index("row"), count)
    turns = [0] + [step for k in range(1, count // 2) for step in (-k, k)] + [count // 2]
    return [ring_index((here + turn + count) % count, count) for turn in turns]


def gather_panels(count, chunks, ordered_ref, turned_ref):
    position = lax.axis_index("row")
    start = 0
    for chunk in chunks:
        rows = chunk.shape[0]
        for j in range(count):
            column = pl.multiple_of(jnp.bitwise_xor(position, j) * PANEL, PANEL)
            ordered_ref[start : start + rows, j * PANEL : (j + 1) * PANEL] = chunk[
                :, pl.ds(column, PANEL)
            ]
        start += rows
    for p in range(0, count, 2):
        span = slice(p * PANEL, (p + 2) * PANEL)
        turned_ref[span] = ordered_ref[:, span].T


def tall_gram(turned_ref, ordered_ref, b):
    return mul(turned_ref[: (b + 2) * PANEL], ordered_ref[:, b * PANEL : (b + 2) * PANEL])


def gram_kernel(count, pieces, first_hbm, *refs):
    chunks, (ordered_ref, *tall_refs) = refs[:pieces], refs[pieces:-3]
    turned_ref, first_ref, arrived = refs[-3:]
    copy = pltpu.make_async_copy(first_hbm, first_ref, arrived)
    copy.start()
    copy.wait()
    gather_panels(count, (first_ref, *chunks), ordered_ref, turned_ref)
    for k, tall_ref in enumerate(tall_refs):
        tall_ref[...] = tall_gram(turned_ref, ordered_ref, 2 * k)


def rounds_kernel(count, pieces, *refs):
    chunks, refs = refs[:pieces], refs[pieces:]
    early_ref, tall_refs = refs[0], refs[1 : 1 + count // 2]
    out_ref, ordered_ref, turned_ref = refs[1 + count // 2 :]
    width = PANEL
    depth = count.bit_length() - 1
    gather_panels(count, chunks, ordered_ref, turned_ref)

    live = [None] * (ROUNDS + 1)
    live[ROUNDS] = [0]
    for turn in reversed(range(ROUNDS)):
        bit = 1 << turn % depth
        live[turn] = sorted({a for p in live[turn + 1] for a in (p, p ^ bit)})

    row_scale, column_scale, total, grams = {}, {}, {}, {}
    for b in range(0, count, 2):
        tall = tall_refs[b // 2][...] + tall_gram(turned_ref, ordered_ref, b)
        for i in range(b + 2):
            for j in range(2):
                if i <= b + j:
                    grams[i, b + j] = tall[
                        i * width : (i + 1) * width, j * width : (j + 1) * width
                    ]
    for p in range(count):
        total[p] = diagonal_of(grams[p, p], 0)
        row_scale[p] = lax.rsqrt(total[p])
        column_scale[p] = lax.rsqrt(diagonal_of(grams[p, p], 1))
    first_scale = dict(column_scale)
    blocks = {
        (a, b): column_scale[a] * gram * row_scale[b] for (a, b), gram in grams.items()
    }
    eye = diagonal_mask(width)

    def joined_from(blocks):
        def joined(left, right, corner=lambda block: block):
            def block_of(a, b):
                if a == b:
                    return corner(blocks[a, a])
                return blocks[a, b] if (a, b) in blocks else blocks[b, a].T

            return jnp.concatenate(
                [jnp.concatenate([block_of(a, b) for b in right], axis=1) for a in left], axis=0
            )

        return joined

    history = []
    finish = None
    for turn in range(ROUNDS):
        bit = 1 << turn % depth
        pairs = [(p, p | bit) for p in live[turn] if not p & bit]
        joined = joined_from(blocks)
        whole = [joined(pair, pair) for pair in pairs]
        offs = [
            joined(pair, pair, lambda block: jnp.where(eye, 0.0, block)) for pair in pairs
        ]
        factors = root_factors(whole, offs)
        if finish is not None:
            finish()
        keep = live[turn + 1]
        scales = {}
        if turn + 1 < ROUNDS:
            kept = [[i for i in range(2) if pair[i] in keep] for pair in pairs]
            spans = [
                slice(k[0] * width, (k[-1] + 1) * width) for k in kept
            ]
            fresh, row_scale, column_scale = {}, {}, {}
            for i, pair in enumerate(pairs):
                z, e, thin = factors[i]
                span = spans[i]
                part = offs[i][span] + e[span] + mul(thin[span], half(offs[i]))
                value = part[:, span] + e[span, span] + mul(half(part), thin[:, span])
                for k, at in enumerate(kept[i]):
                    cut = slice(k * width, (k + 1) * width)
                    block = value[cut, cut] + jnp.where(eye, 1.0, 0.0)
                    along = diagonal_of(block, 0)
                    row_scale[pair[at]] = lax.rsqrt(along)
                    column_scale[pair[at]] = lax.rsqrt(diagonal_of(block, 1))
                    total[pair[at]] = total[pair[at]] * along * z * z
                    fresh[pair[at], pair[at]] = block
                    for j, to in list(enumerate(kept[i]))[k + 1 :]:
                        fresh[pair[at], pair[to]] = value[cut, j * width : (j + 1) * width]
            following = 1 << (turn + 1) % depth
            soon, later = [], []
            for j in range(1, len(pairs)):
                near = [
                    i
                    for i in range(j)
                    if any(a ^ following in pairs[j] for a in pairs[i])
                ]
                soon.append((j, near))
                later.append((j, [i for i in range(j) if i not in near]))

            def cross(work, joined, pairs, factors, kept, spans, fresh):
                for j, members in work:
                    if not members:
                        continue
                    tops = []
                    for i in members:
                        source = joined(pairs[i], pairs[j])
                        tops.append(
                            source[spans[i]] + mul(factors[i][2][spans[i]], half(source))
                        )
                    tall = jnp.concatenate(tops, axis=0)
                    tall = tall[:, spans[j]] + mul(half(tall), factors[j][2][:, spans[j]])
                    start = 0
                    for i in members:
                        for at in kept[i]:
                            for k, to in enumerate(kept[j]):
                                fresh[pairs[i][at], pairs[j][to]] = tall[
                                    start : start + width, k * width : (k + 1) * width
                                ]
                            start += width

            def scaled(fresh, column_scale, row_scale):
                return {
                    (a, b): column_scale[a] * value * row_scale[b]
                    for (a, b), value in fresh.items()
                }

            known = (joined_from(blocks), pairs, factors, kept, spans)
            cross(soon, *known, fresh)
            blocks = scaled(fresh, column_scale, row_scale)

            def finish(blocks=blocks, later=later, known=known, down=column_scale, along=row_scale):
                rest = {}
                cross(later, *known, rest)
                blocks.update(scaled(rest, down, along))

            scales = column_scale
        history.append((pairs, factors, scales))

    pairs, factors, _ = history[-1]
    z, e, _ = factors[0]
    combined = {
        pairs[0][0]: jnp.where(eye, 1.0, 0.0) + e[:width, :width],
        pairs[0][1]: e[width:, :width],
    }
    final = z * jnp.sqrt(total[0])
    for pairs, factors, scales in reversed(history[:-1]):
        following = {}
        for pair, (z, e, thin) in zip(pairs, factors):
            parts = [i for i in range(2) if pair[i] in combined]
            tops = {i: scales[pair[i]] * combined[pair[i]] for i in parts}
            stacked = half(jnp.concatenate([tops[i] for i in parts], axis=0))
            moved = mul(thin[:, parts[0] * width : (parts[-1] + 1) * width], stacked)
            for i in range(2):
                rows = moved[i * width : (i + 1) * width]
                following[pair[i]] = tops[i] + rows if i in tops else rows
        combined = following
    weights = jnp.concatenate(
        [first_scale[p] * combined[p] for p in range(count)], axis=0
    ) * final
    high = half(weights)
    low = half(weights - high.astype(jnp.float32))
    own = out_ref.shape[0]
    chunk = own // count
    both = jnp.concatenate([high, low], axis=1)
    origins = ring_origins(count)
    for source_ref, first, rows in ((early_ref, 0, own - chunk), (ordered_ref, count - 1, chunk)):
        product = mul(source_ref[:rows], both)
        result = product[:, :width] + product[:, width:]
        for k in range(rows // chunk):
            start = pl.multiple_of(origins[first + k] * chunk, chunk)
            out_ref[pl.ds(start, chunk), :] = result[k * chunk : (k + 1) * chunk]


def all_rounds(mine, other):
    total = mine[0].shape[1]
    count = total // PANEL
    inside = pl.BlockSpec(memory_space=pltpu.VMEM)
    early = mine[:-2] + other[:-2]
    last = mine[-2:] + other[-2:]
    early_rows = sum(block.shape[0] for block in early)
    last_rows = sum(block.shape[0] for block in last)
    early_gram = pl.pallas_call(
        functools.partial(gram_kernel, count, len(early) - 1),
        out_shape=[jax.ShapeDtypeStruct((early_rows, total), jnp.bfloat16)]
        + [
            jax.ShapeDtypeStruct(((b + 2) * PANEL, 2 * PANEL), jnp.float32)
            for b in range(0, count, 2)
        ],
        in_specs=[pl.BlockSpec(memory_space=pltpu.HBM)] + [inside] * (len(early) - 1),
        out_specs=[inside] * (1 + count // 2),
        scratch_shapes=[
            pltpu.VMEM((total, early_rows), jnp.bfloat16),
            pltpu.VMEM(mine[0].shape, jnp.bfloat16),
            pltpu.SemaphoreType.DMA,
        ],
        compiler_params=pltpu.CompilerParams(vmem_limit_bytes=16 << 20),
        cost_estimate=pl.CostEstimate(
            flops=2 * early_rows * total * total,
            bytes_accessed=4 * early_rows * total + 3 * total * total,
            transcendentals=0,
        ),
    )
    ordered, *talls = early_gram(*early)
    return pl.pallas_call(
        functools.partial(rounds_kernel, count, len(last)),
        out_shape=jax.ShapeDtypeStruct(((early_rows + last_rows) // 2, PANEL), jnp.float32),
        in_specs=[inside] * (len(last) + 1 + len(talls)),
        out_specs=inside,
        scratch_shapes=[
            pltpu.VMEM((last_rows, total), jnp.bfloat16),
            pltpu.VMEM((total, last_rows), jnp.bfloat16),
        ],
        compiler_params=pltpu.CompilerParams(vmem_limit_bytes=32 << 20),
    )(*last, ordered, *talls)


def ring_gather(block, axis):
    count = lax.axis_size(axis)
    ring = list(range(0, count, 2)) + list(range(1, count, 2))[::-1]
    onward = [(ring[i], ring[(i + 1) % count]) for i in range(count)]
    back = [(b, a) for a, b in onward]
    blocks = [block]
    ahead = behind = block
    for _ in range(1, count // 2):
        ahead = lax.ppermute(ahead, axis, onward)
        behind = lax.ppermute(behind, axis, back)
        blocks += [ahead, behind]
    middle = block.shape[0] // 2
    blocks.append(lax.ppermute(ahead[:middle], axis, onward))
    blocks.append(lax.ppermute(behind[middle:], axis, back))
    return blocks


def gathered_rounds(sketch):
    mine = ring_gather(sketch, "row")
    other = [lax.ppermute(block, "grp", [(0, 1), (1, 0)]) for block in mine]
    return all_rounds(mine, other)


def pair_transform(gram):
    squares = jnp.sum(jnp.where(diagonal_mask(gram.shape[0]), gram, 0.0), axis=0)
    inv_root = lax.rsqrt(squares)
    normed = gram * inv_root[:, None] * inv_root[None, :]
    bound = jnp.max(jnp.sum(jnp.abs(normed), axis=1))
    identity = jnp.eye(gram.shape[0], dtype=jnp.float32)
    current = normed / bound
    inverse = identity
    for _ in range(NS_ITERS):
        middle = 1.5 * identity - 0.5 * jnp.dot(inverse, current, precision=lax.Precision.HIGHEST)
        current_next = jnp.dot(current, middle, precision=lax.Precision.HIGHEST)
        inverse = jnp.dot(middle, inverse, precision=lax.Precision.HIGHEST)
        current = current_next
    return inv_root[:, None] * inverse * (jnp.sqrt(squares) / jnp.sqrt(bound))[None, :]


def cross_product(left, right):
    return lax.dot_general(
        left,
        right,
        (((0,), (0,)), ((), ())),
        precision=lax.Precision.HIGHEST,
        preferred_element_type=jnp.float32,
    )


def gram_blocks(own, partner):
    return (cross_product(own, own), cross_product(own, partner), cross_product(partner, partner))


def pair_update(own, partner, blocks, lower):
    self_gram, cross_gram, other_gram = blocks
    low_low = jnp.where(lower, self_gram, other_gram)
    high_high = jnp.where(lower, other_gram, self_gram)
    low_high = jnp.where(lower, cross_gram, cross_gram.T)
    gram = jnp.concatenate(
        [
            jnp.concatenate([low_low, low_high], axis=1),
            jnp.concatenate([low_high.T, high_high], axis=1),
        ],
        axis=0,
    )
    mixing = pair_transform(gram)
    width = own.shape[1]
    own_own = jnp.where(lower, mixing[:width, :width], mixing[width:, width:])
    other_own = jnp.where(lower, mixing[width:, :width], mixing[:width, width:])
    return jnp.dot(own, own_own, precision=lax.Precision.HIGHEST) + jnp.dot(
        partner, other_own, precision=lax.Precision.HIGHEST
    )


def exchanged_rounds(sketch):
    regrouped = lax.all_to_all(sketch, "row", split_axis=1, concat_axis=0, tiled=True)
    half_rows = regrouped.shape[0]
    depth = lax.axis_size("row").bit_length() - 1
    position = lax.axis_index("row")
    working = lax.all_gather(regrouped, "grp", axis=0, tiled=True).astype(jnp.float32)
    for turn in range(ROUNDS):
        bit = turn % depth
        partner = swapped(working.astype(jnp.bfloat16), "row", bit).astype(working.dtype)
        lower = position >> bit & 1 == 0
        working = pair_update(working, partner, gram_blocks(working, partner), lower)
    return lax.dynamic_slice_in_dim(working, lax.axis_index("grp") * half_rows, half_rows, 0)


def gathers(devices, columns):
    return 2 * KB * devices * columns + 4 * columns * columns <= GATHER_BYTES


def per_device(design, target, coeffs, tau_level, bucket, sign_bit, panel_order):
    sketch = sketch_local(design, target, coeffs, tau_level, bucket, sign_bit, panel_order)
    columns = design.shape[1]
    if gathers(lax.axis_size("row") * lax.axis_size("grp"), columns):
        return gathered_rounds(sketch)
    return exchanged_rounds(sketch)


def solution(mesh):
    placed = (
        P(("parts", "grp", "row"), None),
        P(("parts", "grp", "row")),
        P("parts"),
        P(("parts", "grp", "row")),
        P(("parts", "grp", "row")),
        P(("parts", "grp", "row")),
        P("parts"),
    )
    return jax.shard_map(
        per_device,
        mesh=mesh,
        in_specs=placed,
        out_specs=P(("parts", "grp"), "row"),
        check_vma=False,
    )
```

```python
import functools

import jax
import jax.numpy as jnp
from jax import lax
from jax.experimental import pallas as pl
from jax.experimental.pallas import tpu as pltpu
from jax.sharding import PartitionSpec as P

PANEL = 128
KB = 64
ROUNDS = 5
NS_ITERS = 4
GATHER_BYTES = 12 << 20


def swapped(block, axis, bit):
    count = lax.axis_size(axis)
    route = []
    for low in range(count):
        high = low | 1 << bit
        if high != low and high < count:
            route += [(low, high), (high, low)]
    return lax.ppermute(block, axis, route)


def sketch_kernel(design_hbm, target_hbm, coeffs_hbm, level_ref, bucket_hbm, sign_hbm, order_ref,
                  out_ref, design_ref, target_ref, coeffs_ref, bucket_ref, sign_ref, arrived):
    copies = [
        pltpu.make_async_copy(source, here, arrived.at[i])
        for i, (source, here) in enumerate(
            [
                (coeffs_hbm, coeffs_ref),
                (design_hbm, design_ref),
                (target_hbm, target_ref),
                (bucket_hbm, bucket_ref),
                (sign_hbm, sign_ref),
            ]
        )
    ]
    for copy in copies:
        copy.start()
    for copy in copies:
        copy.wait()
    rows = design_ref.shape[0]
    design = design_ref[...]
    fitted = lax.dot_general(
        coeffs_ref[...].reshape(1, -1),
        design,
        (((1,), (1,)), ((), ())),
        preferred_element_type=jnp.float32,
    )
    residual = target_ref[...].reshape(1, rows) - fitted
    blocks = level_ref.shape[0]
    lane = lax.broadcasted_iota(jnp.int32, (1, rows), 1)
    level = jnp.full((1, rows), level_ref[0], jnp.int32)
    for block in range(1, blocks):
        level = jnp.where(lane >= block * (rows // blocks), level_ref[block], level)
    quantile = 0.1 + 0.25 * level.astype(jnp.float32)
    upper = jax.nn.sigmoid(residual / 0.2)
    weight = (quantile * upper + (1.0 - quantile) * (1.0 - upper)) / jnp.sqrt(
        residual * residual + 0.25
    )
    sign = 2.0 * sign_ref[...].reshape(1, rows).astype(jnp.float32) - 1.0
    signed = (sign * jnp.sqrt(weight)).astype(jnp.bfloat16).astype(jnp.float32)
    slots = lax.broadcasted_iota(jnp.int32, (KB, rows), 0)
    embed = jnp.where(slots == bucket_ref[...].reshape(1, rows), signed, 0.0).astype(jnp.bfloat16)
    for j in range(order_ref.shape[0]):
        column = pl.multiple_of(order_ref[j] * PANEL, PANEL)
        out_ref[:, j * PANEL : (j + 1) * PANEL] = jnp.dot(
            embed, design_ref[:, pl.ds(column, PANEL)], preferred_element_type=jnp.float32
        ).astype(jnp.bfloat16)


def sketch_local(design, target, coeffs, tau_level, bucket, sign_bit, panel_order):
    rows, columns = design.shape
    anywhere = pl.BlockSpec(memory_space=pltpu.HBM)
    numbers = pl.BlockSpec(memory_space=pltpu.SMEM)
    return pl.pallas_call(
        sketch_kernel,
        out_shape=jax.ShapeDtypeStruct((KB, columns), jnp.bfloat16),
        in_specs=[anywhere] * 3 + [numbers] + [anywhere] * 2 + [numbers],
        out_specs=pl.BlockSpec(memory_space=pltpu.VMEM),
        scratch_shapes=[
            pltpu.VMEM((rows, columns), jnp.bfloat16),
            pltpu.VMEM((rows,), jnp.float32),
            pltpu.VMEM((columns,), jnp.bfloat16),
            pltpu.VMEM((rows,), jnp.int32),
            pltpu.VMEM((rows,), jnp.int32),
            pltpu.SemaphoreType.DMA((5,)),
        ],
        compiler_params=pltpu.CompilerParams(vmem_limit_bytes=67043328),
    )(design, target, coeffs, tau_level, bucket, sign_bit, panel_order)


def half(block):
    return block.astype(jnp.bfloat16)


def mul(left, right):
    return jnp.dot(left, right, preferred_element_type=jnp.float32)


def diagonal_mask(width):
    rows = lax.broadcasted_iota(jnp.int32, (width, width), 0)
    columns = lax.broadcasted_iota(jnp.int32, (width, width), 1)
    return rows == columns


def root_factors(grams, offs):
    w, t, v, z = [], [], [], []
    for gram, off in zip(grams, offs):
        bound = jnp.max(jnp.sum(jnp.abs(gram), axis=0, keepdims=True), axis=1, keepdims=True)
        w.append(1.0 / bound)
        t.append(1.5 - 0.5 * w[-1])
        v.append((-0.5 * w[-1] / t[-1]) * off)
        z.append(lax.rsqrt(bound))
    s = [jnp.ones_like(a) for a in w]
    thin = [half(a) for a in v]
    doubles = []
    for step in range(NS_ITERS):
        z = [a * b for a, b in zip(z, t)]
        after = [1.5 - 0.5 * a * a * b for a, b in zip(t, w)]
        gain = [a * a * a / b for a, b in zip(t, after)]
        linear = [1.0 - b / a for a, b in zip(t, w)]
        square = [2.0 - 0.5 * b / a for a, b in zip(t, w)]
        if step % 2 == 0:
            squared = [mul(a, a) for a in thin]
        if step % 2 == 0 and step + 2 >= NS_ITERS and step + 1 < NS_ITERS:
            parts = []
            for g, a, b, c, x, q in zip(gain, linear, square, s, v, squared):
                outer = half(q)
                inner = half((g * (1.0 + b) * c * c * c) * x + (g * c * c * c * c) * q)
                parts.append(
                    ((1.0 + g * a) * c) * x + (g * (a + b) * c * c) * q + mul(inner, outer)
                )
            doubles.append(parts)
        elif step % 2 == 0 and step + 1 == NS_ITERS:
            doubles.append([c * x for c, x in zip(s, v)])
        if step + 2 < NS_ITERS or step % 2 == 1 and step + 1 < NS_ITERS:
            if step % 2 == 1:
                squared = [mul(a, a) for a in thin]
            inner = [half((b / c) * x + q) for b, c, x, q in zip(square, s, v, squared)]
            before, flat, size = v, thin, s
            v = [
                (a / (c * c)) * x + mul(r, y)
                for a, c, x, r, y in zip(linear, s, v, inner, thin)
            ]
            thin = [half(a) for a in v]
            s = [g * c * c * c for g, c in zip(gain, s)]
            if step % 2 == 0:
                doubles.append(
                    [
                        c * x + d * (y + c * mul(a, b))
                        for c, x, d, y, a, b in zip(size, before, s, v, thin, flat)
                    ]
                )
        w = [a * a * b for a, b in zip(t, w)]
        t = after
    e = doubles[0]
    thin = [half(a) for a in e]
    for parts in doubles[1:]:
        e = [a + b + mul(half(b), c) for a, b, c in zip(e, parts, thin)]
        thin = [half(a) for a in e]
    return list(zip(z, e, thin))


def diagonal_of(block, axis):
    return jnp.sum(jnp.where(diagonal_mask(block.shape[0]), block, 0.0), axis=axis, keepdims=True)


def ring_place(index, count):
    return jnp.where(index % 2 == 0, index // 2, count - 1 - index // 2)


def ring_index(place, count):
    return jnp.where(place < count // 2, 2 * place, 2 * (count - 1 - place) + 1)


def ring_origins(count):
    here = ring_place(lax.axis_index("row"), count)
    turns = [0] + [step for k in range(1, count // 2) for step in (-k, k)] + [count // 2]
    return [ring_index((here + turn + count) % count, count) for turn in turns]


def gather_panels(count, chunks, ordered_ref, turned_ref):
    position = lax.axis_index("row")
    start = 0
    for chunk in chunks:
        rows = chunk.shape[0]
        for j in range(count):
            column = pl.multiple_of(jnp.bitwise_xor(position, j) * PANEL, PANEL)
            ordered_ref[start : start + rows, j * PANEL : (j + 1) * PANEL] = chunk[
                :, pl.ds(column, PANEL)
            ]
        start += rows
    for p in range(0, count, 2):
        span = slice(p * PANEL, (p + 2) * PANEL)
        turned_ref[span] = ordered_ref[:, span].T


def tall_gram(turned_ref, ordered_ref, b):
    return mul(turned_ref[: (b + 2) * PANEL], ordered_ref[:, b * PANEL : (b + 2) * PANEL])


def gram_kernel(count, pieces, *refs):
    chunks, before, after = refs[:pieces], refs[pieces : -2 - count // 2], refs[-2 - count // 2 :]
    ordered_ref, *tall_refs, turned_ref = after
    gather_panels(count, chunks, ordered_ref, turned_ref)
    for k, tall_ref in enumerate(tall_refs):
        tall = tall_gram(turned_ref, ordered_ref, 2 * k)
        tall_ref[...] = tall + before[k][...] if before else tall


def rounds_kernel(count, pieces, *refs):
    chunks, refs = refs[:pieces], refs[pieces:]
    *earlier, out_ref, ordered_ref, turned_ref = refs
    early_refs, tall_refs = earlier[: -(count // 2)], earlier[-(count // 2) :]
    width = PANEL
    depth = count.bit_length() - 1
    gather_panels(count, chunks, ordered_ref, turned_ref)

    live = [None] * (ROUNDS + 1)
    live[ROUNDS] = [0]
    for turn in reversed(range(ROUNDS)):
        bit = 1 << turn % depth
        live[turn] = sorted({a for p in live[turn + 1] for a in (p, p ^ bit)})

    row_scale, column_scale, total, grams = {}, {}, {}, {}
    for b in range(0, count, 2):
        tall = tall_refs[b // 2][...] + tall_gram(turned_ref, ordered_ref, b)
        for i in range(b + 2):
            for j in range(2):
                if i <= b + j:
                    grams[i, b + j] = tall[
                        i * width : (i + 1) * width, j * width : (j + 1) * width
                    ]
    for p in range(count):
        total[p] = diagonal_of(grams[p, p], 0)
        row_scale[p] = lax.rsqrt(total[p])
        column_scale[p] = lax.rsqrt(diagonal_of(grams[p, p], 1))
    first_scale = dict(column_scale)
    blocks = {
        (a, b): column_scale[a] * gram * row_scale[b] for (a, b), gram in grams.items()
    }
    eye = diagonal_mask(width)

    def joined_from(blocks):
        def joined(left, right, corner=lambda block: block):
            def block_of(a, b):
                if a == b:
                    return corner(blocks[a, a])
                return blocks[a, b] if (a, b) in blocks else blocks[b, a].T

            return jnp.concatenate(
                [jnp.concatenate([block_of(a, b) for b in right], axis=1) for a in left], axis=0
            )

        return joined

    history = []
    finish = None
    for turn in range(ROUNDS):
        bit = 1 << turn % depth
        pairs = [(p, p | bit) for p in live[turn] if not p & bit]
        joined = joined_from(blocks)
        whole = [joined(pair, pair) for pair in pairs]
        offs = [
            joined(pair, pair, lambda block: jnp.where(eye, 0.0, block)) for pair in pairs
        ]
        factors = root_factors(whole, offs)
        if finish is not None:
            finish()
        keep = live[turn + 1]
        scales = {}
        if turn + 1 < ROUNDS:
            kept = [[i for i in range(2) if pair[i] in keep] for pair in pairs]
            spans = [
                slice(k[0] * width, (k[-1] + 1) * width) for k in kept
            ]
            fresh, row_scale, column_scale = {}, {}, {}
            for i, pair in enumerate(pairs):
                z, e, thin = factors[i]
                span = spans[i]
                part = offs[i][span] + e[span] + mul(thin[span], half(offs[i]))
                value = part[:, span] + e[span, span] + mul(half(part), thin[:, span])
                for k, at in enumerate(kept[i]):
                    cut = slice(k * width, (k + 1) * width)
                    block = value[cut, cut] + jnp.where(eye, 1.0, 0.0)
                    along = diagonal_of(block, 0)
                    row_scale[pair[at]] = lax.rsqrt(along)
                    column_scale[pair[at]] = lax.rsqrt(diagonal_of(block, 1))
                    total[pair[at]] = total[pair[at]] * along * z * z
                    fresh[pair[at], pair[at]] = block
                    for j, to in list(enumerate(kept[i]))[k + 1 :]:
                        fresh[pair[at], pair[to]] = value[cut, j * width : (j + 1) * width]
            following = 1 << (turn + 1) % depth
            soon, later = [], []
            for j in range(1, len(pairs)):
                near = [
                    i
                    for i in range(j)
                    if any(a ^ following in pairs[j] for a in pairs[i])
                ]
                soon.append((j, near))
                later.append((j, [i for i in range(j) if i not in near]))

            def cross(work, joined, pairs, factors, kept, spans, fresh):
                for j, members in work:
                    if not members:
                        continue
                    tops = []
                    for i in members:
                        source = joined(pairs[i], pairs[j])
                        tops.append(
                            source[spans[i]] + mul(factors[i][2][spans[i]], half(source))
                        )
                    tall = jnp.concatenate(tops, axis=0)
                    tall = tall[:, spans[j]] + mul(half(tall), factors[j][2][:, spans[j]])
                    start = 0
                    for i in members:
                        for at in kept[i]:
                            for k, to in enumerate(kept[j]):
                                fresh[pairs[i][at], pairs[j][to]] = tall[
                                    start : start + width, k * width : (k + 1) * width
                                ]
                            start += width

            def scaled(fresh, column_scale, row_scale):
                return {
                    (a, b): column_scale[a] * value * row_scale[b]
                    for (a, b), value in fresh.items()
                }

            known = (joined_from(blocks), pairs, factors, kept, spans)
            cross(soon, *known, fresh)
            blocks = scaled(fresh, column_scale, row_scale)

            def finish(blocks=blocks, later=later, known=known, down=column_scale, along=row_scale):
                rest = {}
                cross(later, *known, rest)
                blocks.update(scaled(rest, down, along))

            scales = column_scale
        history.append((pairs, factors, scales))

    pairs, factors, _ = history[-1]
    z, e, _ = factors[0]
    combined = {
        pairs[0][0]: jnp.where(eye, 1.0, 0.0) + e[:width, :width],
        pairs[0][1]: e[width:, :width],
    }
    final = z * jnp.sqrt(total[0])
    for pairs, factors, scales in reversed(history[:-1]):
        following = {}
        for pair, (z, e, thin) in zip(pairs, factors):
            parts = [i for i in range(2) if pair[i] in combined]
            tops = {i: scales[pair[i]] * combined[pair[i]] for i in parts}
            stacked = half(jnp.concatenate([tops[i] for i in parts], axis=0))
            moved = mul(thin[:, parts[0] * width : (parts[-1] + 1) * width], stacked)
            for i in range(2):
                rows = moved[i * width : (i + 1) * width]
                following[pair[i]] = tops[i] + rows if i in tops else rows
        combined = following
    weights = jnp.concatenate(
        [first_scale[p] * combined[p] for p in range(count)], axis=0
    ) * final
    high = half(weights)
    low = half(weights - high.astype(jnp.float32))
    own = out_ref.shape[0]
    chunk = own // count
    both = jnp.concatenate([high, low], axis=1)
    origins = ring_origins(count)
    first = 0
    for source_ref in (*early_refs, ordered_ref):
        rows = source_ref.shape[0] // 2
        product = mul(source_ref[:rows], both)
        result = product[:, :width] + product[:, width:]
        for k in range(rows // chunk):
            start = pl.multiple_of(origins[first + k] * chunk, chunk)
            out_ref[pl.ds(start, chunk), :] = result[k * chunk : (k + 1) * chunk]
        first += rows // chunk


def add_gram(blocks, talls):
    rows, total = sum(block.shape[0] for block in blocks), blocks[0].shape[1]
    count = total // PANEL
    inside = pl.BlockSpec(memory_space=pltpu.VMEM)
    ordered, *talls = pl.pallas_call(
        functools.partial(gram_kernel, count, len(blocks)),
        out_shape=[jax.ShapeDtypeStruct((rows, total), jnp.bfloat16)]
        + [
            jax.ShapeDtypeStruct(((b + 2) * PANEL, 2 * PANEL), jnp.float32)
            for b in range(0, count, 2)
        ],
        in_specs=[inside] * (len(blocks) + len(talls)),
        out_specs=[inside] * (1 + count // 2),
        input_output_aliases={len(blocks) + k: 1 + k for k in range(len(talls))},
        scratch_shapes=[pltpu.VMEM((total, rows), jnp.bfloat16)],
        compiler_params=pltpu.CompilerParams(vmem_limit_bytes=16 << 20),
        cost_estimate=pl.CostEstimate(
            flops=2 * rows * total * total,
            bytes_accessed=4 * rows * total + 3 * total * total,
            transcendentals=0,
        ),
    )(*blocks, *talls)
    return ordered, talls


def all_rounds(mine, other):
    total = mine[0].shape[1]
    count = total // PANEL
    inside = pl.BlockSpec(memory_space=pltpu.VMEM)
    talls, early = [], []
    near = len(mine) // 3
    for span in (slice(0, near), slice(near, -2)):
        ordered, talls = add_gram(mine[span] + other[span], talls)
        early.append(ordered)
    last = mine[-2:] + other[-2:]
    last_rows = sum(block.shape[0] for block in last)
    own_rows = sum(block.shape[0] for block in mine)
    return pl.pallas_call(
        functools.partial(rounds_kernel, count, len(last)),
        out_shape=jax.ShapeDtypeStruct((own_rows, PANEL), jnp.float32),
        in_specs=[inside] * (len(last) + len(early) + len(talls)),
        out_specs=inside,
        scratch_shapes=[
            pltpu.VMEM((last_rows, total), jnp.bfloat16),
            pltpu.VMEM((total, last_rows), jnp.bfloat16),
        ],
        compiler_params=pltpu.CompilerParams(vmem_limit_bytes=32 << 20),
    )(*last, *early, *talls)


def ring_gather(block, axis):
    count = lax.axis_size(axis)
    ring = list(range(0, count, 2)) + list(range(1, count, 2))[::-1]
    onward = [(ring[i], ring[(i + 1) % count]) for i in range(count)]
    back = [(b, a) for a, b in onward]
    blocks = [block]
    ahead = behind = block
    for _ in range(1, count // 2):
        ahead = lax.ppermute(ahead, axis, onward)
        behind = lax.ppermute(behind, axis, back)
        blocks += [ahead, behind]
    middle = block.shape[0] // 2
    blocks.append(lax.ppermute(ahead[:middle], axis, onward))
    blocks.append(lax.ppermute(behind[middle:], axis, back))
    return blocks


def gathered_rounds(sketch):
    mine = ring_gather(sketch, "row")
    other = []
    for block in mine:
        other.append(lax.ppermute(block, "grp", [(0, 1), (1, 0)]))
    return all_rounds(mine, other)


def pair_transform(gram):
    squares = jnp.sum(jnp.where(diagonal_mask(gram.shape[0]), gram, 0.0), axis=0)
    inv_root = lax.rsqrt(squares)
    normed = gram * inv_root[:, None] * inv_root[None, :]
    bound = jnp.max(jnp.sum(jnp.abs(normed), axis=1))
    identity = jnp.eye(gram.shape[0], dtype=jnp.float32)
    current = normed / bound
    inverse = identity
    for _ in range(NS_ITERS):
        middle = 1.5 * identity - 0.5 * jnp.dot(inverse, current, precision=lax.Precision.HIGHEST)
        current_next = jnp.dot(current, middle, precision=lax.Precision.HIGHEST)
        inverse = jnp.dot(middle, inverse, precision=lax.Precision.HIGHEST)
        current = current_next
    return inv_root[:, None] * inverse * (jnp.sqrt(squares) / jnp.sqrt(bound))[None, :]


def cross_product(left, right):
    return lax.dot_general(
        left,
        right,
        (((0,), (0,)), ((), ())),
        precision=lax.Precision.HIGHEST,
        preferred_element_type=jnp.float32,
    )


def gram_blocks(own, partner):
    return (cross_product(own, own), cross_product(own, partner), cross_product(partner, partner))


def pair_update(own, partner, blocks, lower):
    self_gram, cross_gram, other_gram = blocks
    low_low = jnp.where(lower, self_gram, other_gram)
    high_high = jnp.where(lower, other_gram, self_gram)
    low_high = jnp.where(lower, cross_gram, cross_gram.T)
    gram = jnp.concatenate(
        [
            jnp.concatenate([low_low, low_high], axis=1),
            jnp.concatenate([low_high.T, high_high], axis=1),
        ],
        axis=0,
    )
    mixing = pair_transform(gram)
    width = own.shape[1]
    own_own = jnp.where(lower, mixing[:width, :width], mixing[width:, width:])
    other_own = jnp.where(lower, mixing[width:, :width], mixing[:width, width:])
    return jnp.dot(own, own_own, precision=lax.Precision.HIGHEST) + jnp.dot(
        partner, other_own, precision=lax.Precision.HIGHEST
    )


def exchanged_rounds(sketch):
    regrouped = lax.all_to_all(sketch, "row", split_axis=1, concat_axis=0, tiled=True)
    half_rows = regrouped.shape[0]
    depth = lax.axis_size("row").bit_length() - 1
    position = lax.axis_index("row")
    working = lax.all_gather(regrouped, "grp", axis=0, tiled=True).astype(jnp.float32)
    for turn in range(ROUNDS):
        bit = turn % depth
        partner = swapped(working.astype(jnp.bfloat16), "row", bit).astype(working.dtype)
        lower = position >> bit & 1 == 0
        working = pair_update(working, partner, gram_blocks(working, partner), lower)
    return lax.dynamic_slice_in_dim(working, lax.axis_index("grp") * half_rows, half_rows, 0)


def gathers(devices, columns):
    return 2 * KB * devices * columns + 4 * columns * columns <= GATHER_BYTES


def per_device(design, target, coeffs, tau_level, bucket, sign_bit, panel_order):
    sketch = sketch_local(design, target, coeffs, tau_level, bucket, sign_bit, panel_order)
    columns = design.shape[1]
    if gathers(lax.axis_size("row") * lax.axis_size("grp"), columns):
        return gathered_rounds(sketch)
    return exchanged_rounds(sketch)


def solution(mesh):
    placed = (
        P(("parts", "grp", "row"), None),
        P(("parts", "grp", "row")),
        P("parts"),
        P(("parts", "grp", "row")),
        P(("parts", "grp", "row")),
        P(("parts", "grp", "row")),
        P("parts"),
    )
    return jax.shard_map(
        per_device,
        mesh=mesh,
        in_specs=placed,
        out_specs=P(("parts", "grp"), "row"),
        check_vma=False,
    )
```

```python
import functools

import jax
import jax.numpy as jnp
from jax import lax
from jax.experimental import pallas as pl
from jax.experimental.pallas import tpu as pltpu
from jax.sharding import PartitionSpec as P

PANEL = 128
KB = 64
ROUNDS = 5
NS_ITERS = 4
GATHER_BYTES = 12 << 20


def swapped(block, axis, bit):
    count = lax.axis_size(axis)
    route = []
    for low in range(count):
        high = low | 1 << bit
        if high != low and high < count:
            route += [(low, high), (high, low)]
    return lax.ppermute(block, axis, route)


def sketch_kernel(*refs):
    sources, out_ref, places, arrived = refs[:7], refs[7], refs[8:15], refs[15]
    design_ref, target_ref, coeffs_ref, level_ref, bucket_ref, sign_ref, order_ref = places
    copies = [
        pltpu.make_async_copy(source, here, arrived.at[i])
        for i, (source, here) in enumerate(zip(sources, places))
    ]
    for copy in copies:
        copy.start()
    for copy in copies:
        copy.wait()
    rows = design_ref.shape[0]
    design = design_ref[...]
    fitted = lax.dot_general(
        coeffs_ref[...].reshape(1, -1),
        design,
        (((1,), (1,)), ((), ())),
        preferred_element_type=jnp.float32,
    )
    residual = target_ref[...].reshape(1, rows) - fitted
    blocks = level_ref.shape[0]
    lane = lax.broadcasted_iota(jnp.int32, (1, rows), 1)
    level = jnp.full((1, rows), level_ref[0], jnp.int32)
    for block in range(1, blocks):
        level = jnp.where(lane >= block * (rows // blocks), level_ref[block], level)
    quantile = 0.1 + 0.25 * level.astype(jnp.float32)
    upper = jax.nn.sigmoid(residual / 0.2)
    weight = (quantile * upper + (1.0 - quantile) * (1.0 - upper)) / jnp.sqrt(
        residual * residual + 0.25
    )
    sign = 2.0 * sign_ref[...].reshape(1, rows).astype(jnp.float32) - 1.0
    signed = (sign * jnp.sqrt(weight)).astype(jnp.bfloat16).astype(jnp.float32)
    slots = lax.broadcasted_iota(jnp.int32, (KB, rows), 0)
    embed = jnp.where(slots == bucket_ref[...].reshape(1, rows), signed, 0.0).astype(jnp.bfloat16)
    for j in range(order_ref.shape[0]):
        column = pl.multiple_of(order_ref[j] * PANEL, PANEL)
        out_ref[:, j * PANEL : (j + 1) * PANEL] = jnp.dot(
            embed, design_ref[:, pl.ds(column, PANEL)], preferred_element_type=jnp.float32
        ).astype(jnp.bfloat16)


def sketch_local(design, target, coeffs, tau_level, bucket, sign_bit, panel_order):
    rows, columns = design.shape
    anywhere = pl.BlockSpec(memory_space=pltpu.HBM)
    return pl.pallas_call(
        sketch_kernel,
        out_shape=jax.ShapeDtypeStruct((KB, columns), jnp.bfloat16),
        in_specs=[anywhere] * 7,
        out_specs=pl.BlockSpec(memory_space=pltpu.VMEM),
        scratch_shapes=[
            pltpu.VMEM((rows, columns), jnp.bfloat16),
            pltpu.VMEM((rows,), jnp.float32),
            pltpu.VMEM((columns,), jnp.bfloat16),
            pltpu.SMEM(tau_level.shape, jnp.int32),
            pltpu.VMEM((rows,), jnp.int32),
            pltpu.VMEM((rows,), jnp.int32),
            pltpu.SMEM(panel_order.shape, jnp.int32),
            pltpu.SemaphoreType.DMA((7,)),
        ],
        compiler_params=pltpu.CompilerParams(vmem_limit_bytes=67043328),
    )(design, target, coeffs, tau_level, bucket, sign_bit, panel_order)


def half(block):
    return block.astype(jnp.bfloat16)


def mul(left, right):
    return jnp.dot(left, right, preferred_element_type=jnp.float32)


def diagonal_mask(width):
    rows = lax.broadcasted_iota(jnp.int32, (width, width), 0)
    columns = lax.broadcasted_iota(jnp.int32, (width, width), 1)
    return rows == columns


def root_factors(grams, offs):
    w, t, v, z = [], [], [], []
    for gram, off in zip(grams, offs):
        bound = jnp.max(jnp.sum(jnp.abs(gram), axis=0, keepdims=True), axis=1, keepdims=True)
        w.append(1.0 / bound)
        t.append(1.5 - 0.5 * w[-1])
        v.append((-0.5 * w[-1] / t[-1]) * off)
        z.append(lax.rsqrt(bound))
    s = [jnp.ones_like(a) for a in w]
    thin = [half(a) for a in v]
    doubles = []
    for step in range(NS_ITERS):
        z = [a * b for a, b in zip(z, t)]
        after = [1.5 - 0.5 * a * a * b for a, b in zip(t, w)]
        gain = [a * a * a / b for a, b in zip(t, after)]
        linear = [1.0 - b / a for a, b in zip(t, w)]
        square = [2.0 - 0.5 * b / a for a, b in zip(t, w)]
        if step % 2 == 0:
            squared = [mul(a, a) for a in thin]
        if step % 2 == 0 and step + 2 >= NS_ITERS and step + 1 < NS_ITERS:
            parts = []
            for g, a, b, c, x, q in zip(gain, linear, square, s, v, squared):
                outer = half(q)
                inner = half((g * (1.0 + b) * c * c * c) * x + (g * c * c * c * c) * q)
                parts.append(
                    ((1.0 + g * a) * c) * x + (g * (a + b) * c * c) * q + mul(inner, outer)
                )
            doubles.append(parts)
        elif step % 2 == 0 and step + 1 == NS_ITERS:
            doubles.append([c * x for c, x in zip(s, v)])
        if step + 2 < NS_ITERS or step % 2 == 1 and step + 1 < NS_ITERS:
            if step % 2 == 1:
                squared = [mul(a, a) for a in thin]
            inner = [half((b / c) * x + q) for b, c, x, q in zip(square, s, v, squared)]
            before, flat, size = v, thin, s
            v = [
                (a / (c * c)) * x + mul(r, y)
                for a, c, x, r, y in zip(linear, s, v, inner, thin)
            ]
            thin = [half(a) for a in v]
            s = [g * c * c * c for g, c in zip(gain, s)]
            if step % 2 == 0:
                doubles.append(
                    [
                        c * x + d * (y + c * mul(a, b))
                        for c, x, d, y, a, b in zip(size, before, s, v, thin, flat)
                    ]
                )
        w = [a * a * b for a, b in zip(t, w)]
        t = after
    e = doubles[0]
    thin = [half(a) for a in e]
    for parts in doubles[1:]:
        e = [a + b + mul(half(b), c) for a, b, c in zip(e, parts, thin)]
        thin = [half(a) for a in e]
    return list(zip(z, e, thin))


def diagonal_of(block, axis):
    return jnp.sum(jnp.where(diagonal_mask(block.shape[0]), block, 0.0), axis=axis, keepdims=True)


def ring_place(index, count):
    return jnp.where(index % 2 == 0, index // 2, count - 1 - index // 2)


def ring_index(place, count):
    return jnp.where(place < count // 2, 2 * place, 2 * (count - 1 - place) + 1)


def ring_origins(count):
    here = ring_place(lax.axis_index("row"), count)
    turns = [0] + [step for k in range(1, count // 2) for step in (-k, k)] + [count // 2]
    return [ring_index((here + turn + count) % count, count) for turn in turns]


def gather_panels(count, chunks, ordered_ref, turned_ref):
    position = lax.axis_index("row")
    start = 0
    for chunk in chunks:
        rows = chunk.shape[0]
        for j in range(count):
            column = pl.multiple_of(jnp.bitwise_xor(position, j) * PANEL, PANEL)
            ordered_ref[start : start + rows, j * PANEL : (j + 1) * PANEL] = chunk[
                :, pl.ds(column, PANEL)
            ]
        start += rows
    for p in range(0, count, 2):
        span = slice(p * PANEL, (p + 2) * PANEL)
        turned_ref[span] = ordered_ref[:, span].T


def tall_gram(turned_ref, ordered_ref, b):
    return mul(turned_ref[: (b + 2) * PANEL], ordered_ref[:, b * PANEL : (b + 2) * PANEL])


def gram_kernel(count, pieces, *refs):
    chunks, before, after = refs[:pieces], refs[pieces : -2 - count // 2], refs[-2 - count // 2 :]
    ordered_ref, *tall_refs, turned_ref = after
    gather_panels(count, chunks, ordered_ref, turned_ref)
    for k, tall_ref in enumerate(tall_refs):
        tall = tall_gram(turned_ref, ordered_ref, 2 * k)
        tall_ref[...] = tall + before[k][...] if before else tall


def rounds_kernel(count, pieces, *refs):
    chunks, refs = refs[:pieces], refs[pieces:]
    *earlier, out_ref, ordered_ref, turned_ref = refs
    early_refs, tall_refs = earlier[: -(count // 2)], earlier[-(count // 2) :]
    width = PANEL
    depth = count.bit_length() - 1
    gather_panels(count, chunks, ordered_ref, turned_ref)

    live = [None] * (ROUNDS + 1)
    live[ROUNDS] = [0]
    for turn in reversed(range(ROUNDS)):
        bit = 1 << turn % depth
        live[turn] = sorted({a for p in live[turn + 1] for a in (p, p ^ bit)})

    row_scale, column_scale, total, grams = {}, {}, {}, {}
    for b in range(0, count, 2):
        tall = tall_refs[b // 2][...] + tall_gram(turned_ref, ordered_ref, b)
        for i in range(b + 2):
            for j in range(2):
                if i <= b + j:
                    grams[i, b + j] = tall[
                        i * width : (i + 1) * width, j * width : (j + 1) * width
                    ]
    for p in range(count):
        total[p] = diagonal_of(grams[p, p], 0)
        row_scale[p] = lax.rsqrt(total[p])
        column_scale[p] = lax.rsqrt(diagonal_of(grams[p, p], 1))
    first_scale = dict(column_scale)
    blocks = {
        (a, b): column_scale[a] * gram * row_scale[b] for (a, b), gram in grams.items()
    }
    eye = diagonal_mask(width)

    def joined_from(blocks):
        def joined(left, right, corner=lambda block: block):
            def block_of(a, b):
                if a == b:
                    return corner(blocks[a, a])
                return blocks[a, b] if (a, b) in blocks else blocks[b, a].T

            return jnp.concatenate(
                [jnp.concatenate([block_of(a, b) for b in right], axis=1) for a in left], axis=0
            )

        return joined

    history = []
    finish = None
    for turn in range(ROUNDS):
        bit = 1 << turn % depth
        pairs = [(p, p | bit) for p in live[turn] if not p & bit]
        joined = joined_from(blocks)
        whole = [joined(pair, pair) for pair in pairs]
        offs = [
            joined(pair, pair, lambda block: jnp.where(eye, 0.0, block)) for pair in pairs
        ]
        factors = root_factors(whole, offs)
        if finish is not None:
            finish()
        keep = live[turn + 1]
        scales = {}
        if turn + 1 < ROUNDS:
            kept = [[i for i in range(2) if pair[i] in keep] for pair in pairs]
            spans = [
                slice(k[0] * width, (k[-1] + 1) * width) for k in kept
            ]
            fresh, row_scale, column_scale = {}, {}, {}
            for i, pair in enumerate(pairs):
                z, e, thin = factors[i]
                span = spans[i]
                part = offs[i][span] + e[span] + mul(thin[span], half(offs[i]))
                value = part[:, span] + e[span, span] + mul(half(part), thin[:, span])
                for k, at in enumerate(kept[i]):
                    cut = slice(k * width, (k + 1) * width)
                    block = value[cut, cut] + jnp.where(eye, 1.0, 0.0)
                    along = diagonal_of(block, 0)
                    row_scale[pair[at]] = lax.rsqrt(along)
                    column_scale[pair[at]] = lax.rsqrt(diagonal_of(block, 1))
                    total[pair[at]] = total[pair[at]] * along * z * z
                    fresh[pair[at], pair[at]] = block
                    for j, to in list(enumerate(kept[i]))[k + 1 :]:
                        fresh[pair[at], pair[to]] = value[cut, j * width : (j + 1) * width]
            following = 1 << (turn + 1) % depth
            soon, later = [], []
            for j in range(1, len(pairs)):
                near = [
                    i
                    for i in range(j)
                    if any(a ^ following in pairs[j] for a in pairs[i])
                ]
                soon.append((j, near))
                later.append((j, [i for i in range(j) if i not in near]))

            def cross(work, joined, pairs, factors, kept, spans, fresh):
                for j, members in work:
                    if not members:
                        continue
                    tops = []
                    for i in members:
                        source = joined(pairs[i], pairs[j])
                        tops.append(
                            source[spans[i]] + mul(factors[i][2][spans[i]], half(source))
                        )
                    tall = jnp.concatenate(tops, axis=0)
                    tall = tall[:, spans[j]] + mul(half(tall), factors[j][2][:, spans[j]])
                    start = 0
                    for i in members:
                        for at in kept[i]:
                            for k, to in enumerate(kept[j]):
                                fresh[pairs[i][at], pairs[j][to]] = tall[
                                    start : start + width, k * width : (k + 1) * width
                                ]
                            start += width

            def scaled(fresh, column_scale, row_scale):
                return {
                    (a, b): column_scale[a] * value * row_scale[b]
                    for (a, b), value in fresh.items()
                }

            known = (joined_from(blocks), pairs, factors, kept, spans)
            cross(soon, *known, fresh)
            blocks = scaled(fresh, column_scale, row_scale)

            def finish(blocks=blocks, later=later, known=known, down=column_scale, along=row_scale):
                rest = {}
                cross(later, *known, rest)
                blocks.update(scaled(rest, down, along))

            scales = column_scale
        history.append((pairs, factors, scales))

    pairs, factors, _ = history[-1]
    z, e, _ = factors[0]
    combined = {
        pairs[0][0]: jnp.where(eye, 1.0, 0.0) + e[:width, :width],
        pairs[0][1]: e[width:, :width],
    }
    final = z * jnp.sqrt(total[0])
    for pairs, factors, scales in reversed(history[:-1]):
        following = {}
        for pair, (z, e, thin) in zip(pairs, factors):
            parts = [i for i in range(2) if pair[i] in combined]
            tops = {i: scales[pair[i]] * combined[pair[i]] for i in parts}
            stacked = half(jnp.concatenate([tops[i] for i in parts], axis=0))
            moved = mul(thin[:, parts[0] * width : (parts[-1] + 1) * width], stacked)
            for i in range(2):
                rows = moved[i * width : (i + 1) * width]
                following[pair[i]] = tops[i] + rows if i in tops else rows
        combined = following
    weights = jnp.concatenate(
        [first_scale[p] * combined[p] for p in range(count)], axis=0
    ) * final
    high = half(weights)
    low = half(weights - high.astype(jnp.float32))
    own = out_ref.shape[0]
    chunk = own // count
    both = jnp.concatenate([high, low], axis=1)
    origins = ring_origins(count)
    first = 0
    for source_ref in (*early_refs, ordered_ref):
        rows = source_ref.shape[0] // 2
        product = mul(source_ref[:rows], both)
        result = product[:, :width] + product[:, width:]
        for k in range(rows // chunk):
            start = pl.multiple_of(origins[first + k] * chunk, chunk)
            out_ref[pl.ds(start, chunk), :] = result[k * chunk : (k + 1) * chunk]
        first += rows // chunk


def add_gram(blocks, talls):
    rows, total = sum(block.shape[0] for block in blocks), blocks[0].shape[1]
    count = total // PANEL
    inside = pl.BlockSpec(memory_space=pltpu.VMEM)
    ordered, *talls = pl.pallas_call(
        functools.partial(gram_kernel, count, len(blocks)),
        out_shape=[jax.ShapeDtypeStruct((rows, total), jnp.bfloat16)]
        + [
            jax.ShapeDtypeStruct(((b + 2) * PANEL, 2 * PANEL), jnp.float32)
            for b in range(0, count, 2)
        ],
        in_specs=[inside] * (len(blocks) + len(talls)),
        out_specs=[inside] * (1 + count // 2),
        input_output_aliases={len(blocks) + k: 1 + k for k in range(len(talls))},
        scratch_shapes=[pltpu.VMEM((total, rows), jnp.bfloat16)],
        compiler_params=pltpu.CompilerParams(vmem_limit_bytes=16 << 20),
        cost_estimate=pl.CostEstimate(
            flops=2 * rows * total * total,
            bytes_accessed=4 * rows * total + 3 * total * total,
            transcendentals=0,
        ),
    )(*blocks, *talls)
    return ordered, talls


def all_rounds(mine, other):
    total = mine[0].shape[1]
    count = total // PANEL
    inside = pl.BlockSpec(memory_space=pltpu.VMEM)
    talls, early = [], []
    near = len(mine) // 3
    for span in (slice(0, near), slice(near, -2)):
        ordered, talls = add_gram(mine[span] + other[span], talls)
        early.append(ordered)
    last = mine[-2:] + other[-2:]
    last_rows = sum(block.shape[0] for block in last)
    own_rows = sum(block.shape[0] for block in mine)
    return pl.pallas_call(
        functools.partial(rounds_kernel, count, len(last)),
        out_shape=jax.ShapeDtypeStruct((own_rows, PANEL), jnp.float32),
        in_specs=[inside] * (len(last) + len(early) + len(talls)),
        out_specs=inside,
        scratch_shapes=[
            pltpu.VMEM((last_rows, total), jnp.bfloat16),
            pltpu.VMEM((total, last_rows), jnp.bfloat16),
        ],
        compiler_params=pltpu.CompilerParams(vmem_limit_bytes=32 << 20),
    )(*last, *early, *talls)


def ring_gather(block, axis):
    count = lax.axis_size(axis)
    ring = list(range(0, count, 2)) + list(range(1, count, 2))[::-1]
    onward = [(ring[i], ring[(i + 1) % count]) for i in range(count)]
    back = [(b, a) for a, b in onward]
    blocks = [block]
    ahead = behind = block
    for _ in range(1, count // 2):
        ahead = lax.ppermute(ahead, axis, onward)
        behind = lax.ppermute(behind, axis, back)
        blocks += [ahead, behind]
    middle = block.shape[0] // 2
    blocks.append(lax.ppermute(ahead[:middle], axis, onward))
    blocks.append(lax.ppermute(behind[middle:], axis, back))
    return blocks


def gathered_rounds(sketch):
    mine = ring_gather(sketch, "row")
    other = []
    for block in mine:
        other.append(lax.ppermute(block, "grp", [(0, 1), (1, 0)]))
    return all_rounds(mine, other)


def pair_transform(gram):
    squares = jnp.sum(jnp.where(diagonal_mask(gram.shape[0]), gram, 0.0), axis=0)
    inv_root = lax.rsqrt(squares)
    normed = gram * inv_root[:, None] * inv_root[None, :]
    bound = jnp.max(jnp.sum(jnp.abs(normed), axis=1))
    identity = jnp.eye(gram.shape[0], dtype=jnp.float32)
    current = normed / bound
    inverse = identity
    for _ in range(NS_ITERS):
        middle = 1.5 * identity - 0.5 * jnp.dot(inverse, current, precision=lax.Precision.HIGHEST)
        current_next = jnp.dot(current, middle, precision=lax.Precision.HIGHEST)
        inverse = jnp.dot(middle, inverse, precision=lax.Precision.HIGHEST)
        current = current_next
    return inv_root[:, None] * inverse * (jnp.sqrt(squares) / jnp.sqrt(bound))[None, :]


def cross_product(left, right):
    return lax.dot_general(
        left,
        right,
        (((0,), (0,)), ((), ())),
        precision=lax.Precision.HIGHEST,
        preferred_element_type=jnp.float32,
    )


def gram_blocks(own, partner):
    return (cross_product(own, own), cross_product(own, partner), cross_product(partner, partner))


def pair_update(own, partner, blocks, lower):
    self_gram, cross_gram, other_gram = blocks
    low_low = jnp.where(lower, self_gram, other_gram)
    high_high = jnp.where(lower, other_gram, self_gram)
    low_high = jnp.where(lower, cross_gram, cross_gram.T)
    gram = jnp.concatenate(
        [
            jnp.concatenate([low_low, low_high], axis=1),
            jnp.concatenate([low_high.T, high_high], axis=1),
        ],
        axis=0,
    )
    mixing = pair_transform(gram)
    width = own.shape[1]
    own_own = jnp.where(lower, mixing[:width, :width], mixing[width:, width:])
    other_own = jnp.where(lower, mixing[width:, :width], mixing[:width, width:])
    return jnp.dot(own, own_own, precision=lax.Precision.HIGHEST) + jnp.dot(
        partner, other_own, precision=lax.Precision.HIGHEST
    )


def exchanged_rounds(sketch):
    regrouped = lax.all_to_all(sketch, "row", split_axis=1, concat_axis=0, tiled=True)
    half_rows = regrouped.shape[0]
    depth = lax.axis_size("row").bit_length() - 1
    position = lax.axis_index("row")
    working = lax.all_gather(regrouped, "grp", axis=0, tiled=True).astype(jnp.float32)
    for turn in range(ROUNDS):
        bit = turn % depth
        partner = swapped(working.astype(jnp.bfloat16), "row", bit).astype(working.dtype)
        lower = position >> bit & 1 == 0
        working = pair_update(working, partner, gram_blocks(working, partner), lower)
    return lax.dynamic_slice_in_dim(working, lax.axis_index("grp") * half_rows, half_rows, 0)


def gathers(devices, columns):
    return 2 * KB * devices * columns + 4 * columns * columns <= GATHER_BYTES


def per_device(design, target, coeffs, tau_level, bucket, sign_bit, panel_order):
    sketch = sketch_local(design, target, coeffs, tau_level, bucket, sign_bit, panel_order)
    columns = design.shape[1]
    if gathers(lax.axis_size("row") * lax.axis_size("grp"), columns):
        return gathered_rounds(sketch)
    return exchanged_rounds(sketch)


def solution(mesh):
    placed = (
        P(("parts", "grp", "row"), None),
        P(("parts", "grp", "row")),
        P("parts"),
        P(("parts", "grp", "row")),
        P(("parts", "grp", "row")),
        P(("parts", "grp", "row")),
        P("parts"),
    )
    return jax.shard_map(
        per_device,
        mesh=mesh,
        in_specs=placed,
        out_specs=P(("parts", "grp"), "row"),
        check_vma=False,
    )
```

```python
import functools

import jax
import jax.numpy as jnp
from jax import lax
from jax.experimental import pallas as pl
from jax.experimental.pallas import tpu as pltpu
from jax.sharding import PartitionSpec as P

PANEL = 128
KB = 64
ROUNDS = 5
NS_ITERS = 4
GATHER_BYTES = 12 << 20


def swapped(block, axis, bit):
    count = lax.axis_size(axis)
    route = []
    for low in range(count):
        high = low | 1 << bit
        if high != low and high < count:
            route += [(low, high), (high, low)]
    return lax.ppermute(block, axis, route)


def sketch_kernel(*refs):
    sources, out_ref, places, arrived = refs[:7], refs[7], refs[8:15], refs[15]
    design_ref, target_ref, coeffs_ref, level_ref, bucket_ref, sign_ref, order_ref = places
    copies = [
        pltpu.make_async_copy(source, here, arrived.at[i])
        for i, (source, here) in enumerate(zip(sources, places))
    ]
    for copy in copies:
        copy.start()
    for copy in copies:
        copy.wait()
    rows = design_ref.shape[0]
    design = design_ref[...]
    fitted = lax.dot_general(
        coeffs_ref[...].reshape(1, -1),
        design,
        (((1,), (1,)), ((), ())),
        preferred_element_type=jnp.float32,
    )
    residual = target_ref[...].reshape(1, rows) - fitted
    blocks = level_ref.shape[0]
    lane = lax.broadcasted_iota(jnp.int32, (1, rows), 1)
    level = jnp.full((1, rows), level_ref[0], jnp.int32)
    for block in range(1, blocks):
        level = jnp.where(lane >= block * (rows // blocks), level_ref[block], level)
    quantile = 0.1 + 0.25 * level.astype(jnp.float32)
    upper = jax.nn.sigmoid(residual / 0.2)
    weight = (quantile * upper + (1.0 - quantile) * (1.0 - upper)) / jnp.sqrt(
        residual * residual + 0.25
    )
    sign = 2.0 * sign_ref[...].reshape(1, rows).astype(jnp.float32) - 1.0
    signed = (sign * jnp.sqrt(weight)).astype(jnp.bfloat16).astype(jnp.float32)
    slots = lax.broadcasted_iota(jnp.int32, (KB, rows), 0)
    embed = jnp.where(slots == bucket_ref[...].reshape(1, rows), signed, 0.0).astype(jnp.bfloat16)
    for j in range(order_ref.shape[0]):
        column = pl.multiple_of(order_ref[j] * PANEL, PANEL)
        out_ref[:, j * PANEL : (j + 1) * PANEL] = jnp.dot(
            embed, design_ref[:, pl.ds(column, PANEL)], preferred_element_type=jnp.float32
        ).astype(jnp.bfloat16)


def sketch_local(design, target, coeffs, tau_level, bucket, sign_bit, panel_order):
    rows, columns = design.shape
    anywhere = pl.BlockSpec(memory_space=pltpu.HBM)
    return pl.pallas_call(
        sketch_kernel,
        out_shape=jax.ShapeDtypeStruct((KB, columns), jnp.bfloat16),
        in_specs=[anywhere] * 7,
        out_specs=pl.BlockSpec(memory_space=pltpu.VMEM),
        scratch_shapes=[
            pltpu.VMEM((rows, columns), jnp.bfloat16),
            pltpu.VMEM((rows,), jnp.float32),
            pltpu.VMEM((columns,), jnp.bfloat16),
            pltpu.SMEM(tau_level.shape, jnp.int32),
            pltpu.VMEM((rows,), jnp.int32),
            pltpu.VMEM((rows,), jnp.int32),
            pltpu.SMEM(panel_order.shape, jnp.int32),
            pltpu.SemaphoreType.DMA((7,)),
        ],
        compiler_params=pltpu.CompilerParams(vmem_limit_bytes=67043328),
    )(design, target, coeffs, tau_level, bucket, sign_bit, panel_order)


def half(block):
    return block.astype(jnp.bfloat16)


def mul(left, right):
    return jnp.dot(left, right, preferred_element_type=jnp.float32)


def diagonal_mask(width):
    rows = lax.broadcasted_iota(jnp.int32, (width, width), 0)
    columns = lax.broadcasted_iota(jnp.int32, (width, width), 1)
    return rows == columns


def root_factors(grams, offs):
    thin = [half(a) for a in offs]
    squared = [mul(a, a) for a in thin]
    w, t, s, z = [], [], [], []
    for gram in grams:
        bound = jnp.max(jnp.sum(jnp.abs(gram), axis=0, keepdims=True), axis=1, keepdims=True)
        w.append(1.0 / bound)
        t.append(1.5 - 0.5 * w[-1])
        s.append(-0.5 * w[-1] / t[-1])
        z.append(lax.rsqrt(bound))
    v = offs
    doubles = []
    for step in range(NS_ITERS):
        z = [a * b for a, b in zip(z, t)]
        after = [1.5 - 0.5 * a * a * b for a, b in zip(t, w)]
        gain = [a * a * a / b for a, b in zip(t, after)]
        linear = [1.0 - b / a for a, b in zip(t, w)]
        square = [2.0 - 0.5 * b / a for a, b in zip(t, w)]
        if step:
            squared = [mul(a, a) for a in thin]
        if step % 2 == 0 and step + 2 >= NS_ITERS and step + 1 < NS_ITERS:
            parts = []
            for g, a, b, c, x, q in zip(gain, linear, square, s, v, squared):
                outer = half(q)
                inner = half((g * (1.0 + b) * c * c * c) * x + (g * c * c * c * c) * q)
                parts.append(
                    ((1.0 + g * a) * c) * x + (g * (a + b) * c * c) * q + mul(inner, outer)
                )
            doubles.append(parts)
        elif step % 2 == 0 and step + 1 == NS_ITERS:
            doubles.append([c * x for c, x in zip(s, v)])
        if step + 2 < NS_ITERS or step % 2 == 1 and step + 1 < NS_ITERS:
            before, flat, size = v, thin, s
            if step:
                s = [g * c * c * c for g, c in zip(gain, s)]
                share = [jnp.ones_like(a) for a in s]
            else:
                s = [jnp.ones_like(a) for a in s]
                share = [g * c * c * c for g, c in zip(gain, size)]
            inner = [
                half((d * b / c) * x + (d * q if step == 0 else q))
                for d, b, c, x, q in zip(share, square, size, v, squared)
            ]
            v = [
                (d * a / (c * c)) * x + mul(r, y)
                for d, a, c, x, r, y in zip(share, linear, size, v, inner, thin)
            ]
            thin = [half(a) for a in v]
            if step % 2 == 0:
                doubles.append(
                    [
                        c * x + d * (y + c * mul(a, b))
                        for c, x, d, y, a, b in zip(size, before, s, v, thin, flat)
                    ]
                )
        w = [a * a * b for a, b in zip(t, w)]
        t = after
    e = doubles[0]
    thin = [half(a) for a in e]
    for parts in doubles[1:]:
        e = [a + b + mul(half(b), c) for a, b, c in zip(e, parts, thin)]
        thin = [half(a) for a in e]
    return list(zip(z, e, thin))


def diagonal_of(block):
    return jnp.sum(jnp.where(diagonal_mask(block.shape[0]), block, 0.0), axis=0, keepdims=True)


def turned_rows(row):
    return jnp.broadcast_to(row, (row.shape[1], row.shape[1])).T


def ring_place(index, count):
    return jnp.where(index % 2 == 0, index // 2, count - 1 - index // 2)


def ring_index(place, count):
    return jnp.where(place < count // 2, 2 * place, 2 * (count - 1 - place) + 1)


def ring_origins(count):
    here = ring_place(lax.axis_index("row"), count)
    turns = [0] + [step for k in range(1, count // 2) for step in (-k, k)] + [count // 2]
    return [ring_index((here + turn + count) % count, count) for turn in turns]


def gather_panels(count, chunks, ordered_ref, turned_ref):
    position = lax.axis_index("row")
    start = 0
    for chunk in chunks:
        rows = chunk.shape[0]
        for j in range(count):
            column = pl.multiple_of(jnp.bitwise_xor(position, j) * PANEL, PANEL)
            ordered_ref[start : start + rows, j * PANEL : (j + 1) * PANEL] = chunk[
                :, pl.ds(column, PANEL)
            ]
        start += rows
    for p in range(0, count, 2):
        span = slice(p * PANEL, (p + 2) * PANEL)
        turned_ref[span] = ordered_ref[:, span].T


def tall_gram(turned_ref, ordered_ref, b):
    return mul(turned_ref[: (b + 2) * PANEL], ordered_ref[:, b * PANEL : (b + 2) * PANEL])


def gram_kernel(count, pieces, *refs):
    chunks, before, after = refs[:pieces], refs[pieces : -2 - count // 2], refs[-2 - count // 2 :]
    ordered_ref, *tall_refs, turned_ref = after
    gather_panels(count, chunks, ordered_ref, turned_ref)
    for k, tall_ref in enumerate(tall_refs):
        tall = tall_gram(turned_ref, ordered_ref, 2 * k)
        tall_ref[...] = tall + before[k][...] if before else tall


def rounds_kernel(count, pieces, *refs):
    chunks, refs = refs[:pieces], refs[pieces:]
    *earlier, out_ref, ordered_ref, turned_ref = refs
    early_refs, tall_refs = earlier[: -(count // 2)], earlier[-(count // 2) :]
    width = PANEL
    depth = count.bit_length() - 1
    gather_panels(count, chunks, ordered_ref, turned_ref)

    live = [None] * (ROUNDS + 1)
    live[ROUNDS] = [0]
    for turn in reversed(range(ROUNDS)):
        bit = 1 << turn % depth
        live[turn] = sorted({a for p in live[turn + 1] for a in (p, p ^ bit)})

    row_scale, column_scale, total, grams = {}, {}, {}, {}
    for b in range(0, count, 2):
        tall = tall_refs[b // 2][...] + tall_gram(turned_ref, ordered_ref, b)
        for i in range(b + 2):
            for j in range(2):
                if i <= b + j:
                    grams[i, b + j] = tall[
                        i * width : (i + 1) * width, j * width : (j + 1) * width
                    ]
    for p in range(count):
        total[p] = diagonal_of(grams[p, p])
        row_scale[p] = lax.rsqrt(total[p])
        column_scale[p] = turned_rows(row_scale[p])
    first_scale = dict(column_scale)
    blocks = {
        (a, b): column_scale[a] * gram * row_scale[b] for (a, b), gram in grams.items()
    }
    eye = diagonal_mask(width)

    def joined_from(blocks):
        def joined(left, right, corner=lambda block: block):
            def block_of(a, b):
                if a == b:
                    return corner(blocks[a, a])
                return blocks[a, b] if (a, b) in blocks else blocks[b, a].T

            return jnp.concatenate(
                [jnp.concatenate([block_of(a, b) for b in right], axis=1) for a in left], axis=0
            )

        return joined

    history = []
    finish = None
    for turn in range(ROUNDS):
        bit = 1 << turn % depth
        pairs = [(p, p | bit) for p in live[turn] if not p & bit]
        joined = joined_from(blocks)
        whole = [joined(pair, pair) for pair in pairs]
        offs = [
            joined(pair, pair, lambda block: jnp.where(eye, 0.0, block)) for pair in pairs
        ]
        factors = root_factors(whole, offs)
        if finish is not None:
            finish()
        keep = live[turn + 1]
        scales = {}
        if turn + 1 < ROUNDS:
            kept = [[i for i in range(2) if pair[i] in keep] for pair in pairs]
            spans = [
                slice(k[0] * width, (k[-1] + 1) * width) for k in kept
            ]
            fresh, row_scale, column_scale = {}, {}, {}
            for i, pair in enumerate(pairs):
                z, e, thin = factors[i]
                span = spans[i]
                part = offs[i][span] + e[span] + mul(thin[span], half(offs[i]))
                value = part[:, span] + e[span, span] + mul(half(part), thin[:, span])
                for k, at in enumerate(kept[i]):
                    cut = slice(k * width, (k + 1) * width)
                    block = value[cut, cut] + jnp.where(eye, 1.0, 0.0)
                    along = diagonal_of(block)
                    row_scale[pair[at]] = lax.rsqrt(along)
                    column_scale[pair[at]] = turned_rows(row_scale[pair[at]])
                    total[pair[at]] = total[pair[at]] * along * z * z
                    fresh[pair[at], pair[at]] = block
                    for j, to in list(enumerate(kept[i]))[k + 1 :]:
                        fresh[pair[at], pair[to]] = value[cut, j * width : (j + 1) * width]
            following = 1 << (turn + 1) % depth
            soon, later = [], []
            for j in range(1, len(pairs)):
                near = [
                    i
                    for i in range(j)
                    if any(a ^ following in pairs[j] for a in pairs[i])
                ]
                soon.append((j, near))
                later.append((j, [i for i in range(j) if i not in near]))

            def cross(work, joined, pairs, factors, kept, spans, fresh):
                for j, members in work:
                    if not members:
                        continue
                    tops = []
                    for i in members:
                        source = joined(pairs[i], pairs[j])
                        tops.append(
                            source[spans[i]] + mul(factors[i][2][spans[i]], half(source))
                        )
                    tall = jnp.concatenate(tops, axis=0)
                    tall = tall[:, spans[j]] + mul(half(tall), factors[j][2][:, spans[j]])
                    start = 0
                    for i in members:
                        for at in kept[i]:
                            for k, to in enumerate(kept[j]):
                                fresh[pairs[i][at], pairs[j][to]] = tall[
                                    start : start + width, k * width : (k + 1) * width
                                ]
                            start += width

            def scaled(fresh, column_scale, row_scale):
                return {
                    (a, b): column_scale[a] * value * row_scale[b]
                    for (a, b), value in fresh.items()
                }

            known = (joined_from(blocks), pairs, factors, kept, spans)
            cross(soon, *known, fresh)
            blocks = scaled(fresh, column_scale, row_scale)

            def finish(blocks=blocks, later=later, known=known, down=column_scale, along=row_scale):
                rest = {}
                cross(later, *known, rest)
                blocks.update(scaled(rest, down, along))

            scales = column_scale
        history.append((pairs, factors, scales))

    pairs, factors, _ = history[-1]
    z, e, _ = factors[0]
    combined = {
        pairs[0][0]: jnp.where(eye, 1.0, 0.0) + e[:width, :width],
        pairs[0][1]: e[width:, :width],
    }
    final = z * jnp.sqrt(total[0])
    for pairs, factors, scales in reversed(history[:-1]):
        following = {}
        for pair, (z, e, thin) in zip(pairs, factors):
            parts = [i for i in range(2) if pair[i] in combined]
            tops = {i: scales[pair[i]] * combined[pair[i]] for i in parts}
            stacked = half(jnp.concatenate([tops[i] for i in parts], axis=0))
            moved = mul(thin[:, parts[0] * width : (parts[-1] + 1) * width], stacked)
            for i in range(2):
                rows = moved[i * width : (i + 1) * width]
                following[pair[i]] = tops[i] + rows if i in tops else rows
        combined = following
    weights = jnp.concatenate(
        [first_scale[p] * combined[p] for p in range(count)], axis=0
    ) * final
    high = half(weights)
    low = half(weights - high.astype(jnp.float32))
    own = out_ref.shape[0]
    chunk = own // count
    both = jnp.concatenate([high, low], axis=1)
    origins = ring_origins(count)
    first = 0
    for source_ref in (*early_refs, ordered_ref):
        rows = source_ref.shape[0] // 2
        product = mul(source_ref[:rows], both)
        result = product[:, :width] + product[:, width:]
        for k in range(rows // chunk):
            start = pl.multiple_of(origins[first + k] * chunk, chunk)
            out_ref[pl.ds(start, chunk), :] = result[k * chunk : (k + 1) * chunk]
        first += rows // chunk


def add_gram(blocks, talls):
    rows, total = sum(block.shape[0] for block in blocks), blocks[0].shape[1]
    count = total // PANEL
    inside = pl.BlockSpec(memory_space=pltpu.VMEM)
    ordered, *talls = pl.pallas_call(
        functools.partial(gram_kernel, count, len(blocks)),
        out_shape=[jax.ShapeDtypeStruct((rows, total), jnp.bfloat16)]
        + [
            jax.ShapeDtypeStruct(((b + 2) * PANEL, 2 * PANEL), jnp.float32)
            for b in range(0, count, 2)
        ],
        in_specs=[inside] * (len(blocks) + len(talls)),
        out_specs=[inside] * (1 + count // 2),
        input_output_aliases={len(blocks) + k: 1 + k for k in range(len(talls))},
        scratch_shapes=[pltpu.VMEM((total, rows), jnp.bfloat16)],
        compiler_params=pltpu.CompilerParams(vmem_limit_bytes=16 << 20),
        cost_estimate=pl.CostEstimate(
            flops=2 * rows * total * total,
            bytes_accessed=4 * rows * total + 3 * total * total,
            transcendentals=0,
        ),
    )(*blocks, *talls)
    return ordered, talls


def all_rounds(mine, other):
    total = mine[0].shape[1]
    count = total // PANEL
    inside = pl.BlockSpec(memory_space=pltpu.VMEM)
    talls, early = [], []
    near = len(mine) // 3
    for span in (slice(0, near), slice(near, -2)):
        ordered, talls = add_gram(mine[span] + other[span], talls)
        early.append(ordered)
    last = mine[-2:] + other[-2:]
    last_rows = sum(block.shape[0] for block in last)
    own_rows = sum(block.shape[0] for block in mine)
    return pl.pallas_call(
        functools.partial(rounds_kernel, count, len(last)),
        out_shape=jax.ShapeDtypeStruct((own_rows, PANEL), jnp.float32),
        in_specs=[inside] * (len(last) + len(early) + len(talls)),
        out_specs=inside,
        scratch_shapes=[
            pltpu.VMEM((last_rows, total), jnp.bfloat16),
            pltpu.VMEM((total, last_rows), jnp.bfloat16),
        ],
        compiler_params=pltpu.CompilerParams(vmem_limit_bytes=32 << 20),
    )(*last, *early, *talls)


def ring_gather(block, axis):
    count = lax.axis_size(axis)
    ring = list(range(0, count, 2)) + list(range(1, count, 2))[::-1]
    onward = [(ring[i], ring[(i + 1) % count]) for i in range(count)]
    back = [(b, a) for a, b in onward]
    blocks = [block]
    ahead = behind = block
    for _ in range(1, count // 2):
        ahead = lax.ppermute(ahead, axis, onward)
        behind = lax.ppermute(behind, axis, back)
        blocks += [ahead, behind]
    middle = block.shape[0] // 2
    blocks.append(lax.ppermute(ahead[:middle], axis, onward))
    blocks.append(lax.ppermute(behind[middle:], axis, back))
    return blocks


def gathered_rounds(sketch):
    mine = ring_gather(sketch, "row")
    other = []
    for block in mine:
        other.append(lax.ppermute(block, "grp", [(0, 1), (1, 0)]))
    return all_rounds(mine, other)


def pair_transform(gram):
    squares = jnp.sum(jnp.where(diagonal_mask(gram.shape[0]), gram, 0.0), axis=0)
    inv_root = lax.rsqrt(squares)
    normed = gram * inv_root[:, None] * inv_root[None, :]
    bound = jnp.max(jnp.sum(jnp.abs(normed), axis=1))
    identity = jnp.eye(gram.shape[0], dtype=jnp.float32)
    current = normed / bound
    inverse = identity
    for _ in range(NS_ITERS):
        middle = 1.5 * identity - 0.5 * jnp.dot(inverse, current, precision=lax.Precision.HIGHEST)
        current_next = jnp.dot(current, middle, precision=lax.Precision.HIGHEST)
        inverse = jnp.dot(middle, inverse, precision=lax.Precision.HIGHEST)
        current = current_next
    return inv_root[:, None] * inverse * (jnp.sqrt(squares) / jnp.sqrt(bound))[None, :]


def cross_product(left, right):
    return lax.dot_general(
        left,
        right,
        (((0,), (0,)), ((), ())),
        precision=lax.Precision.HIGHEST,
        preferred_element_type=jnp.float32,
    )


def gram_blocks(own, partner):
    return (cross_product(own, own), cross_product(own, partner), cross_product(partner, partner))


def pair_update(own, partner, blocks, lower):
    self_gram, cross_gram, other_gram = blocks
    low_low = jnp.where(lower, self_gram, other_gram)
    high_high = jnp.where(lower, other_gram, self_gram)
    low_high = jnp.where(lower, cross_gram, cross_gram.T)
    gram = jnp.concatenate(
        [
            jnp.concatenate([low_low, low_high], axis=1),
            jnp.concatenate([low_high.T, high_high], axis=1),
        ],
        axis=0,
    )
    mixing = pair_transform(gram)
    width = own.shape[1]
    own_own = jnp.where(lower, mixing[:width, :width], mixing[width:, width:])
    other_own = jnp.where(lower, mixing[width:, :width], mixing[:width, width:])
    return jnp.dot(own, own_own, precision=lax.Precision.HIGHEST) + jnp.dot(
        partner, other_own, precision=lax.Precision.HIGHEST
    )


def exchanged_rounds(sketch):
    regrouped = lax.all_to_all(sketch, "row", split_axis=1, concat_axis=0, tiled=True)
    half_rows = regrouped.shape[0]
    depth = lax.axis_size("row").bit_length() - 1
    position = lax.axis_index("row")
    working = lax.all_gather(regrouped, "grp", axis=0, tiled=True).astype(jnp.float32)
    for turn in range(ROUNDS):
        bit = turn % depth
        partner = swapped(working.astype(jnp.bfloat16), "row", bit).astype(working.dtype)
        lower = position >> bit & 1 == 0
        working = pair_update(working, partner, gram_blocks(working, partner), lower)
    return lax.dynamic_slice_in_dim(working, lax.axis_index("grp") * half_rows, half_rows, 0)


def gathers(devices, columns):
    return 2 * KB * devices * columns + 4 * columns * columns <= GATHER_BYTES


def per_device(design, target, coeffs, tau_level, bucket, sign_bit, panel_order):
    sketch = sketch_local(design, target, coeffs, tau_level, bucket, sign_bit, panel_order)
    columns = design.shape[1]
    if gathers(lax.axis_size("row") * lax.axis_size("grp"), columns):
        return gathered_rounds(sketch)
    return exchanged_rounds(sketch)


def solution(mesh):
    placed = (
        P(("parts", "grp", "row"), None),
        P(("parts", "grp", "row")),
        P("parts"),
        P(("parts", "grp", "row")),
        P(("parts", "grp", "row")),
        P(("parts", "grp", "row")),
        P("parts"),
    )
    return jax.shard_map(
        per_device,
        mesh=mesh,
        in_specs=placed,
        out_specs=P(("parts", "grp"), "row"),
        check_vma=False,
    )
```

```python
import functools

import jax
import jax.numpy as jnp
from jax import lax
from jax.experimental import pallas as pl
from jax.experimental.pallas import tpu as pltpu
from jax.sharding import PartitionSpec as P

PANEL = 128
KB = 64
ROUNDS = 5
NS_ITERS = 4
GATHER_BYTES = 12 << 20


def swapped(block, axis, bit):
    count = lax.axis_size(axis)
    route = []
    for low in range(count):
        high = low | 1 << bit
        if high != low and high < count:
            route += [(low, high), (high, low)]
    return lax.ppermute(block, axis, route)


def sketch_kernel(*refs):
    sources, out_ref, places, arrived = refs[:7], refs[7], refs[8:15], refs[15]
    design_ref, target_ref, coeffs_ref, level_ref, bucket_ref, sign_ref, order_ref = places
    copies = [
        pltpu.make_async_copy(source, here, arrived.at[i])
        for i, (source, here) in enumerate(zip(sources, places))
    ]
    for copy in copies:
        copy.start()
    for copy in copies:
        copy.wait()
    rows = design_ref.shape[0]
    design = design_ref[...]
    fitted = lax.dot_general(
        coeffs_ref[...].reshape(1, -1),
        design,
        (((1,), (1,)), ((), ())),
        preferred_element_type=jnp.float32,
    )
    residual = target_ref[...].reshape(1, rows) - fitted
    blocks = level_ref.shape[0]
    lane = lax.broadcasted_iota(jnp.int32, (1, rows), 1)
    level = jnp.full((1, rows), level_ref[0], jnp.int32)
    for block in range(1, blocks):
        level = jnp.where(lane >= block * (rows // blocks), level_ref[block], level)
    quantile = 0.1 + 0.25 * level.astype(jnp.float32)
    upper = jax.nn.sigmoid(residual / 0.2)
    weight = (quantile * upper + (1.0 - quantile) * (1.0 - upper)) / jnp.sqrt(
        residual * residual + 0.25
    )
    sign = 2.0 * sign_ref[...].reshape(1, rows).astype(jnp.float32) - 1.0
    signed = (sign * jnp.sqrt(weight)).astype(jnp.bfloat16).astype(jnp.float32)
    slots = lax.broadcasted_iota(jnp.int32, (KB, rows), 0)
    embed = jnp.where(slots == bucket_ref[...].reshape(1, rows), signed, 0.0).astype(jnp.bfloat16)
    for j in range(order_ref.shape[0]):
        column = pl.multiple_of(order_ref[j] * PANEL, PANEL)
        out_ref[:, j * PANEL : (j + 1) * PANEL] = jnp.dot(
            embed, design_ref[:, pl.ds(column, PANEL)], preferred_element_type=jnp.float32
        ).astype(jnp.bfloat16)


def sketch_local(design, target, coeffs, tau_level, bucket, sign_bit, panel_order):
    rows, columns = design.shape
    anywhere = pl.BlockSpec(memory_space=pltpu.HBM)
    return pl.pallas_call(
        sketch_kernel,
        out_shape=jax.ShapeDtypeStruct((KB, columns), jnp.bfloat16),
        in_specs=[anywhere] * 7,
        out_specs=pl.BlockSpec(memory_space=pltpu.VMEM),
        scratch_shapes=[
            pltpu.VMEM((rows, columns), jnp.bfloat16),
            pltpu.VMEM((rows,), jnp.float32),
            pltpu.VMEM((columns,), jnp.bfloat16),
            pltpu.SMEM(tau_level.shape, jnp.int32),
            pltpu.VMEM((rows,), jnp.int32),
            pltpu.VMEM((rows,), jnp.int32),
            pltpu.SMEM(panel_order.shape, jnp.int32),
            pltpu.SemaphoreType.DMA((7,)),
        ],
        compiler_params=pltpu.CompilerParams(vmem_limit_bytes=67043328),
    )(design, target, coeffs, tau_level, bucket, sign_bit, panel_order)


def half(block):
    return block.astype(jnp.bfloat16)


def mul(left, right):
    return jnp.dot(left, right, preferred_element_type=jnp.float32)


def diagonal_mask(width):
    rows = lax.broadcasted_iota(jnp.int32, (width, width), 0)
    columns = lax.broadcasted_iota(jnp.int32, (width, width), 1)
    return rows == columns


def root_factors(grams, offs):
    thin = [half(a) for a in offs]
    squared = [mul(a, a) for a in thin]
    w, t, s, z = [], [], [], []
    for gram in grams:
        bound = jnp.max(jnp.sum(jnp.abs(gram), axis=0, keepdims=True), axis=1, keepdims=True)
        w.append(1.0 / bound)
        t.append(1.5 - 0.5 * w[-1])
        s.append(-0.5 * w[-1] / t[-1])
        z.append(lax.rsqrt(bound))
    v = offs
    doubles = []
    for step in range(NS_ITERS):
        z = [a * b for a, b in zip(z, t)]
        after = [1.5 - 0.5 * a * a * b for a, b in zip(t, w)]
        gain = [a * a * a / b for a, b in zip(t, after)]
        linear = [1.0 - b / a for a, b in zip(t, w)]
        square = [2.0 - 0.5 * b / a for a, b in zip(t, w)]
        if step:
            squared = [mul(a, a) for a in thin]
        if step % 2 == 0 and step + 2 >= NS_ITERS and step + 1 < NS_ITERS:
            parts = []
            for g, a, b, c, x, q in zip(gain, linear, square, s, v, squared):
                outer = half(q)
                inner = half((g * (1.0 + b) * c * c * c) * x + (g * c * c * c * c) * q)
                parts.append(
                    ((1.0 + g * a) * c) * x + (g * (a + b) * c * c) * q + mul(inner, outer)
                )
            doubles.append(parts)
        elif step % 2 == 0 and step + 1 == NS_ITERS:
            doubles.append([c * x for c, x in zip(s, v)])
        if step + 2 < NS_ITERS or step % 2 == 1 and step + 1 < NS_ITERS:
            before, flat, size = v, thin, s
            if step:
                s = [g * c * c * c for g, c in zip(gain, s)]
                share = [jnp.ones_like(a) for a in s]
            else:
                s = [jnp.ones_like(a) for a in s]
                share = [g * c * c * c for g, c in zip(gain, size)]
            inner = [
                half((d * b / c) * x + (d * q if step == 0 else q))
                for d, b, c, x, q in zip(share, square, size, v, squared)
            ]
            v = [
                (d * a / (c * c)) * x + mul(r, y)
                for d, a, c, x, r, y in zip(share, linear, size, v, inner, thin)
            ]
            thin = [half(a) for a in v]
            if step % 2 == 0:
                doubles.append(
                    [
                        c * x + d * (y + c * mul(a, b))
                        for c, x, d, y, a, b in zip(size, before, s, v, thin, flat)
                    ]
                )
        w = [a * a * b for a, b in zip(t, w)]
        t = after
    e = doubles[0]
    thin = [half(a) for a in e]
    for parts in doubles[1:]:
        e = [a + b + mul(half(b), c) for a, b, c in zip(e, parts, thin)]
        thin = [half(a) for a in e]
    return list(zip(z, e, thin))


def diagonal_of(block):
    return jnp.sum(jnp.where(diagonal_mask(block.shape[0]), block, 0.0), axis=0, keepdims=True)


def turned_rows(row):
    return jnp.broadcast_to(row, (row.shape[1], row.shape[1])).T


def ring_place(index, count):
    return jnp.where(index % 2 == 0, index // 2, count - 1 - index // 2)


def ring_index(place, count):
    return jnp.where(place < count // 2, 2 * place, 2 * (count - 1 - place) + 1)


def ring_origins(count):
    here = ring_place(lax.axis_index("row"), count)
    turns = [0] + [step for k in range(1, count // 2) for step in (-k, k)] + [count // 2]
    return [ring_index((here + turn + count) % count, count) for turn in turns]


def gather_panels(count, chunks, ordered_ref, turned_ref):
    position = lax.axis_index("row")
    start = 0
    for chunk in chunks:
        rows = chunk.shape[0]
        for j in range(count):
            column = pl.multiple_of(jnp.bitwise_xor(position, j) * PANEL, PANEL)
            ordered_ref[start : start + rows, j * PANEL : (j + 1) * PANEL] = chunk[
                :, pl.ds(column, PANEL)
            ]
        start += rows
    for p in range(0, count, 2):
        span = slice(p * PANEL, (p + 2) * PANEL)
        turned_ref[span] = ordered_ref[:, span].T


def tall_gram(turned_ref, ordered_ref, b):
    return mul(turned_ref[: (b + 2) * PANEL], ordered_ref[:, b * PANEL : (b + 2) * PANEL])


def gram_kernel(count, pieces, *refs):
    chunks, before, after = refs[:pieces], refs[pieces : -2 - count // 2], refs[-2 - count // 2 :]
    ordered_ref, *tall_refs, turned_ref = after
    gather_panels(count, chunks, ordered_ref, turned_ref)
    for k, tall_ref in enumerate(tall_refs):
        tall = tall_gram(turned_ref, ordered_ref, 2 * k)
        tall_ref[...] = tall + before[k][...] if before else tall


def rounds_kernel(count, pieces, *refs):
    chunks, refs = refs[:pieces], refs[pieces:]
    *earlier, out_ref, ordered_ref, turned_ref = refs
    early_refs, tall_refs = earlier[: -(count // 2)], earlier[-(count // 2) :]
    width = PANEL
    depth = count.bit_length() - 1
    gather_panels(count, chunks, ordered_ref, turned_ref)

    live = [None] * (ROUNDS + 1)
    live[ROUNDS] = [0]
    for turn in reversed(range(ROUNDS)):
        bit = 1 << turn % depth
        live[turn] = sorted({a for p in live[turn + 1] for a in (p, p ^ bit)})

    row_scale, column_scale, total, grams = {}, {}, {}, {}
    for b in range(0, count, 2):
        tall = tall_refs[b // 2][...] + tall_gram(turned_ref, ordered_ref, b)
        for i in range(b + 2):
            for j in range(2):
                if i <= b + j:
                    grams[i, b + j] = tall[
                        i * width : (i + 1) * width, j * width : (j + 1) * width
                    ]
    for p in range(count):
        total[p] = diagonal_of(grams[p, p])
        row_scale[p] = lax.rsqrt(total[p])
        column_scale[p] = turned_rows(row_scale[p])
    first_scale = dict(column_scale)
    blocks = {
        (a, b): column_scale[a] * gram * row_scale[b] for (a, b), gram in grams.items()
    }
    eye = diagonal_mask(width)

    def joined_from(blocks):
        def joined(left, right, corner=lambda block: block):
            def block_of(a, b):
                if a == b:
                    return corner(blocks[a, a])
                return blocks[a, b] if (a, b) in blocks else blocks[b, a].T

            return jnp.concatenate(
                [jnp.concatenate([block_of(a, b) for b in right], axis=1) for a in left], axis=0
            )

        return joined

    history = []
    finish = None
    for turn in range(ROUNDS):
        bit = 1 << turn % depth
        pairs = [(p, p | bit) for p in live[turn] if not p & bit]
        joined = joined_from(blocks)
        whole = [joined(pair, pair) for pair in pairs]
        offs = [
            joined(pair, pair, lambda block: jnp.where(eye, 0.0, block)) for pair in pairs
        ]
        factors = root_factors(whole, offs)
        if finish is not None:
            finish()
        keep = live[turn + 1]
        scales = {}
        if turn + 1 < ROUNDS:
            kept = [[i for i in range(2) if pair[i] in keep] for pair in pairs]
            spans = [
                slice(k[0] * width, (k[-1] + 1) * width) for k in kept
            ]
            fresh, row_scale, column_scale = {}, {}, {}
            for i, pair in enumerate(pairs):
                z, e, thin = factors[i]
                span = spans[i]
                part = offs[i][span] + e[span] + mul(thin[span], half(offs[i]))
                value = part[:, span] + e[span, span] + mul(half(part), thin[:, span])
                for k, at in enumerate(kept[i]):
                    cut = slice(k * width, (k + 1) * width)
                    block = value[cut, cut] + jnp.where(eye, 1.0, 0.0)
                    along = diagonal_of(block)
                    row_scale[pair[at]] = lax.rsqrt(along)
                    column_scale[pair[at]] = turned_rows(row_scale[pair[at]])
                    total[pair[at]] = total[pair[at]] * along * z * z
                    fresh[pair[at], pair[at]] = block
                    for j, to in list(enumerate(kept[i]))[k + 1 :]:
                        fresh[pair[at], pair[to]] = value[cut, j * width : (j + 1) * width]
            following = 1 << (turn + 1) % depth
            soon, later = [], []
            for j in range(1, len(pairs)):
                near = [
                    i
                    for i in range(j)
                    if any(a ^ following in pairs[j] for a in pairs[i])
                ]
                soon.append((j, near))
                later.append((j, [i for i in range(j) if i not in near]))

            def cross(work, joined, pairs, factors, kept, spans, fresh):
                for j, members in work:
                    if not members:
                        continue
                    tops = []
                    for i in members:
                        source = joined(pairs[i], pairs[j])
                        tops.append(
                            source[spans[i]] + mul(factors[i][2][spans[i]], half(source))
                        )
                    tall = jnp.concatenate(tops, axis=0)
                    tall = tall[:, spans[j]] + mul(half(tall), factors[j][2][:, spans[j]])
                    start = 0
                    for i in members:
                        for at in kept[i]:
                            for k, to in enumerate(kept[j]):
                                fresh[pairs[i][at], pairs[j][to]] = tall[
                                    start : start + width, k * width : (k + 1) * width
                                ]
                            start += width

            def scaled(fresh, column_scale, row_scale):
                return {
                    (a, b): column_scale[a] * value * row_scale[b]
                    for (a, b), value in fresh.items()
                }

            known = (joined_from(blocks), pairs, factors, kept, spans)
            cross(soon, *known, fresh)
            blocks = scaled(fresh, column_scale, row_scale)

            def finish(blocks=blocks, later=later, known=known, down=column_scale, along=row_scale):
                rest = {}
                cross(later, *known, rest)
                blocks.update(scaled(rest, down, along))

            scales = column_scale
        history.append((pairs, factors, scales))

    pairs, factors, _ = history[-1]
    z, e, _ = factors[0]
    combined = {
        pairs[0][0]: jnp.where(eye, 1.0, 0.0) + e[:width, :width],
        pairs[0][1]: e[width:, :width],
    }
    final = z * jnp.sqrt(total[0])
    for pairs, factors, scales in reversed(history[:-1]):
        following = {}
        for pair, (z, e, thin) in zip(pairs, factors):
            parts = [i for i in range(2) if pair[i] in combined]
            tops = {i: scales[pair[i]] * combined[pair[i]] for i in parts}
            stacked = half(jnp.concatenate([tops[i] for i in parts], axis=0))
            moved = mul(thin[:, parts[0] * width : (parts[-1] + 1) * width], stacked)
            for i in range(2):
                rows = moved[i * width : (i + 1) * width]
                following[pair[i]] = tops[i] + rows if i in tops else rows
        combined = following
    weights = jnp.concatenate(
        [first_scale[p] * combined[p] for p in range(count)], axis=0
    ) * final
    high = half(weights)
    low = half(weights - high.astype(jnp.float32))
    own = out_ref.shape[0]
    chunk = own // count
    both = jnp.concatenate([high, low], axis=1)
    origins = ring_origins(count)
    first = 0
    for source_ref in (*early_refs, ordered_ref):
        rows = source_ref.shape[0] // 2
        product = mul(source_ref[:rows], both)
        result = product[:, :width] + product[:, width:]
        for k in range(rows // chunk):
            start = pl.multiple_of(origins[first + k] * chunk, chunk)
            out_ref[pl.ds(start, chunk), :] = result[k * chunk : (k + 1) * chunk]
        first += rows // chunk


def add_gram(blocks, talls):
    rows, total = sum(block.shape[0] for block in blocks), blocks[0].shape[1]
    count = total // PANEL
    inside = pl.BlockSpec(memory_space=pltpu.VMEM)
    ordered, *talls = pl.pallas_call(
        functools.partial(gram_kernel, count, len(blocks)),
        out_shape=[jax.ShapeDtypeStruct((rows, total), jnp.bfloat16)]
        + [
            jax.ShapeDtypeStruct(((b + 2) * PANEL, 2 * PANEL), jnp.float32)
            for b in range(0, count, 2)
        ],
        in_specs=[inside] * (len(blocks) + len(talls)),
        out_specs=[inside] * (1 + count // 2),
        input_output_aliases={len(blocks) + k: 1 + k for k in range(len(talls))},
        scratch_shapes=[pltpu.VMEM((total, rows), jnp.bfloat16)],
        compiler_params=pltpu.CompilerParams(vmem_limit_bytes=16 << 20),
        cost_estimate=pl.CostEstimate(
            flops=2 * rows * total * total,
            bytes_accessed=4 * rows * total + 3 * total * total,
            transcendentals=0,
        ),
    )(*blocks, *talls)
    return ordered, talls


def all_rounds(mine, other):
    total = mine[0].shape[1]
    count = total // PANEL
    inside = pl.BlockSpec(memory_space=pltpu.VMEM)
    talls, early = [], []
    near = count // 2 - 1
    for span in (slice(0, near), slice(near, -1)):
        ordered, talls = add_gram(mine[span] + other[span], talls)
        early.append(ordered)
    last = mine[-1:] + other[-1:]
    last_rows = sum(block.shape[0] for block in last)
    own_rows = sum(block.shape[0] for block in mine)
    return pl.pallas_call(
        functools.partial(rounds_kernel, count, len(last)),
        out_shape=jax.ShapeDtypeStruct((own_rows, PANEL), jnp.float32),
        in_specs=[inside] * (len(last) + len(early) + len(talls)),
        out_specs=inside,
        scratch_shapes=[
            pltpu.VMEM((last_rows, total), jnp.bfloat16),
            pltpu.VMEM((total, last_rows), jnp.bfloat16),
        ],
        compiler_params=pltpu.CompilerParams(vmem_limit_bytes=32 << 20),
    )(*last, *early, *talls)


def ring_gather(block, axis):
    count = lax.axis_size(axis)
    ring = list(range(0, count, 2)) + list(range(1, count, 2))[::-1]
    onward = [(ring[i], ring[(i + 1) % count]) for i in range(count)]
    back = [(b, a) for a, b in onward]
    blocks = [block]
    ahead = behind = block
    for _ in range(1, count // 2):
        ahead = lax.ppermute(ahead, axis, onward)
        behind = lax.ppermute(behind, axis, back)
        blocks += [ahead, behind]
    blocks.append(lax.ppermute(ahead, axis, onward))
    return blocks


def gathered_rounds(sketch):
    mine = ring_gather(sketch, "row")
    other = []
    for block in mine:
        other.append(lax.ppermute(block, "grp", [(0, 1), (1, 0)]))
    return all_rounds(mine, other)


def pair_transform(gram):
    squares = jnp.sum(jnp.where(diagonal_mask(gram.shape[0]), gram, 0.0), axis=0)
    inv_root = lax.rsqrt(squares)
    normed = gram * inv_root[:, None] * inv_root[None, :]
    bound = jnp.max(jnp.sum(jnp.abs(normed), axis=1))
    identity = jnp.eye(gram.shape[0], dtype=jnp.float32)
    current = normed / bound
    inverse = identity
    for _ in range(NS_ITERS):
        middle = 1.5 * identity - 0.5 * jnp.dot(inverse, current, precision=lax.Precision.HIGHEST)
        current_next = jnp.dot(current, middle, precision=lax.Precision.HIGHEST)
        inverse = jnp.dot(middle, inverse, precision=lax.Precision.HIGHEST)
        current = current_next
    return inv_root[:, None] * inverse * (jnp.sqrt(squares) / jnp.sqrt(bound))[None, :]


def cross_product(left, right):
    return lax.dot_general(
        left,
        right,
        (((0,), (0,)), ((), ())),
        precision=lax.Precision.HIGHEST,
        preferred_element_type=jnp.float32,
    )


def gram_blocks(own, partner):
    return (cross_product(own, own), cross_product(own, partner), cross_product(partner, partner))


def pair_update(own, partner, blocks, lower):
    self_gram, cross_gram, other_gram = blocks
    low_low = jnp.where(lower, self_gram, other_gram)
    high_high = jnp.where(lower, other_gram, self_gram)
    low_high = jnp.where(lower, cross_gram, cross_gram.T)
    gram = jnp.concatenate(
        [
            jnp.concatenate([low_low, low_high], axis=1),
            jnp.concatenate([low_high.T, high_high], axis=1),
        ],
        axis=0,
    )
    mixing = pair_transform(gram)
    width = own.shape[1]
    own_own = jnp.where(lower, mixing[:width, :width], mixing[width:, width:])
    other_own = jnp.where(lower, mixing[width:, :width], mixing[:width, width:])
    return jnp.dot(own, own_own, precision=lax.Precision.HIGHEST) + jnp.dot(
        partner, other_own, precision=lax.Precision.HIGHEST
    )


def exchanged_rounds(sketch):
    regrouped = lax.all_to_all(sketch, "row", split_axis=1, concat_axis=0, tiled=True)
    half_rows = regrouped.shape[0]
    depth = lax.axis_size("row").bit_length() - 1
    position = lax.axis_index("row")
    working = lax.all_gather(regrouped, "grp", axis=0, tiled=True).astype(jnp.float32)
    for turn in range(ROUNDS):
        bit = turn % depth
        partner = swapped(working.astype(jnp.bfloat16), "row", bit).astype(working.dtype)
        lower = position >> bit & 1 == 0
        working = pair_update(working, partner, gram_blocks(working, partner), lower)
    return lax.dynamic_slice_in_dim(working, lax.axis_index("grp") * half_rows, half_rows, 0)


def gathers(devices, columns):
    return 2 * KB * devices * columns + 4 * columns * columns <= GATHER_BYTES


def per_device(design, target, coeffs, tau_level, bucket, sign_bit, panel_order):
    sketch = sketch_local(design, target, coeffs, tau_level, bucket, sign_bit, panel_order)
    columns = design.shape[1]
    if gathers(lax.axis_size("row") * lax.axis_size("grp"), columns):
        return gathered_rounds(sketch)
    return exchanged_rounds(sketch)


def solution(mesh):
    placed = (
        P(("parts", "grp", "row"), None),
        P(("parts", "grp", "row")),
        P("parts"),
        P(("parts", "grp", "row")),
        P(("parts", "grp", "row")),
        P(("parts", "grp", "row")),
        P("parts"),
    )
    return jax.shard_map(
        per_device,
        mesh=mesh,
        in_specs=placed,
        out_specs=P(("parts", "grp"), "row"),
        check_vma=False,
    )
```

```python
import functools

import jax
import jax.numpy as jnp
from jax import lax
from jax.experimental import pallas as pl
from jax.experimental.pallas import tpu as pltpu
from jax.sharding import PartitionSpec as P

PANEL = 128
KB = 64
ROUNDS = 5
NS_ITERS = 4
GATHER_BYTES = 12 << 20


def swapped(block, axis, bit):
    count = lax.axis_size(axis)
    route = []
    for low in range(count):
        high = low | 1 << bit
        if high != low and high < count:
            route += [(low, high), (high, low)]
    return lax.ppermute(block, axis, route)


def sketch_kernel(*refs):
    sources, out_ref, places, arrived = refs[:7], refs[7], refs[8:15], refs[15]
    design_ref, target_ref, coeffs_ref, level_ref, bucket_ref, sign_ref, order_ref = places
    copies = [
        pltpu.make_async_copy(source, here, arrived.at[i])
        for i, (source, here) in enumerate(zip(sources, places))
    ]
    for copy in copies:
        copy.start()
    for copy in copies:
        copy.wait()
    rows = design_ref.shape[0]
    design = design_ref[...]
    fitted = lax.dot_general(
        coeffs_ref[...].reshape(1, -1),
        design,
        (((1,), (1,)), ((), ())),
        preferred_element_type=jnp.float32,
    )
    residual = target_ref[...].reshape(1, rows) - fitted
    blocks = level_ref.shape[0]
    lane = lax.broadcasted_iota(jnp.int32, (1, rows), 1)
    level = jnp.full((1, rows), level_ref[0], jnp.int32)
    for block in range(1, blocks):
        level = jnp.where(lane >= block * (rows // blocks), level_ref[block], level)
    quantile = 0.1 + 0.25 * level.astype(jnp.float32)
    upper = jax.nn.sigmoid(residual / 0.2)
    weight = (quantile * upper + (1.0 - quantile) * (1.0 - upper)) / jnp.sqrt(
        residual * residual + 0.25
    )
    sign = 2.0 * sign_ref[...].reshape(1, rows).astype(jnp.float32) - 1.0
    signed = (sign * jnp.sqrt(weight)).astype(jnp.bfloat16).astype(jnp.float32)
    slots = lax.broadcasted_iota(jnp.int32, (KB, rows), 0)
    embed = jnp.where(slots == bucket_ref[...].reshape(1, rows), signed, 0.0).astype(jnp.bfloat16)
    for j in range(order_ref.shape[0]):
        column = pl.multiple_of(order_ref[j] * PANEL, PANEL)
        out_ref[:, j * PANEL : (j + 1) * PANEL] = jnp.dot(
            embed, design_ref[:, pl.ds(column, PANEL)], preferred_element_type=jnp.float32
        ).astype(jnp.bfloat16)


def sketch_local(design, target, coeffs, tau_level, bucket, sign_bit, panel_order):
    rows, columns = design.shape
    anywhere = pl.BlockSpec(memory_space=pltpu.HBM)
    return pl.pallas_call(
        sketch_kernel,
        out_shape=jax.ShapeDtypeStruct((KB, columns), jnp.bfloat16),
        in_specs=[anywhere] * 7,
        out_specs=pl.BlockSpec(memory_space=pltpu.VMEM),
        scratch_shapes=[
            pltpu.VMEM((rows, columns), jnp.bfloat16),
            pltpu.VMEM((rows,), jnp.float32),
            pltpu.VMEM((columns,), jnp.bfloat16),
            pltpu.SMEM(tau_level.shape, jnp.int32),
            pltpu.VMEM((rows,), jnp.int32),
            pltpu.VMEM((rows,), jnp.int32),
            pltpu.SMEM(panel_order.shape, jnp.int32),
            pltpu.SemaphoreType.DMA((7,)),
        ],
        compiler_params=pltpu.CompilerParams(vmem_limit_bytes=67043328),
    )(design, target, coeffs, tau_level, bucket, sign_bit, panel_order)


def half(block):
    return block.astype(jnp.bfloat16)


def mul(left, right):
    return jnp.dot(left, right, preferred_element_type=jnp.float32)


def diagonal_mask(width):
    rows = lax.broadcasted_iota(jnp.int32, (width, width), 0)
    columns = lax.broadcasted_iota(jnp.int32, (width, width), 1)
    return rows == columns


def root_factors(grams, offs):
    thin = [half(a) for a in offs]
    squared = [mul(a, a) for a in thin]
    w, t, s, z = [], [], [], []
    for gram in grams:
        bound = jnp.max(jnp.sum(jnp.abs(gram), axis=0, keepdims=True), axis=1, keepdims=True)
        w.append(1.0 / bound)
        t.append(1.5 - 0.5 * w[-1])
        s.append(-0.5 * w[-1] / t[-1])
        z.append(lax.rsqrt(bound))
    v = offs
    doubles = []
    for step in range(NS_ITERS):
        z = [a * b for a, b in zip(z, t)]
        after = [1.5 - 0.5 * a * a * b for a, b in zip(t, w)]
        gain = [a * a * a / b for a, b in zip(t, after)]
        linear = [1.0 - b / a for a, b in zip(t, w)]
        square = [2.0 - 0.5 * b / a for a, b in zip(t, w)]
        if step:
            squared = [mul(a, a) for a in thin]
        if step % 2 == 0 and step + 2 >= NS_ITERS and step + 1 < NS_ITERS:
            parts = []
            for g, a, b, c, x, q in zip(gain, linear, square, s, v, squared):
                outer = half(q)
                inner = half((g * (1.0 + b) * c * c * c) * x + (g * c * c * c * c) * q)
                parts.append(
                    ((1.0 + g * a) * c) * x + (g * (a + b) * c * c) * q + mul(inner, outer)
                )
            doubles.append(parts)
        elif step % 2 == 0 and step + 1 == NS_ITERS:
            doubles.append([c * x for c, x in zip(s, v)])
        if step + 2 < NS_ITERS or step % 2 == 1 and step + 1 < NS_ITERS:
            before, flat, size = v, thin, s
            if step:
                s = [g * c * c * c for g, c in zip(gain, s)]
                share = [jnp.ones_like(a) for a in s]
            else:
                s = [jnp.ones_like(a) for a in s]
                share = [g * c * c * c for g, c in zip(gain, size)]
            inner = [
                half((d * b / c) * x + (d * q if step == 0 else q))
                for d, b, c, x, q in zip(share, square, size, v, squared)
            ]
            v = [
                (d * a / (c * c)) * x + mul(r, y)
                for d, a, c, x, r, y in zip(share, linear, size, v, inner, thin)
            ]
            thin = [half(a) for a in v]
            if step % 2 == 0:
                doubles.append(
                    [
                        c * x + d * (y + c * mul(a, b))
                        for c, x, d, y, a, b in zip(size, before, s, v, thin, flat)
                    ]
                )
        w = [a * a * b for a, b in zip(t, w)]
        t = after
    e = doubles[0]
    thin = [half(a) for a in e]
    for parts in doubles[1:]:
        e = [a + b + mul(half(b), c) for a, b, c in zip(e, parts, thin)]
        thin = [half(a) for a in e]
    return list(zip(z, e, thin))


def diagonal_of(block):
    return jnp.sum(jnp.where(diagonal_mask(block.shape[0]), block, 0.0), axis=0, keepdims=True)


def turned_rows(row):
    return jnp.broadcast_to(row, (row.shape[1], row.shape[1])).T


def ring_place(index, count):
    return jnp.where(index % 2 == 0, index // 2, count - 1 - index // 2)


def ring_index(place, count):
    return jnp.where(place < count // 2, 2 * place, 2 * (count - 1 - place) + 1)


def ring_origins(count):
    here = ring_place(lax.axis_index("row"), count)
    turns = [0] + [step for k in range(1, count // 2) for step in (-k, k)] + [count // 2]
    return [ring_index((here + turn + count) % count, count) for turn in turns]


def gather_panels(count, chunks, ordered_ref, turned_ref):
    position = lax.axis_index("row")
    start = 0
    for chunk in chunks:
        rows = chunk.shape[0]
        for j in range(count):
            column = pl.multiple_of(jnp.bitwise_xor(position, j) * PANEL, PANEL)
            ordered_ref[start : start + rows, j * PANEL : (j + 1) * PANEL] = chunk[
                :, pl.ds(column, PANEL)
            ]
        start += rows
    for p in range(0, count, 2):
        span = slice(p * PANEL, (p + 2) * PANEL)
        turned_ref[span] = ordered_ref[:, span].T


def tall_gram(turned_ref, ordered_ref, b):
    return mul(turned_ref[: (b + 2) * PANEL], ordered_ref[:, b * PANEL : (b + 2) * PANEL])


def gram_kernel(count, pieces, *refs):
    chunks, before, after = refs[:pieces], refs[pieces : -2 - count // 2], refs[-2 - count // 2 :]
    ordered_ref, *tall_refs, turned_ref = after
    gather_panels(count, chunks, ordered_ref, turned_ref)
    for k, tall_ref in enumerate(tall_refs):
        tall = tall_gram(turned_ref, ordered_ref, 2 * k)
        tall_ref[...] = tall + before[k][...] if before else tall


def rounds_kernel(count, pieces, *refs):
    chunks, refs = refs[:pieces], refs[pieces:]
    *earlier, out_ref, ordered_ref, turned_ref = refs
    early_refs, tall_refs = earlier[: -(count // 2)], earlier[-(count // 2) :]
    width = PANEL
    depth = count.bit_length() - 1
    gather_panels(count, chunks, ordered_ref, turned_ref)

    live = [None] * (ROUNDS + 1)
    live[ROUNDS] = [0]
    for turn in reversed(range(ROUNDS)):
        bit = 1 << turn % depth
        live[turn] = sorted({a for p in live[turn + 1] for a in (p, p ^ bit)})

    row_scale, column_scale, total, grams = {}, {}, {}, {}
    for b in range(0, count, 2):
        tall = tall_refs[b // 2][...] + tall_gram(turned_ref, ordered_ref, b)
        for i in range(b + 2):
            for j in range(2):
                if i <= b + j:
                    grams[i, b + j] = tall[
                        i * width : (i + 1) * width, j * width : (j + 1) * width
                    ]
    for p in range(count):
        total[p] = diagonal_of(grams[p, p])
        row_scale[p] = lax.rsqrt(total[p])
        column_scale[p] = turned_rows(row_scale[p])
    first_scale = dict(column_scale)
    blocks = {
        (a, b): column_scale[a] * gram * row_scale[b] for (a, b), gram in grams.items()
    }
    eye = diagonal_mask(width)

    def joined_from(blocks):
        def joined(left, right, corner=lambda block: block):
            def block_of(a, b):
                if a == b:
                    return corner(blocks[a, a])
                return blocks[a, b] if (a, b) in blocks else blocks[b, a].T

            return jnp.concatenate(
                [jnp.concatenate([block_of(a, b) for b in right], axis=1) for a in left], axis=0
            )

        return joined

    history = []
    finish = None
    for turn in range(ROUNDS):
        bit = 1 << turn % depth
        pairs = [(p, p | bit) for p in live[turn] if not p & bit]
        joined = joined_from(blocks)
        whole = [joined(pair, pair) for pair in pairs]
        offs = [
            joined(pair, pair, lambda block: jnp.where(eye, 0.0, block)) for pair in pairs
        ]
        if finish is not None:
            finish()
        factors = root_factors(whole, offs)
        keep = live[turn + 1]
        scales = {}
        if turn + 1 < ROUNDS:
            kept = [[i for i in range(2) if pair[i] in keep] for pair in pairs]
            spans = [
                slice(k[0] * width, (k[-1] + 1) * width) for k in kept
            ]
            fresh, row_scale, column_scale = {}, {}, {}
            sides = [
                off[span] + e[span] + mul(thin[span], half(off))
                for off, span, (_, e, thin) in zip(offs, spans, factors)
            ]
            values = [
                side[:, span] + e[span, span] + mul(half(side), thin[:, span])
                for side, span, (_, e, thin) in zip(sides, spans, factors)
            ]
            for i, pair in enumerate(pairs):
                z, value = factors[i][0], values[i]
                for k, at in enumerate(kept[i]):
                    cut = slice(k * width, (k + 1) * width)
                    block = value[cut, cut] + jnp.where(eye, 1.0, 0.0)
                    along = diagonal_of(block)
                    row_scale[pair[at]] = lax.rsqrt(along)
                    column_scale[pair[at]] = turned_rows(row_scale[pair[at]])
                    total[pair[at]] = total[pair[at]] * along * z * z
                    fresh[pair[at], pair[at]] = block
                    for j, to in list(enumerate(kept[i]))[k + 1 :]:
                        fresh[pair[at], pair[to]] = value[cut, j * width : (j + 1) * width]
            following = 1 << (turn + 1) % depth
            soon, later = [], []
            for j in range(1, len(pairs)):
                near = [
                    i
                    for i in range(j)
                    if any(a ^ following in pairs[j] for a in pairs[i])
                ]
                soon.append((j, near))
                later.append((j, [i for i in range(j) if i not in near]))

            def cross(work, joined, pairs, factors, kept, spans, fresh):
                for j, members in work:
                    if not members:
                        continue
                    tops = []
                    for i in members:
                        source = joined(pairs[i], pairs[j])
                        tops.append(
                            source[spans[i]] + mul(factors[i][2][spans[i]], half(source))
                        )
                    tall = jnp.concatenate(tops, axis=0)
                    tall = tall[:, spans[j]] + mul(half(tall), factors[j][2][:, spans[j]])
                    start = 0
                    for i in members:
                        for at in kept[i]:
                            for k, to in enumerate(kept[j]):
                                fresh[pairs[i][at], pairs[j][to]] = tall[
                                    start : start + width, k * width : (k + 1) * width
                                ]
                            start += width

            def scaled(fresh, column_scale, row_scale):
                return {
                    (a, b): column_scale[a] * value * row_scale[b]
                    for (a, b), value in fresh.items()
                }

            known = (joined_from(blocks), pairs, factors, kept, spans)
            cross(soon, *known, fresh)
            blocks = scaled(fresh, column_scale, row_scale)

            def finish(blocks=blocks, later=later, known=known, down=column_scale, along=row_scale):
                rest = {}
                cross(later, *known, rest)
                blocks.update(scaled(rest, down, along))

            scales = column_scale
        history.append((pairs, factors, scales))

    pairs, factors, _ = history[-1]
    z, e, _ = factors[0]
    combined = {
        pairs[0][0]: jnp.where(eye, 1.0, 0.0) + e[:width, :width],
        pairs[0][1]: e[width:, :width],
    }
    final = z * jnp.sqrt(total[0])
    for pairs, factors, scales in reversed(history[:-1]):
        following = {}
        for pair, (z, e, thin) in zip(pairs, factors):
            parts = [i for i in range(2) if pair[i] in combined]
            tops = {i: scales[pair[i]] * combined[pair[i]] for i in parts}
            stacked = half(jnp.concatenate([tops[i] for i in parts], axis=0))
            moved = mul(thin[:, parts[0] * width : (parts[-1] + 1) * width], stacked)
            for i in range(2):
                rows = moved[i * width : (i + 1) * width]
                following[pair[i]] = tops[i] + rows if i in tops else rows
        combined = following
    weights = jnp.concatenate(
        [first_scale[p] * combined[p] for p in range(count)], axis=0
    ) * final
    high = half(weights)
    low = half(weights - high.astype(jnp.float32))
    own = out_ref.shape[0]
    chunk = own // count
    both = jnp.concatenate([high, low], axis=1)
    origins = ring_origins(count)
    first = 0
    for source_ref in (*early_refs, ordered_ref):
        rows = source_ref.shape[0] // 2
        product = mul(source_ref[:rows], both)
        result = product[:, :width] + product[:, width:]
        for k in range(rows // chunk):
            start = pl.multiple_of(origins[first + k] * chunk, chunk)
            out_ref[pl.ds(start, chunk), :] = result[k * chunk : (k + 1) * chunk]
        first += rows // chunk


def add_gram(blocks, talls):
    rows, total = sum(block.shape[0] for block in blocks), blocks[0].shape[1]
    count = total // PANEL
    inside = pl.BlockSpec(memory_space=pltpu.VMEM)
    ordered, *talls = pl.pallas_call(
        functools.partial(gram_kernel, count, len(blocks)),
        out_shape=[jax.ShapeDtypeStruct((rows, total), jnp.bfloat16)]
        + [
            jax.ShapeDtypeStruct(((b + 2) * PANEL, 2 * PANEL), jnp.float32)
            for b in range(0, count, 2)
        ],
        in_specs=[inside] * (len(blocks) + len(talls)),
        out_specs=[inside] * (1 + count // 2),
        input_output_aliases={len(blocks) + k: 1 + k for k in range(len(talls))},
        scratch_shapes=[pltpu.VMEM((total, rows), jnp.bfloat16)],
        compiler_params=pltpu.CompilerParams(vmem_limit_bytes=16 << 20),
        cost_estimate=pl.CostEstimate(
            flops=2 * rows * total * total,
            bytes_accessed=4 * rows * total + 3 * total * total,
            transcendentals=0,
        ),
    )(*blocks, *talls)
    return ordered, talls


def all_rounds(mine, other):
    total = mine[0].shape[1]
    count = total // PANEL
    inside = pl.BlockSpec(memory_space=pltpu.VMEM)
    talls, early = [], []
    near = count // 2 - 1
    for span in (slice(0, near), slice(near, -1)):
        ordered, talls = add_gram(mine[span] + other[span], talls)
        early.append(ordered)
    last = mine[-1:] + other[-1:]
    last_rows = sum(block.shape[0] for block in last)
    own_rows = sum(block.shape[0] for block in mine)
    return pl.pallas_call(
        functools.partial(rounds_kernel, count, len(last)),
        out_shape=jax.ShapeDtypeStruct((own_rows, PANEL), jnp.float32),
        in_specs=[inside] * (len(last) + len(early) + len(talls)),
        out_specs=inside,
        scratch_shapes=[
            pltpu.VMEM((last_rows, total), jnp.bfloat16),
            pltpu.VMEM((total, last_rows), jnp.bfloat16),
        ],
        compiler_params=pltpu.CompilerParams(vmem_limit_bytes=32 << 20),
    )(*last, *early, *talls)


def ring_gather(block, axis):
    count = lax.axis_size(axis)
    ring = list(range(0, count, 2)) + list(range(1, count, 2))[::-1]
    onward = [(ring[i], ring[(i + 1) % count]) for i in range(count)]
    back = [(b, a) for a, b in onward]
    blocks = [block]
    ahead = behind = block
    for _ in range(1, count // 2):
        ahead = lax.ppermute(ahead, axis, onward)
        behind = lax.ppermute(behind, axis, back)
        blocks += [ahead, behind]
    blocks.append(lax.ppermute(ahead, axis, onward))
    return blocks


def gathered_rounds(sketch):
    mine = ring_gather(sketch, "row")
    other = []
    for block in mine:
        other.append(lax.ppermute(block, "grp", [(0, 1), (1, 0)]))
    return all_rounds(mine, other)


def pair_transform(gram):
    squares = jnp.sum(jnp.where(diagonal_mask(gram.shape[0]), gram, 0.0), axis=0)
    inv_root = lax.rsqrt(squares)
    normed = gram * inv_root[:, None] * inv_root[None, :]
    bound = jnp.max(jnp.sum(jnp.abs(normed), axis=1))
    identity = jnp.eye(gram.shape[0], dtype=jnp.float32)
    current = normed / bound
    inverse = identity
    for _ in range(NS_ITERS):
        middle = 1.5 * identity - 0.5 * jnp.dot(inverse, current, precision=lax.Precision.HIGHEST)
        current_next = jnp.dot(current, middle, precision=lax.Precision.HIGHEST)
        inverse = jnp.dot(middle, inverse, precision=lax.Precision.HIGHEST)
        current = current_next
    return inv_root[:, None] * inverse * (jnp.sqrt(squares) / jnp.sqrt(bound))[None, :]


def cross_product(left, right):
    return lax.dot_general(
        left,
        right,
        (((0,), (0,)), ((), ())),
        precision=lax.Precision.HIGHEST,
        preferred_element_type=jnp.float32,
    )


def gram_blocks(own, partner):
    return (cross_product(own, own), cross_product(own, partner), cross_product(partner, partner))


def pair_update(own, partner, blocks, lower):
    self_gram, cross_gram, other_gram = blocks
    low_low = jnp.where(lower, self_gram, other_gram)
    high_high = jnp.where(lower, other_gram, self_gram)
    low_high = jnp.where(lower, cross_gram, cross_gram.T)
    gram = jnp.concatenate(
        [
            jnp.concatenate([low_low, low_high], axis=1),
            jnp.concatenate([low_high.T, high_high], axis=1),
        ],
        axis=0,
    )
    mixing = pair_transform(gram)
    width = own.shape[1]
    own_own = jnp.where(lower, mixing[:width, :width], mixing[width:, width:])
    other_own = jnp.where(lower, mixing[width:, :width], mixing[:width, width:])
    return jnp.dot(own, own_own, precision=lax.Precision.HIGHEST) + jnp.dot(
        partner, other_own, precision=lax.Precision.HIGHEST
    )


def exchanged_rounds(sketch):
    regrouped = lax.all_to_all(sketch, "row", split_axis=1, concat_axis=0, tiled=True)
    half_rows = regrouped.shape[0]
    depth = lax.axis_size("row").bit_length() - 1
    position = lax.axis_index("row")
    working = lax.all_gather(regrouped, "grp", axis=0, tiled=True).astype(jnp.float32)
    for turn in range(ROUNDS):
        bit = turn % depth
        partner = swapped(working.astype(jnp.bfloat16), "row", bit).astype(working.dtype)
        lower = position >> bit & 1 == 0
        working = pair_update(working, partner, gram_blocks(working, partner), lower)
    return lax.dynamic_slice_in_dim(working, lax.axis_index("grp") * half_rows, half_rows, 0)


def gathers(devices, columns):
    return 2 * KB * devices * columns + 4 * columns * columns <= GATHER_BYTES


def per_device(design, target, coeffs, tau_level, bucket, sign_bit, panel_order):
    sketch = sketch_local(design, target, coeffs, tau_level, bucket, sign_bit, panel_order)
    columns = design.shape[1]
    if gathers(lax.axis_size("row") * lax.axis_size("grp"), columns):
        return gathered_rounds(sketch)
    return exchanged_rounds(sketch)


def solution(mesh):
    placed = (
        P(("parts", "grp", "row"), None),
        P(("parts", "grp", "row")),
        P("parts"),
        P(("parts", "grp", "row")),
        P(("parts", "grp", "row")),
        P(("parts", "grp", "row")),
        P("parts"),
    )
    return jax.shard_map(
        per_device,
        mesh=mesh,
        in_specs=placed,
        out_specs=P(("parts", "grp"), "row"),
        check_vma=False,
    )
```

```python
import functools

import jax
import jax.numpy as jnp
from jax import lax
from jax.experimental import pallas as pl
from jax.experimental.pallas import tpu as pltpu
from jax.sharding import PartitionSpec as P

PANEL = 128
KB = 64
ROUNDS = 5
NS_ITERS = 4
GATHER_BYTES = 12 << 20


def swapped(block, axis, bit):
    count = lax.axis_size(axis)
    route = []
    for low in range(count):
        high = low | 1 << bit
        if high != low and high < count:
            route += [(low, high), (high, low)]
    return lax.ppermute(block, axis, route)


def sketch_kernel(*refs):
    sources, out_ref, places, arrived = refs[:7], refs[7], refs[8:15], refs[15]
    design_ref, target_ref, coeffs_ref, level_ref, bucket_ref, sign_ref, order_ref = places
    copies = [
        pltpu.make_async_copy(source, here, arrived.at[i])
        for i, (source, here) in enumerate(zip(sources, places))
    ]
    for copy in copies:
        copy.start()
    for copy in copies:
        copy.wait()
    rows = design_ref.shape[0]
    design = design_ref[...]
    fitted = lax.dot_general(
        coeffs_ref[...].reshape(1, -1),
        design,
        (((1,), (1,)), ((), ())),
        preferred_element_type=jnp.float32,
    )
    residual = target_ref[...].reshape(1, rows) - fitted
    blocks = level_ref.shape[0]
    lane = lax.broadcasted_iota(jnp.int32, (1, rows), 1)
    level = jnp.full((1, rows), level_ref[0], jnp.int32)
    for block in range(1, blocks):
        level = jnp.where(lane >= block * (rows // blocks), level_ref[block], level)
    quantile = 0.1 + 0.25 * level.astype(jnp.float32)
    upper = jax.nn.sigmoid(residual / 0.2)
    weight = (quantile * upper + (1.0 - quantile) * (1.0 - upper)) / jnp.sqrt(
        residual * residual + 0.25
    )
    sign = 2.0 * sign_ref[...].reshape(1, rows).astype(jnp.float32) - 1.0
    signed = (sign * jnp.sqrt(weight)).astype(jnp.bfloat16).astype(jnp.float32)
    slots = lax.broadcasted_iota(jnp.int32, (KB, rows), 0)
    embed = jnp.where(slots == bucket_ref[...].reshape(1, rows), signed, 0.0).astype(jnp.bfloat16)
    for j in range(order_ref.shape[0]):
        column = pl.multiple_of(order_ref[j] * PANEL, PANEL)
        out_ref[:, j * PANEL : (j + 1) * PANEL] = jnp.dot(
            embed, design_ref[:, pl.ds(column, PANEL)], preferred_element_type=jnp.float32
        ).astype(jnp.bfloat16)


def sketch_local(design, target, coeffs, tau_level, bucket, sign_bit, panel_order):
    rows, columns = design.shape
    anywhere = pl.BlockSpec(memory_space=pltpu.HBM)
    return pl.pallas_call(
        sketch_kernel,
        out_shape=jax.ShapeDtypeStruct((KB, columns), jnp.bfloat16),
        in_specs=[anywhere] * 7,
        out_specs=pl.BlockSpec(memory_space=pltpu.VMEM),
        scratch_shapes=[
            pltpu.VMEM((rows, columns), jnp.bfloat16),
            pltpu.VMEM((rows,), jnp.float32),
            pltpu.VMEM((columns,), jnp.bfloat16),
            pltpu.SMEM(tau_level.shape, jnp.int32),
            pltpu.VMEM((rows,), jnp.int32),
            pltpu.VMEM((rows,), jnp.int32),
            pltpu.SMEM(panel_order.shape, jnp.int32),
            pltpu.SemaphoreType.DMA((7,)),
        ],
        compiler_params=pltpu.CompilerParams(vmem_limit_bytes=67043328),
    )(design, target, coeffs, tau_level, bucket, sign_bit, panel_order)


def half(block):
    return block.astype(jnp.bfloat16)


def mul(left, right):
    return jnp.dot(left, right, preferred_element_type=jnp.float32)


def diagonal_mask(width):
    rows = lax.broadcasted_iota(jnp.int32, (width, width), 0)
    columns = lax.broadcasted_iota(jnp.int32, (width, width), 1)
    return rows == columns


def root_factors(grams, offs):
    thin = [half(a) for a in offs]
    squared = [mul(a, a) for a in thin]
    w, t, s, z = [], [], [], []
    for gram in grams:
        bound = jnp.max(jnp.sum(jnp.abs(gram), axis=0, keepdims=True), axis=1, keepdims=True)
        w.append(1.0 / bound)
        t.append(1.5 - 0.5 * w[-1])
        s.append(-0.5 * w[-1] / t[-1])
        z.append(lax.rsqrt(bound))
    v = offs
    doubles = []
    for step in range(NS_ITERS):
        z = [a * b for a, b in zip(z, t)]
        after = [1.5 - 0.5 * a * a * b for a, b in zip(t, w)]
        gain = [a * a * a / b for a, b in zip(t, after)]
        linear = [1.0 - b / a for a, b in zip(t, w)]
        square = [2.0 - 0.5 * b / a for a, b in zip(t, w)]
        if step:
            squared = [mul(a, a) for a in thin]
        if step % 2 == 0 and step + 2 >= NS_ITERS and step + 1 < NS_ITERS:
            parts = []
            for g, a, b, c, x, q in zip(gain, linear, square, s, v, squared):
                outer = half(q)
                inner = half((g * (1.0 + b) * c * c * c) * x + (g * c * c * c * c) * q)
                parts.append(
                    ((1.0 + g * a) * c) * x + (g * (a + b) * c * c) * q + mul(inner, outer)
                )
            doubles.append(parts)
        elif step % 2 == 0 and step + 1 == NS_ITERS:
            doubles.append([c * x for c, x in zip(s, v)])
        if step + 2 < NS_ITERS or step % 2 == 1 and step + 1 < NS_ITERS:
            before, flat, size = v, thin, s
            if step:
                s = [g * c * c * c for g, c in zip(gain, s)]
                share = [jnp.ones_like(a) for a in s]
            else:
                s = [jnp.ones_like(a) for a in s]
                share = [g * c * c * c for g, c in zip(gain, size)]
            inner = [
                half((d * b / c) * x + (d * q if step == 0 else q))
                for d, b, c, x, q in zip(share, square, size, v, squared)
            ]
            v = [
                (d * a / (c * c)) * x + mul(r, y)
                for d, a, c, x, r, y in zip(share, linear, size, v, inner, thin)
            ]
            thin = [half(a) for a in v]
            if step % 2 == 0:
                doubles.append(
                    [
                        c * x + d * (y + c * mul(a, b))
                        for c, x, d, y, a, b in zip(size, before, s, v, thin, flat)
                    ]
                )
        w = [a * a * b for a, b in zip(t, w)]
        t = after
    e = doubles[0]
    thin = [half(a) for a in e]
    for parts in doubles[1:]:
        e = [a + b + mul(half(b), c) for a, b, c in zip(e, parts, thin)]
        thin = [half(a) for a in e]
    return list(zip(z, e, thin))


def diagonal_of(block):
    return jnp.sum(jnp.where(diagonal_mask(block.shape[0]), block, 0.0), axis=0, keepdims=True)


def turned_rows(row):
    return jnp.broadcast_to(row, (row.shape[1], row.shape[1])).T


def ring_place(index, count):
    return jnp.where(index % 2 == 0, index // 2, count - 1 - index // 2)


def ring_index(place, count):
    return jnp.where(place < count // 2, 2 * place, 2 * (count - 1 - place) + 1)


def ring_origins(count):
    here = ring_place(lax.axis_index("row"), count)
    turns = [0] + [step for k in range(1, count // 2) for step in (-k, k)] + [count // 2]
    return [ring_index((here + turn + count) % count, count) for turn in turns]


def gather_panels(count, chunks, ordered_ref, turned_ref):
    position = lax.axis_index("row")
    start = 0
    for chunk in chunks:
        rows = chunk.shape[0]
        for j in range(count):
            column = pl.multiple_of(jnp.bitwise_xor(position, j) * PANEL, PANEL)
            ordered_ref[start : start + rows, j * PANEL : (j + 1) * PANEL] = chunk[
                :, pl.ds(column, PANEL)
            ]
        start += rows
    for p in range(0, count, 2):
        span = slice(p * PANEL, (p + 2) * PANEL)
        turned_ref[span] = ordered_ref[:, span].T


def tall_gram(turned_ref, ordered_ref, b):
    return mul(turned_ref[: (b + 2) * PANEL], ordered_ref[:, b * PANEL : (b + 2) * PANEL])


def gram_kernel(count, pieces, *refs):
    chunks, before, after = refs[:pieces], refs[pieces : -2 - count // 2], refs[-2 - count // 2 :]
    ordered_ref, *tall_refs, turned_ref = after
    gather_panels(count, chunks, ordered_ref, turned_ref)
    for k, tall_ref in enumerate(tall_refs):
        tall = tall_gram(turned_ref, ordered_ref, 2 * k)
        tall_ref[...] = tall + before[k][...] if before else tall


def rounds_kernel(count, pieces, *refs):
    chunks, refs = refs[:pieces], refs[pieces:]
    *earlier, out_ref, ordered_ref, turned_ref = refs
    early_refs, tall_refs = earlier[: -(count // 2)], earlier[-(count // 2) :]
    width = PANEL
    depth = count.bit_length() - 1
    gather_panels(count, chunks, ordered_ref, turned_ref)

    live = [None] * (ROUNDS + 1)
    live[ROUNDS] = [0]
    for turn in reversed(range(ROUNDS)):
        bit = 1 << turn % depth
        live[turn] = sorted({a for p in live[turn + 1] for a in (p, p ^ bit)})

    row_scale, column_scale, total, grams = {}, {}, {}, {}
    for b in reversed(range(0, count, 2)):
        tall = tall_refs[b // 2][...] + tall_gram(turned_ref, ordered_ref, b)
        for i in range(b + 2):
            for j in range(2):
                if i <= b + j:
                    grams[i, b + j] = tall[
                        i * width : (i + 1) * width, j * width : (j + 1) * width
                    ]
    for p in range(count):
        total[p] = diagonal_of(grams[p, p])
        row_scale[p] = lax.rsqrt(total[p])
        column_scale[p] = turned_rows(row_scale[p])
    first_scale = dict(column_scale)
    blocks = {
        (a, b): column_scale[a] * gram * row_scale[b] for (a, b), gram in grams.items()
    }
    eye = diagonal_mask(width)

    def joined_from(blocks):
        def joined(left, right, corner=lambda block: block):
            def block_of(a, b):
                if a == b:
                    return corner(blocks[a, a])
                return blocks[a, b] if (a, b) in blocks else blocks[b, a].T

            return jnp.concatenate(
                [jnp.concatenate([block_of(a, b) for b in right], axis=1) for a in left], axis=0
            )

        return joined

    history = []
    finish = None
    for turn in range(ROUNDS):
        bit = 1 << turn % depth
        pairs = [(p, p | bit) for p in live[turn] if not p & bit]
        joined = joined_from(blocks)
        whole = [joined(pair, pair) for pair in pairs]
        offs = [
            joined(pair, pair, lambda block: jnp.where(eye, 0.0, block)) for pair in pairs
        ]
        if finish is not None:
            finish()
        factors = root_factors(whole, offs)
        keep = live[turn + 1]
        scales = {}
        if turn + 1 < ROUNDS:
            kept = [[i for i in range(2) if pair[i] in keep] for pair in pairs]
            spans = [
                slice(k[0] * width, (k[-1] + 1) * width) for k in kept
            ]
            fresh, row_scale, column_scale = {}, {}, {}
            sides = [
                off[span] + e[span] + mul(thin[span], half(off))
                for off, span, (_, e, thin) in zip(offs, spans, factors)
            ]
            values = [
                side[:, span] + e[span, span] + mul(half(side), thin[:, span])
                for side, span, (_, e, thin) in zip(sides, spans, factors)
            ]
            for i, pair in enumerate(pairs):
                z, value = factors[i][0], values[i]
                for k, at in enumerate(kept[i]):
                    cut = slice(k * width, (k + 1) * width)
                    block = value[cut, cut] + jnp.where(eye, 1.0, 0.0)
                    along = diagonal_of(block)
                    row_scale[pair[at]] = lax.rsqrt(along)
                    column_scale[pair[at]] = turned_rows(row_scale[pair[at]])
                    total[pair[at]] = total[pair[at]] * along * z * z
                    fresh[pair[at], pair[at]] = block
                    for j, to in list(enumerate(kept[i]))[k + 1 :]:
                        fresh[pair[at], pair[to]] = value[cut, j * width : (j + 1) * width]
            following = 1 << (turn + 1) % depth
            soon, later = [], []
            for j in range(1, len(pairs)):
                near = [
                    i
                    for i in range(j)
                    if any(a ^ following in pairs[j] for a in pairs[i])
                ]
                soon.append((j, near))
                later.append((j, [i for i in range(j) if i not in near]))

            def cross(work, joined, pairs, factors, kept, spans, fresh):
                work = [(j, members) for j, members in work if members]
                talls = []
                for j, members in work:
                    sources = [joined(pairs[i], pairs[j]) for i in members]
                    talls.append(
                        jnp.concatenate(
                            [
                                source[spans[i]] + mul(factors[i][2][spans[i]], half(source))
                                for i, source in zip(members, sources)
                            ],
                            axis=0,
                        )
                    )
                talls = [
                    tall[:, spans[j]] + mul(half(tall), factors[j][2][:, spans[j]])
                    for (j, _), tall in zip(work, talls)
                ]
                for (j, members), tall in zip(work, talls):
                    start = 0
                    for i in members:
                        for at in kept[i]:
                            for k, to in enumerate(kept[j]):
                                fresh[pairs[i][at], pairs[j][to]] = tall[
                                    start : start + width, k * width : (k + 1) * width
                                ]
                            start += width

            def scaled(fresh, column_scale, row_scale):
                return {
                    (a, b): column_scale[a] * value * row_scale[b]
                    for (a, b), value in fresh.items()
                }

            known = (joined_from(blocks), pairs, factors, kept, spans)
            cross(soon, *known, fresh)
            blocks = scaled(fresh, column_scale, row_scale)

            def finish(blocks=blocks, later=later, known=known, down=column_scale, along=row_scale):
                rest = {}
                cross(later, *known, rest)
                blocks.update(scaled(rest, down, along))

            scales = column_scale
        history.append((pairs, factors, scales))

    pairs, factors, _ = history[-1]
    z, e, _ = factors[0]
    combined = {
        pairs[0][0]: jnp.where(eye, 1.0, 0.0) + e[:width, :width],
        pairs[0][1]: e[width:, :width],
    }
    final = z * jnp.sqrt(total[0])
    for pairs, factors, scales in reversed(history[:-1]):
        following = {}
        for pair, (z, e, thin) in zip(pairs, factors):
            parts = [i for i in range(2) if pair[i] in combined]
            tops = {i: scales[pair[i]] * combined[pair[i]] for i in parts}
            stacked = half(jnp.concatenate([tops[i] for i in parts], axis=0))
            moved = mul(thin[:, parts[0] * width : (parts[-1] + 1) * width], stacked)
            for i in range(2):
                rows = moved[i * width : (i + 1) * width]
                following[pair[i]] = tops[i] + rows if i in tops else rows
        combined = following
    weights = jnp.concatenate(
        [first_scale[p] * combined[p] for p in range(count)], axis=0
    ) * final
    high = half(weights)
    low = half(weights - high.astype(jnp.float32))
    own = out_ref.shape[0]
    chunk = own // count
    both = jnp.concatenate([high, low], axis=1)
    origins = ring_origins(count)
    first = 0
    for source_ref in (*early_refs, ordered_ref):
        rows = source_ref.shape[0] // 2
        product = mul(source_ref[:rows], both)
        result = product[:, :width] + product[:, width:]
        for k in range(rows // chunk):
            start = pl.multiple_of(origins[first + k] * chunk, chunk)
            out_ref[pl.ds(start, chunk), :] = result[k * chunk : (k + 1) * chunk]
        first += rows // chunk


def add_gram(blocks, talls):
    rows, total = sum(block.shape[0] for block in blocks), blocks[0].shape[1]
    count = total // PANEL
    inside = pl.BlockSpec(memory_space=pltpu.VMEM)
    ordered, *talls = pl.pallas_call(
        functools.partial(gram_kernel, count, len(blocks)),
        out_shape=[jax.ShapeDtypeStruct((rows, total), jnp.bfloat16)]
        + [
            jax.ShapeDtypeStruct(((b + 2) * PANEL, 2 * PANEL), jnp.float32)
            for b in range(0, count, 2)
        ],
        in_specs=[inside] * (len(blocks) + len(talls)),
        out_specs=[inside] * (1 + count // 2),
        input_output_aliases={len(blocks) + k: 1 + k for k in range(len(talls))},
        scratch_shapes=[pltpu.VMEM((total, rows), jnp.bfloat16)],
        compiler_params=pltpu.CompilerParams(vmem_limit_bytes=16 << 20),
        cost_estimate=pl.CostEstimate(
            flops=2 * rows * total * total,
            bytes_accessed=4 * rows * total + 3 * total * total,
            transcendentals=0,
        ),
    )(*blocks, *talls)
    return ordered, talls


def all_rounds(mine, other):
    total = mine[0].shape[1]
    count = total // PANEL
    inside = pl.BlockSpec(memory_space=pltpu.VMEM)
    talls, early = [], []
    near = count // 2 - 1
    for span in (slice(0, near), slice(near, -1)):
        ordered, talls = add_gram(mine[span] + other[span], talls)
        early.append(ordered)
    last = mine[-1:] + other[-1:]
    last_rows = sum(block.shape[0] for block in last)
    own_rows = sum(block.shape[0] for block in mine)
    return pl.pallas_call(
        functools.partial(rounds_kernel, count, len(last)),
        out_shape=jax.ShapeDtypeStruct((own_rows, PANEL), jnp.float32),
        in_specs=[inside] * (len(last) + len(early) + len(talls)),
        out_specs=inside,
        scratch_shapes=[
            pltpu.VMEM((last_rows, total), jnp.bfloat16),
            pltpu.VMEM((total, last_rows), jnp.bfloat16),
        ],
        compiler_params=pltpu.CompilerParams(vmem_limit_bytes=32 << 20),
    )(*last, *early, *talls)


def ring_gather(block, axis):
    count = lax.axis_size(axis)
    ring = list(range(0, count, 2)) + list(range(1, count, 2))[::-1]
    onward = [(ring[i], ring[(i + 1) % count]) for i in range(count)]
    back = [(b, a) for a, b in onward]
    blocks = [block]
    ahead = behind = block
    for _ in range(1, count // 2):
        ahead = lax.ppermute(ahead, axis, onward)
        behind = lax.ppermute(behind, axis, back)
        blocks += [ahead, behind]
    blocks.append(lax.ppermute(ahead, axis, onward))
    return blocks


def gathered_rounds(sketch):
    mine = ring_gather(sketch, "row")
    other = []
    for block in mine:
        other.append(lax.ppermute(block, "grp", [(0, 1), (1, 0)]))
    return all_rounds(mine, other)


def pair_transform(gram):
    squares = jnp.sum(jnp.where(diagonal_mask(gram.shape[0]), gram, 0.0), axis=0)
    inv_root = lax.rsqrt(squares)
    normed = gram * inv_root[:, None] * inv_root[None, :]
    bound = jnp.max(jnp.sum(jnp.abs(normed), axis=1))
    identity = jnp.eye(gram.shape[0], dtype=jnp.float32)
    current = normed / bound
    inverse = identity
    for _ in range(NS_ITERS):
        middle = 1.5 * identity - 0.5 * jnp.dot(inverse, current, precision=lax.Precision.HIGHEST)
        current_next = jnp.dot(current, middle, precision=lax.Precision.HIGHEST)
        inverse = jnp.dot(middle, inverse, precision=lax.Precision.HIGHEST)
        current = current_next
    return inv_root[:, None] * inverse * (jnp.sqrt(squares) / jnp.sqrt(bound))[None, :]


def cross_product(left, right):
    return lax.dot_general(
        left,
        right,
        (((0,), (0,)), ((), ())),
        precision=lax.Precision.HIGHEST,
        preferred_element_type=jnp.float32,
    )


def gram_blocks(own, partner):
    return (cross_product(own, own), cross_product(own, partner), cross_product(partner, partner))


def pair_update(own, partner, blocks, lower):
    self_gram, cross_gram, other_gram = blocks
    low_low = jnp.where(lower, self_gram, other_gram)
    high_high = jnp.where(lower, other_gram, self_gram)
    low_high = jnp.where(lower, cross_gram, cross_gram.T)
    gram = jnp.concatenate(
        [
            jnp.concatenate([low_low, low_high], axis=1),
            jnp.concatenate([low_high.T, high_high], axis=1),
        ],
        axis=0,
    )
    mixing = pair_transform(gram)
    width = own.shape[1]
    own_own = jnp.where(lower, mixing[:width, :width], mixing[width:, width:])
    other_own = jnp.where(lower, mixing[width:, :width], mixing[:width, width:])
    return jnp.dot(own, own_own, precision=lax.Precision.HIGHEST) + jnp.dot(
        partner, other_own, precision=lax.Precision.HIGHEST
    )


def exchanged_rounds(sketch):
    regrouped = lax.all_to_all(sketch, "row", split_axis=1, concat_axis=0, tiled=True)
    half_rows = regrouped.shape[0]
    depth = lax.axis_size("row").bit_length() - 1
    position = lax.axis_index("row")
    working = lax.all_gather(regrouped, "grp", axis=0, tiled=True).astype(jnp.float32)
    for turn in range(ROUNDS):
        bit = turn % depth
        partner = swapped(working.astype(jnp.bfloat16), "row", bit).astype(working.dtype)
        lower = position >> bit & 1 == 0
        working = pair_update(working, partner, gram_blocks(working, partner), lower)
    return lax.dynamic_slice_in_dim(working, lax.axis_index("grp") * half_rows, half_rows, 0)


def gathers(devices, columns):
    return 2 * KB * devices * columns + 4 * columns * columns <= GATHER_BYTES


def per_device(design, target, coeffs, tau_level, bucket, sign_bit, panel_order):
    sketch = sketch_local(design, target, coeffs, tau_level, bucket, sign_bit, panel_order)
    columns = design.shape[1]
    if gathers(lax.axis_size("row") * lax.axis_size("grp"), columns):
        return gathered_rounds(sketch)
    return exchanged_rounds(sketch)


def solution(mesh):
    placed = (
        P(("parts", "grp", "row"), None),
        P(("parts", "grp", "row")),
        P("parts"),
        P(("parts", "grp", "row")),
        P(("parts", "grp", "row")),
        P(("parts", "grp", "row")),
        P("parts"),
    )
    return jax.shard_map(
        per_device,
        mesh=mesh,
        in_specs=placed,
        out_specs=P(("parts", "grp"), "row"),
        check_vma=False,
    )
```
